32 devices in a mesh: fsdp: 4 (over y, x), ctx: 2 (over core), tp: 4 (over z).
Axes of the slice: x: 2, y: 2, z: 4, core: 2. Of those that a mesh axis runs over, the one named last changes fastest.
Arguments:
- tokens: bfloat16 [4, 2048, 1536], P('fsdp', 'ctx'), may hold values from -6 to 6
- segments: int32 [4, 2048], P('fsdp'), may hold values from 0 to 3, never falling along the last dimension, each value on 1 to 1024 neighbouring positions
- norm_gain: float32 [1536], replicated, may hold values from 0.5 to 1.5
- proj_main: bfloat16 [2, 1536, 3072], P(None, 'fsdp', 'tp'), may hold values from -0.15625 to 0.15625
- proj_shared: bfloat16 [1536, 256], P('fsdp'), may hold values from -0.15625 to 0.15625
- proj_step: bfloat16 [1536, 48], P('fsdp', 'tp'), may hold values from -0.15625 to 0.15625
- conv_main: float32 [5, 3072], P(None, 'tp'), may hold values from -0.5 to 0.5
- conv_shared: float32 [5, 256], replicated, may hold values from -0.5 to 0.5
- head_params: float32 [3, 48], P(None, 'tp'), may hold values from -7 to 2.1
- gate_gain: float32 [3072], P('tp'), may hold values from 0.5 to 1.5
- output_projection: bfloat16 [3072, 1536], P('tp', 'fsdp'), may hold values from -0.15625 to 0.15625
- cotangent: bfloat16 [4, 2048, 1536], P('fsdp', 'ctx'), may hold values from -6 to 6
Outputs:
- output: bfloat16 [4, 2048, 1536], P('fsdp', 'ctx', 'tp')
- grad_tokens: float32 [4, 2048, 1536], P('fsdp', 'ctx', 'tp')
- grad_norm_gain: float32 [1536], P('tp')
- grad_proj_main: float32 [2, 1536, 3072], P(None, ('fsdp', 'ctx'), 'tp')
- grad_proj_shared: float32 [1536, 256], P(('fsdp', 'ctx'))
- grad_proj_step: float32 [1536, 48], P(('fsdp', 'ctx'), 'tp')
- grad_conv_main: float32 [5, 3072], P(None, 'tp')
- grad_conv_shared: float32 [5, 256], replicated
- grad_head_params: float32 [3, 48], P(None, 'tp')
- grad_gate_gain: float32 [3072], P('tp')
- grad_proj_out: float32 [3072, 1536], P('tp', ('fsdp', 'ctx'))
The draws below stay inside these ranges and needn't reach their ends.
Inputs may be any that keep to these rules, and one draw needn't show every extreme that they name: `segments`: never falling along a sequence; every sequence holds documents 0 to 3, each of 1 to 1024 positions, one of exactly 1024.
All inputs are finite; a program needn't handle non-finite values.
Results may differ from the reference program's by a relative error of at most 0.02.
Values may be sent and summed in bfloat16 or wider, within the bound.
No kernel may reach another device: no remote copies, remote signals or barrier semaphores. Data moves between devices by JAX's collectives and lax.ppermute only.
A program may use at most 192 MiB of HBM per device.

```python
import math
import jax
import jax.numpy as jnp
import numpy as np
from jax import lax

D = 1536
HEADS = 48
HEADDIM = 64
STATE = 128
CONV = 4
STRETCH = 256
LENGTH = 2048
SEQS = 4
INNER = 3072


def draw_head_params(key, part):
    subkeys = jax.random.split(key, 3)
    log_scale = jax.random.uniform(subkeys[0], (HEADS,), jnp.float32, math.log(0.25), math.log(8.0))
    step_bias = jax.random.uniform(subkeys[1], (HEADS,), jnp.float32, -6.5, -2.5)
    skip_gain = jax.random.uniform(subkeys[2], (HEADS,), jnp.float32, 0.25, 1.25)
    return jnp.stack([log_scale, step_bias, skip_gain])


def raised(values, stream_key, source, target, parts, factor):
    owner, partner = [(jnp.arange(values.shape[position]) // (values.shape[position] // parts)).reshape([-1 if axis == position else 1 for axis in range(values.ndim)]) for position in (source, target)]
    chosen = jax.random.permutation(stream_key, parts)[partner]
    strong = (owner == chosen) | (owner == (partner + parts // 2) % parts)
    return jnp.where(strong, factor * values, values)


def block_levels(own_key, shape, shards, least, top_value):
    gain = 1.0
    for axis_at, blocks in shards:
        steps = jax.random.uniform(jax.random.fold_in(jax.random.fold_in(own_key, 6), axis_at), (blocks,), jnp.float32, least / len(shards), top_value / len(shards))
        gain = gain * jnp.repeat(jnp.exp(steps), shape[axis_at] // blocks).reshape((-1,) + (1,) * (len(shape) - 1 - axis_at))
    return gain


def length_profile(count, total, limit, skew):
    loads = [(1 << 20) // math.isqrt(standing ** skew) + 1 for standing in range(2, count + 1)]
    spare, holding = total - limit - (count - 1), [1] * (count - 1)
    while spare > 0:
        movable = [i for i in range(count - 1) if holding[i] < limit]
        whole, budget = sum([loads[i] for i in movable]), spare
        for i in movable:
            more = min(limit - holding[i], max(1, budget * loads[i] // whole), spare)
            holding[i] = holding[i] + more
            spare = spare - more
    return np.array([limit] + holding)


def uneven_parts(stream_key, amount, total, reach, lean):
    if amount == 2:
        one = jax.random.randint(stream_key, (), max(1, total - reach), min(reach, total - 1) + 1)
        return jnp.stack([one, total - one])
    tallies = jnp.asarray(length_profile(amount, total, reach, lean), jnp.int32)
    couples = (amount - 1) // 2
    donor, sink = tallies[1:1 + 2 * couples:2], tallies[2:2 + 2 * couples:2]
    margin = jnp.minimum(donor - 1, reach - sink)
    moved = jax.random.randint(jax.random.fold_in(stream_key, 1), (couples,), 0, 1 << 20) % (margin + 1)
    tallies = tallies.at[1:1 + 2 * couples:2].set(donor - moved).at[2:2 + 2 * couples:2].set(sink + moved)
    return tallies[jax.random.permutation(jax.random.fold_in(stream_key, 2), amount)]


def gaussian(rng, dims, deviation, limit, cuts=(), held_as=jnp.bfloat16):
    values = deviation * jax.random.normal(rng, dims, jnp.float32)
    if cuts:
        values = values * block_levels(rng, dims, cuts, -0.22, 0.18)
    return jnp.clip(values, -limit, limit).astype(held_as)


def gaussian_with(stream_key, extent, deviation, limit, cuts, heavy, kind=jnp.bfloat16):
    values = deviation * jax.random.normal(stream_key, extent, jnp.float32)
    if cuts:
        values = values * block_levels(stream_key, extent, cuts, -0.22, 0.18)
    return jnp.clip(raised(values, jax.random.fold_in(stream_key, 3), *heavy), -limit, limit).astype(kind)


def setup_inputs(seed: int = 0) -> dict:
    splits = jax.random.split(jax.random.key(seed), 13)
    tokens = gaussian(splits[0], (SEQS, LENGTH, D), 1.0, 6.0, ((0, 4), (1, 2)))
    segments = jax.vmap(lambda own: jnp.searchsorted(jnp.cumsum(uneven_parts(own, 4, LENGTH, LENGTH // 2, 1)), jnp.arange(LENGTH), side="right"))(jax.random.split(splits[1], SEQS)).reshape((SEQS, LENGTH)).astype(jnp.int32)
    norm_gain = jnp.clip(1.0 + 0.1 * jax.random.normal(splits[2], (D,), jnp.float32), 0.5, 1.5)
    proj_main = gaussian(splits[3], (2, D, INNER), D ** -0.5, 0.15625, ((1, 4), (2, 4)))
    proj_shared = gaussian(splits[4], (D, 2 * STATE), D ** -0.5, 0.15625, ((0, 4),))
    proj_step = gaussian(splits[5], (D, HEADS), D ** -0.5, 0.15625, ((0, 4), (1, 4)))
    conv_main = jnp.clip(jax.random.uniform(splits[6], (CONV + 1, INNER), jnp.float32, -0.5, 0.5) * block_levels(splits[6], (CONV + 1, INNER), ((1, 4),), -0.4, 0.0), -0.5, 0.5)
    conv_shared = jnp.clip(jax.random.uniform(splits[7], (CONV + 1, 2 * STATE), jnp.float32, -0.5, 0.5), -0.5, 0.5)
    head_params = draw_head_params(jax.random.fold_in(splits[12], 71), 0)
    gate_gain = jnp.clip(1.0 + 0.1 * jax.random.normal(splits[9], (INNER,), jnp.float32), 0.5, 1.5)
    output_projection = gaussian_with(splits[10], (INNER, D), INNER ** -0.5, 0.15625, ((0, 4), (1, 4)), (0, 1, 4, 2.0))
    cotangent = gaussian(splits[11], (SEQS, LENGTH, D), 1.0, 6.0, ((0, 4), (1, 2)))
    return {"tokens": tokens, "segments": segments, "norm_gain": norm_gain, "proj_main": proj_main, "proj_shared": proj_shared, "proj_step": proj_step, "conv_main": conv_main, "conv_shared": conv_shared, "head_params": head_params, "gate_gain": gate_gain, "output_projection": output_projection, "cotangent": cotangent}


@jax.custom_vjp
def lower_precision(v):
    return lax.optimization_barrier(v.astype(jnp.bfloat16)).astype(jnp.float32)

@jax.custom_vjp
def lower_precision_backward(v):
    return v

def low_keep(v):
    return (lower_precision(v), None)

def low_pass(kept, grad):
    return (grad,)

def back_keep(v):
    return (v, None)

def back_low(kept, grad):
    return (lower_precision(grad),)
lower_precision.defvjp(low_keep, low_pass)
lower_precision_backward.defvjp(back_keep, back_low)
EXACT_PRECISION = lax.Precision.HIGHEST
EPSILON = 1e-05

def apply_silu(values):
    return values * jax.nn.sigmoid(values)

def causal_conv(inputs, segment, kernel):
    kernel_span = kernel.shape[0] - 1
    length = inputs.shape[1]
    padded = jnp.concatenate([jnp.zeros((inputs.shape[0], kernel_span - 1, inputs.shape[2]), jnp.float32), inputs], axis=1)
    segment_padded = jnp.concatenate([jnp.full((segment.shape[0], kernel_span - 1), -1, jnp.int32), segment], axis=1)
    summed = kernel[kernel_span] + jnp.zeros_like(inputs)
    for offset in range(kernel_span):
        matching = (segment_padded[:, offset:offset + length] == segment).astype(jnp.float32)[:, :, None]
        summed = summed + kernel[offset] * padded[:, offset:offset + length] * matching
    return summed

def stretch_step(carry_state, pieces):
    inputs_x, block_keys, block_queries, step_sizes, log_decay, segment, segment_before = pieces
    cumulative = jnp.cumsum(log_decay, axis=1)
    cumulative_heads = jnp.swapaxes(cumulative, 1, 2)
    causal = jnp.tril(jnp.ones((STRETCH, STRETCH), dtype=bool))
    same_doc = ((segment[:, :, None] == segment[:, None, :]) & causal)[:, None]
    differ = cumulative_heads[:, :, :, None] - cumulative_heads[:, :, None, :]
    decay_mask = jnp.exp(jnp.where(same_doc, differ, 0.0)) * same_doc.astype(jnp.float32)
    gram_mat = lower_precision_backward(jnp.einsum('gqn,gsn->gqs', block_queries, block_keys, precision=EXACT_PRECISION))
    step_heads = jnp.swapaxes(step_sizes, 1, 2)
    scores = lower_precision(lower_precision_backward(gram_mat[:, None] * decay_mask * step_heads[:, :, None, :]))
    within = jnp.einsum('ghqs,gshp->gqhp', scores, inputs_x, precision=EXACT_PRECISION)
    alive_mask = (segment == segment_before[:, None]).astype(jnp.float32)
    rising = jnp.exp(cumulative) * alive_mask[:, :, None]
    carried = jnp.einsum('gqn,ghpn->gqhp', block_queries, carry_state, precision=EXACT_PRECISION) * rising[..., None]
    end_match = (segment == segment[:, -1:]).astype(jnp.float32)
    weight_end = jnp.exp(cumulative[:, -1:, :] - cumulative) * end_match[:, :, None] * step_sizes
    stretch_state = jnp.einsum('gqhp,gqn->ghpn', inputs_x * weight_end[..., None], block_keys, precision=EXACT_PRECISION)
    factor = jnp.exp(cumulative[:, -1, :]) * alive_mask[:, -1:]
    new_state = factor[..., None, None] * carry_state + stretch_state
    return (new_state, within + carried)

def mixer(tokens, segment, norm_gain, proj_main, proj_shared, proj_step, conv_main, conv_shared, head_params, gate_gain, output_projection):
    groups = tokens.shape[0]
    inverse_rms = lax.rsqrt(lax.optimization_barrier(jnp.mean(tokens * tokens, axis=-1, keepdims=True)) + EPSILON)
    norm_output = lower_precision(tokens * inverse_rms * norm_gain)

    def project(weight_matrix):
        return lower_precision(lower_precision_backward(jnp.einsum('iqe,ew->iqw', norm_output, weight_matrix, precision=EXACT_PRECISION)))
    gate_input = project(proj_main[0])
    inner_input = project(proj_main[1])
    shared_pre = project(proj_shared)
    step_raw = project(proj_step)
    conv_act = lower_precision(apply_silu(causal_conv(inner_input, segment, conv_main)))
    shared_act = lower_precision(apply_silu(causal_conv(shared_pre, segment, conv_shared)))
    step_sizes = jax.nn.softplus(step_raw + head_params[1])
    log_decay = step_sizes * -jnp.exp(head_params[0])
    inputs_x = conv_act.reshape(groups, LENGTH, HEADS, HEADDIM)
    nchunks = LENGTH // STRETCH

    def blocks_of(array):
        return jnp.moveaxis(array.reshape((groups, nchunks, STRETCH) + array.shape[2:]), 1, 0)
    segment_before = jnp.concatenate([jnp.full((groups, 1), -1, jnp.int32), segment[:, STRETCH - 1:LENGTH - 1:STRETCH]], axis=1)
    start_state = jnp.zeros((groups, HEADS, HEADDIM, STATE), jnp.float32)
    final_state, mixed_out = lax.scan(jax.checkpoint(stretch_step), start_state, (blocks_of(inputs_x), blocks_of(shared_act[..., :STATE]), blocks_of(shared_act[..., STATE:]), blocks_of(step_sizes), blocks_of(log_decay), blocks_of(segment), jnp.moveaxis(segment_before, 1, 0)))
    mixed_out = jnp.moveaxis(mixed_out, 0, 1).reshape(groups, LENGTH, HEADS, HEADDIM)
    ssm_out = lower_precision_backward((mixed_out + head_params[2][:, None] * inputs_x).reshape(groups, LENGTH, INNER))
    gated = ssm_out * apply_silu(gate_input)
    inverse_gate = lax.rsqrt(lax.optimization_barrier(jnp.mean(gated * gated, axis=-1, keepdims=True)) + EPSILON)
    gated_norm_output = lower_precision(gated * inverse_gate * gate_gain)
    return tokens + jnp.einsum('tja,az->tjz', gated_norm_output, output_projection, precision=EXACT_PRECISION)

def reference(tokens, segments, norm_gain, proj_main, proj_shared, proj_step, conv_main, conv_shared, head_params, gate_gain, output_projection, cotangent):
    params = tuple((element.astype(jnp.float32) for element in (norm_gain, proj_main, proj_shared, proj_step, conv_main, conv_shared, head_params, gate_gain, output_projection)))

    def group_step(summed, batch_items):
        tokens_one, segment_one, cot_one = batch_items

        def forward(tokens_single, *weights):
            return mixer(tokens_single, segment_one, *weights)
        result, pullback = jax.vjp(forward, tokens_one.astype(jnp.float32), *params)
        gradients = pullback(cot_one.astype(jnp.float32))
        summed = tuple((running + update for running, update in zip(summed, gradients[1:])))
        return (summed, (result.astype(jnp.bfloat16), gradients[0]))
    zeros_init = tuple((jnp.zeros_like(element) for element in params))
    summed, (outputs, grad_tokens) = lax.scan(group_step, zeros_init, (tokens.reshape(SEQS, 1, LENGTH, D), segments.reshape(SEQS, 1, LENGTH), cotangent.reshape(SEQS, 1, LENGTH, D)))
    return (outputs.reshape(SEQS, LENGTH, D), grad_tokens.reshape(SEQS, LENGTH, D), summed[0], summed[1], summed[2], summed[3], summed[4], summed[5], summed[6], summed[7], summed[8])
```

```python
import functools

import jax
import jax.numpy as jnp
from jax import lax
from jax.experimental import pallas as pl
from jax.experimental.pallas import tpu as pltpu
from jax.sharding import PartitionSpec as P

HEADDIM = 64
STATE = 128
STRETCH = 256
HALF = STRETCH // 2
INNER = 3072
EPSILON = 1e-05
HALO = 16
LANES = 128
SHARED = 2 * STATE
LEAD = SHARED + LANES
BF = jnp.bfloat16
F32 = jnp.float32


def dot_nn(a, b):
    return lax.dot_general(a, b, (((1,), (0,)), ((), ())), preferred_element_type=F32)


def dot_nt(a, b):
    return lax.dot_general(a, b, (((1,), (1,)), ((), ())), preferred_element_type=F32)


def dot_tn(a, b):
    return lax.dot_general(a, b, (((0,), (0,)), ((), ())), preferred_element_type=F32)


def split(v, n):
    terms = []
    for _ in range(n):
        high = v.astype(BF)
        terms.append(high)
        v = v - high.astype(F32)
    return terms


def exact(dot, a, b, n, left):
    total = None
    for term in split(a if left else b, n):
        part = dot(term, b) if left else dot(a, term)
        total = part if total is None else total + part
    return total


def iota(shape, axis):
    return lax.broadcasted_iota(jnp.int32, shape, axis)


def pair_widths(channels):
    return [(at, min(LANES, channels - at)) for at in range(0, channels, LANES)]


def spread(v, pair, width):
    first = v[:, 2 * pair : 2 * pair + 1]
    if width == HEADDIM:
        return jnp.broadcast_to(first, (v.shape[0], HEADDIM))
    second = v[:, 2 * pair + 1 : 2 * pair + 2]
    lane = iota((v.shape[0], LANES), 1)
    return jnp.where(lane < HEADDIM, first, second)


def head_masks(width):
    if width == HEADDIM:
        return [None]
    lane = iota((1, LANES), 1)
    return [(lane < HEADDIM).astype(F32).astype(BF), (lane >= HEADDIM).astype(F32).astype(BF)]


def masked(v, mask):
    return v if mask is None else v * mask


def sigmoid(v):
    return 1.0 / (1.0 + jnp.exp(-v))


def prep_kernel(chunk, rot_ref, tok_ref, halo_ref, cot_ref, gain_ref, normed_ref, own_ref, inv_ref, cotq_ref):
    k = pl.program_id(0)
    rot = rot_ref[0]
    count = tok_ref.shape[1] // chunk

    def scale_of(x):
        return lax.rsqrt(jnp.mean(x * x, axis=-1, keepdims=True) + EPSILON)

    def at(q):
        return pl.multiple_of(lax.rem(rot + q, count) * chunk, LANES)

    inv = scale_of(tok_ref[...].astype(F32))
    inv_ref[...] = jnp.broadcast_to(inv, inv_ref.shape)
    row = pl.multiple_of(HALO + k * STRETCH, HALO)
    for q in range(count):
        here = pl.ds(at(q), chunk)
        x = tok_ref[:, here].astype(F32)
        normed_ref[pl.ds(row, STRETCH), q * chunk : (q + 1) * chunk] = (
            x * inv * gain_ref[0:1, here]
        ).astype(BF)
        cotq_ref[:, q * chunk : (q + 1) * chunk] = cot_ref[:, here]
    own_ref[...] = tok_ref[:, pl.ds(at(0), chunk)]

    @pl.when(k == 0)
    def _():
        inv_halo = scale_of(halo_ref[...].astype(F32))
        for q in range(count):
            here = pl.ds(at(q), chunk)
            x = halo_ref[:, here].astype(F32)
            normed_ref[0:HALO, q * chunk : (q + 1) * chunk] = (
                x * inv_halo * gain_ref[0:1, here]
            ).astype(BF)


def conv_taps(u, taps, masks):
    total = taps[4:5] + taps[3:4] * u[HALO:]
    for j in (1, 2, 3):
        total = total + taps[3 - j : 4 - j] * (pltpu.roll(u, j, 0)[HALO:] * masks[j - 1])
    return total


def act_and_slope(v):
    sig = sigmoid(v)
    act = v * sig
    return act, sig + act * (1.0 - sig)


def first_kernel(
    pre_ref, km_ref, ks_ref, hp_ref, col_ref, expand_ref,
    x_ref, xs_ref, slope_ref, bc_ref, slopes_ref, step_ref, cum_ref, sgm_ref, state_ref, fac_ref, total_ref,
    carry,
):
    k = pl.program_id(0)
    channels = x_ref.shape[1]
    base = pl.multiple_of(k * STRETCH, HALO)
    rows = pl.ds(base, STRETCH + HALO)
    col = col_ref[...]
    masks = [col[:, j : j + 1] for j in range(3)]
    alive, ends = col[:, 3:4], col[:, 4:5]

    raw = pre_ref[pl.ds(base + HALO, STRETCH), SHARED:LEAD].astype(F32)
    pre = raw + hp_ref[1:2, :]
    soft = jnp.exp(-jnp.abs(pre))
    step = jnp.maximum(pre, 0.0) + jnp.log1p(soft)
    step_ref[...] = step
    sgm_ref[...] = sigmoid(pre)
    log_decay = step * -jnp.exp(hp_ref[0:1, :])
    tri = (iota((STRETCH, STRETCH), 0) >= iota((STRETCH, STRETCH), 1)).astype(F32).astype(BF)
    cum = exact(dot_nn, tri, log_decay, 3, False)
    cum_ref[...] = cum
    last = cum[STRETCH - 1 : STRETCH]
    ef = jnp.exp(last - cum) * ends
    factor = jnp.exp(last) * alive[STRETCH - 1 : STRETCH]
    fac_row = exact(dot_nt, jnp.broadcast_to(factor, (8, LANES)), expand_ref[...], 3, True)
    fac_ref[0] = fac_row

    acts, slopes = act_and_slope(
        conv_taps(pre_ref[rows, 0:SHARED].astype(F32), ks_ref[...], masks)
    )
    bc_ref[...] = acts.astype(BF)
    slopes_ref[...] = slopes.astype(BF)
    keys_t = jnp.transpose(acts[:, 0:STATE]).astype(BF)

    @pl.when(k == 0)
    def _():
        carry[...] = jnp.zeros_like(carry)

    for pair, (at, width) in enumerate(pair_widths(channels)):
        lanes = slice(at, at + width)
        u = pre_ref[rows, LEAD + at : LEAD + at + width].astype(F32)
        act, slope = act_and_slope(conv_taps(u, km_ref[:, lanes], masks))
        low = act.astype(BF)
        x_ref[:, lanes] = low
        slope_ref[:, lanes] = slope.astype(BF)
        xs = (low.astype(F32) * spread(step, pair, width)).astype(BF)
        xs_ref[:, lanes] = xs
        xe = (xs.astype(F32) * spread(ef, pair, width)).astype(BF)
        state = dot_nn(keys_t, xe)
        state_ref[0, :, lanes] = state
        carry[:, lanes] = carry[:, lanes] * fac_row[0:1, lanes] + state

    @pl.when(k == pl.num_programs(0) - 1)
    def _():
        total_ref[...] = carry[...].astype(BF)


def doc_mask(seg_col, seg_row, shape, transposed):
    down, across = iota(shape, 0), iota(shape, 1)
    order = (across >= down) if transposed else (down >= across)
    return (seg_col == seg_row) & order


def second_kernel(
    bc_ref, x_ref, xs_ref, cum_ref, state_ref, fac_ref, enter_ref, gate_ref, gng_ref, gain_ref, skip_ref, col_ref, seg_ref,
    y_ref, gg_ref, stat_ref, hist_ref,
    hold,
):
    k = pl.program_id(0)
    channels = x_ref.shape[1]

    @pl.when(k == 0)
    def _():
        hold[...] = enter_ref[...].astype(F32)

    hist_ref[pl.ds(k, 1)] = hold[...].astype(BF)[None]
    col = col_ref[...]
    alive = col[:, 3:4]
    keys, queries = bc_ref[:, 0:STATE], bc_ref[:, STATE:SHARED]
    gram = dot_nt(queries, keys)
    valid = doc_mask(col[:, 5:6], seg_ref[0:1, :], (STRETCH, STRETCH), False)
    gram = jnp.where(valid, gram, 0.0)
    cum = cum_ref[...]
    cum_t = jnp.transpose(cum)
    rise = jnp.exp(cum) * alive
    square = jnp.zeros((STRETCH, LANES), F32)
    cross = jnp.zeros((STRETCH, LANES), F32)
    for pair, (at, width) in enumerate(pair_widths(channels)):
        lanes = slice(at, at + width)
        xs = xs_ref[:, lanes]
        top = bottom = 0.0
        for which, mask in enumerate(head_masks(width)):
            h = 2 * pair + which
            here = masked(xs, mask)
            down, across = cum[:, h : h + 1], cum_t[h : h + 1, :]
            decay = jnp.exp(jnp.minimum(down[:HALF] - across[:, :HALF], 0.0))
            top = top + dot_nn((decay * gram[:HALF, :HALF]).astype(BF), here[:HALF])
            decay = jnp.exp(jnp.minimum(down[HALF:] - across, 0.0))
            bottom = bottom + dot_nn((decay * gram[HALF:]).astype(BF), here)
        within = jnp.concatenate([top, bottom], axis=0)
        old = hold[:, lanes]
        carried = dot_nn(queries, old.astype(BF)) * spread(rise, pair, width)
        hold[:, lanes] = old * fac_ref[0, 0:1, lanes] + state_ref[0, :, lanes]
        y = within + carried + skip_ref[0:1, lanes] * x_ref[:, lanes].astype(F32)
        y_ref[:, lanes] = y
        gate = gate_ref[:, lanes].astype(F32)
        gated = y * (gate * sigmoid(gate))
        scaled = gated * gain_ref[0:1, lanes]
        gg_ref[:, lanes] = scaled.astype(BF)
        sq, cr = gated * gated, scaled * gng_ref[:, lanes].astype(F32)
        if width == LANES:
            square, cross = square + sq, cross + cr
        else:
            pad = jnp.zeros((STRETCH, LANES - width), F32)
            square = square + jnp.concatenate([sq, pad], axis=1)
            cross = cross + jnp.concatenate([cr, pad], axis=1)
    ones = jnp.ones((8, LANES), BF)
    square = exact(dot_nt, ones, square, 3, False)
    cross = exact(dot_nt, ones, cross, 3, False)
    stat_ref[...] = jnp.where(iota((8, STRETCH), 0) == 0, square, cross)

    @pl.when(k == pl.num_programs(0) - 1)
    def _():
        hist_ref[pl.ds(k + 1, 1)] = hold[...].astype(BF)[None]


def third_kernel(
    stat_ref, y_ref, gate_ref, gng_ref, gain_ref, bc_ref, cum_ref, fac_ref, col_ref,
    gy_ref, gi_ref, inv_ref, flow_ref, gaingrad_ref,
    hold,
):
    i = pl.program_id(0)
    channels = y_ref.shape[1]

    @pl.when(i == 0)
    def _():
        hold[...] = jnp.zeros_like(hold)
        gaingrad_ref[...] = jnp.zeros_like(gaingrad_ref)

    pick = iota((8, LANES), 0)
    stat = stat_ref[...]
    square = exact(dot_tn, stat, (pick == 0).astype(F32).astype(BF), 3, True)
    cross = exact(dot_tn, stat, (pick == 1).astype(F32).astype(BF), 3, True)
    inv = lax.rsqrt(square / INNER + EPSILON)
    inv_ref[...] = inv
    back = inv * inv * inv * (cross / INNER)
    rise = jnp.exp(cum_ref[...]) * col_ref[:, 3:4]
    queries_t = jnp.transpose(bc_ref[:, STATE:SHARED].astype(F32)).astype(BF)
    for pair, (at, width) in enumerate(pair_widths(channels)):
        lanes = slice(at, at + width)
        gate = gate_ref[:, lanes].astype(F32)
        act, slope = act_and_slope(gate)
        y = y_ref[:, lanes]
        gated = y * act
        gng = gng_ref[:, lanes].astype(F32)
        along = inv[:, :width]
        grad = along * (gain_ref[0:1, lanes] * gng) - gated * back[:, :width]
        gaingrad_ref[0:1, lanes] += jnp.sum(gng * gated * along, axis=0, keepdims=True)
        gy = (grad * act).astype(BF)
        gy_ref[:, lanes] = gy
        gi_ref[:, lanes] = (grad * y * slope).astype(BF)
        gyr = (gy.astype(F32) * spread(rise, pair, width)).astype(BF)
        hold[:, lanes] = dot_nn(queries_t, gyr) + fac_ref[0, 0:1, lanes] * hold[:, lanes]

    @pl.when(i == pl.num_programs(0) - 1)
    def _():
        flow_ref[...] = hold[...].astype(BF)


def conv_back(post, u, taps, masks, kgrad_ref, lanes):
    full = post.shape[0] + HALO
    pad = jnp.zeros((HALO, post.shape[1]), F32)
    total = jnp.concatenate([pad, post * taps[3:4]], axis=0)
    kgrad_ref[4:5, lanes] += jnp.sum(post, axis=0, keepdims=True)
    kgrad_ref[3:4, lanes] += jnp.sum(post * u[HALO:], axis=0, keepdims=True)
    for j in (1, 2, 3):
        here = post * masks[j - 1]
        kgrad_ref[3 - j : 4 - j, lanes] += jnp.sum(
            here * pltpu.roll(u, j, 0)[HALO:], axis=0, keepdims=True
        )
        wide = jnp.concatenate([pad, here * taps[3 - j : 4 - j]], axis=0)
        total = total + pltpu.roll(wide, full - j, 0)
    return total


def fourth_kernel(
    gy_ref, x_ref, xs_ref, slope_ref, y_ref, bc_ref, slopes_ref, step_ref, cum_ref, sgm_ref, pre_ref,
    ht_ref, hn_ref, fac_ref, enter_ref, km_ref, ks_ref, hp_ref, skip_ref, expand_ref, col_ref, seg_ref,
    g_ref, kmgrad_ref, ksgrad_ref, head_ref, skipgrad_ref,
    hold, edge,
):
    i = pl.program_id(0)
    k = pl.num_programs(0) - 1 - i
    channels = x_ref.shape[1]

    @pl.when(i == 0)
    def _():
        hold[...] = enter_ref[...].astype(F32)
        edge[...] = jnp.zeros_like(edge)
        kmgrad_ref[...] = jnp.zeros_like(kmgrad_ref)
        ksgrad_ref[...] = jnp.zeros_like(ksgrad_ref)
        head_ref[...] = jnp.zeros_like(head_ref)
        skipgrad_ref[...] = jnp.zeros_like(skipgrad_ref)

    base = pl.multiple_of(k * STRETCH, HALO)
    rows = pl.ds(base, STRETCH + HALO)
    mine = pl.ds(base + HALO, STRETCH)
    col = col_ref[...]
    masks = [col[:, j : j + 1] for j in range(3)]
    alive, ends = col[:, 3:4], col[:, 4:5]
    keys, queries = bc_ref[:, 0:STATE], bc_ref[:, STATE:SHARED]
    queries_t = jnp.transpose(queries.astype(F32)).astype(BF)
    valid = doc_mask(col[:, 5:6], seg_ref[0:1, :], (STRETCH, STRETCH), True)
    gram = jnp.where(valid, dot_nt(keys, queries), 0.0)
    step, cum = step_ref[...], cum_ref[...]
    cum_t = jnp.transpose(cum)
    rise = jnp.exp(cum) * alive
    ef = jnp.exp(cum[STRETCH - 1 : STRETCH] - cum) * ends
    gram_top = jnp.zeros((HALF, STRETCH), F32)
    gram_bottom = jnp.zeros((HALF, HALF), F32)
    grad_keys = jnp.zeros((STRETCH, STATE), F32)
    grad_queries = jnp.zeros((STRETCH, STATE), F32)
    rowterm = jnp.zeros((STRETCH, LANES), F32)
    colterm = jnp.zeros((STRETCH, LANES), F32)
    endterm = jnp.zeros((8, LANES), F32)
    for pair, (at, width) in enumerate(pair_widths(channels)):
        lanes = slice(at, at + width)
        expand = expand_ref[lanes, :]
        gy, xs = gy_ref[:, lanes], xs_ref[:, lanes]
        gyf, xf = gy.astype(F32), x_ref[:, lanes].astype(F32)
        skip = skip_ref[0:1, lanes]
        top = bottom = 0.0
        for which, mask in enumerate(head_masks(width)):
            h = 2 * pair + which
            here = masked(gy, mask)
            down, across = cum[:, h : h + 1], cum_t[h : h + 1, :]
            decay = jnp.exp(jnp.minimum(across - down[:HALF], 0.0))
            top = top + dot_nn((decay * gram[:HALF]).astype(BF), here)
            gram_top = gram_top + dot_nt(xs[:HALF], here) * decay
            decay = jnp.exp(jnp.minimum(across[:, HALF:] - down[HALF:], 0.0))
            bottom = bottom + dot_nn((decay * gram[HALF:, HALF:]).astype(BF), here[HALF:])
            gram_bottom = gram_bottom + dot_nt(xs[HALF:], here[HALF:]) * decay
        grad_xs = jnp.concatenate([top, bottom], axis=0)
        after = hold[:, lanes]
        low = after.astype(BF)
        efs = spread(ef, pair, width)
        grad_xs = grad_xs + dot_nn(keys, low) * efs
        gyr = (gyf * spread(rise, pair, width)).astype(BF)
        xe = (xs.astype(F32) * efs).astype(BF)
        grad_queries = grad_queries + dot_nt(gyr, ht_ref[0, :, lanes])
        grad_keys = grad_keys + dot_nt(xe, low)
        ended = jnp.sum(after * hn_ref[0, :, lanes].astype(F32), axis=0, keepdims=True)
        endterm = endterm + exact(dot_nn, jnp.broadcast_to(ended, (8, width)), expand, 3, True)
        hold[:, lanes] = dot_nn(queries_t, gyr) + fac_ref[0, 0:1, lanes] * after
        rowterm = rowterm + exact(dot_nn, gyf * (y_ref[:, lanes] - skip * xf), expand, 2, True)
        colterm = colterm + exact(dot_nn, xf * grad_xs, expand, 2, True)
        skipgrad_ref[0:1, lanes] += jnp.sum(gyf * xf, axis=0, keepdims=True)
        grad_x = grad_xs * spread(step, pair, width) + skip * gyf
        post = grad_x * slope_ref[:, lanes].astype(F32)
        at_g = slice(LEAD + at, LEAD + at + width)
        u = pre_ref[rows, at_g].astype(F32)
        total = conv_back(post, u, km_ref[:, lanes], masks, kmgrad_ref, lanes)
        g_ref[mine, at_g] = total[HALO:].astype(BF)
        tail = pl.ds(base + STRETCH, HALO)
        g_ref[tail, at_g] = (total[STRETCH:] + edge[:, at_g]).astype(BF)
        edge[:, at_g] = total[:HALO]

    gram_top = jnp.where(valid[:HALF], gram_top, 0.0).astype(BF)
    gram_bottom = jnp.where(valid[HALF:, HALF:], gram_bottom, 0.0).astype(BF)
    grad_keys = grad_keys + jnp.concatenate(
        [dot_nn(gram_top, queries), dot_nn(gram_bottom, queries[HALF:])], axis=0
    )
    lower = jnp.concatenate([jnp.zeros((HALF, HALF), BF), gram_bottom], axis=1)
    gram_all = jnp.concatenate([gram_top, lower], axis=0)
    grad_queries = grad_queries + dot_tn(gram_all, keys)
    post = jnp.concatenate([grad_keys, grad_queries], axis=1) * slopes_ref[...].astype(F32)
    u = pre_ref[rows, 0:SHARED].astype(F32)
    total = conv_back(post, u, ks_ref[...], masks, ksgrad_ref, slice(0, SHARED))
    g_ref[mine, 0:SHARED] = total[HALO:].astype(BF)
    tail = pl.ds(base + STRETCH, HALO)
    g_ref[tail, 0:SHARED] = (total[STRETCH:] + edge[:, 0:SHARED]).astype(BF)
    edge[:, 0:SHARED] = total[:HALO]

    rate = -jnp.exp(hp_ref[0:1, :])
    grad_cum = rowterm - step * colterm
    at_end = iota((STRETCH, LANES), 0) == STRETCH - 1
    grad_cum = grad_cum + jnp.where(at_end, endterm[0:1], 0.0)
    upper = (iota((STRETCH, STRETCH), 1) >= iota((STRETCH, STRETCH), 0)).astype(F32).astype(BF)
    grad_log = exact(dot_nn, upper, grad_cum, 3, False)
    grad_pre = (colterm + grad_log * rate) * sgm_ref[...]
    g_ref[mine, SHARED:LEAD] = grad_pre.astype(BF)
    head_ref[0:1, :] += jnp.sum(grad_log * step, axis=0, keepdims=True) * rate
    head_ref[1:2, :] += jnp.sum(grad_pre, axis=0, keepdims=True)

    @pl.when(k == 0)
    def _():
        g_ref[0:HALO, 0:SHARED] = edge[:, 0:SHARED].astype(BF)
        g_ref[0:HALO, LEAD:] = edge[:, LEAD:].astype(BF)
        g_ref[0:HALO, SHARED:LEAD] = jnp.zeros((HALO, LANES), BF)
        wide = jnp.broadcast_to(skipgrad_ref[0:1, :], (8, channels))
        head_ref[2:3, :] = exact(dot_nn, wide, expand_ref[...], 3, True)[0:1]


def normed_kernel(chunk, gi_ref, g_ref, w0_ref, w1_ref, normed_ref, halo_ref, out_ref, cross_ref, gain_ref, acc):
    i = pl.program_id(0)
    last = i == pl.num_programs(0) - 1
    rows = gi_ref.shape[0]

    @pl.when(i == 0)
    def _():
        gain_ref[...] = jnp.zeros_like(gain_ref)

    cross = jnp.zeros((rows, LANES), F32)
    for at in range(0, out_ref.shape[1], chunk):
        lanes = slice(at, at + chunk)
        acc[...] = dot_nt(gi_ref[...], w0_ref[lanes, :]) + dot_nt(g_ref[...], w1_ref[lanes, :])
        if halo_ref is not None:

            @pl.when(last)
            def _():
                acc[rows - HALO :, :] += halo_ref[:, lanes]

        total = acc[...]
        out_ref[:, lanes] = total.astype(BF)
        inner = total * normed_ref[:, lanes].astype(F32)
        gain_ref[0:1, lanes] += jnp.sum(inner, axis=0, keepdims=True)
        for part in range(0, chunk, LANES):
            cross = cross + inner[:, part : part + LANES]
    cross_ref[...] = exact(dot_nt, jnp.ones((8, LANES), BF), cross, 3, False)


def weight_kernel(normed_ref, g_ref, out_ref):
    out_ref[...] = dot_tn(normed_ref[...], g_ref[...]).astype(BF)


def gate_out_kernel(normed_ref, gi_ref, cot_ref, inv_ref, gg_ref, out_ref):
    channels = gi_ref.shape[1]
    out_ref[:, 0:channels] = dot_tn(normed_ref[HALO:, :], gi_ref[...]).astype(BF)
    for at in range(0, out_ref.shape[0], LANES):
        lanes = slice(at, at + LANES)
        scaled = (cot_ref[:, lanes].astype(F32) * inv_ref[...]).astype(BF)
        out_ref[lanes, channels:] = dot_tn(scaled, gg_ref[...]).astype(BF)


def whole(array):
    rank = len(array.shape)
    return pl.BlockSpec(array.shape, lambda *_: (0,) * rank)


def call(kernel, grid, ins, in_specs, outs, out_specs, scratch=(), flops=0, prefetch=0):
    moved = sum(a.size * a.dtype.itemsize for a in (*ins, *outs))
    return pl.pallas_call(
        kernel,
        out_shape=outs,
        grid_spec=pltpu.PrefetchScalarGridSpec(
            num_scalar_prefetch=prefetch,
            grid=grid,
            in_specs=in_specs,
            out_specs=out_specs,
            scratch_shapes=list(scratch),
        ),
        compiler_params=pltpu.CompilerParams(dimension_semantics=("arbitrary",) * len(grid)),
        cost_estimate=pl.CostEstimate(flops=int(flops), bytes_accessed=int(moved), transcendentals=0),
    )(*ins)


def shape(dims, kind):
    return jax.ShapeDtypeStruct(dims, kind)


def per_device(
    tokens, segments, norm_gain, proj_main, proj_shared, proj_step, conv_main, conv_shared,
    head_params, gate_gain, output_projection, cotangent,
):
    _, length, width = tokens.shape
    nf, nc, nt = lax.axis_size("fsdp"), lax.axis_size("ctx"), lax.axis_size("tp")
    assert nf == 4 and nc == 2
    f, c, t = lax.axis_index("fsdp"), lax.axis_index("ctx"), lax.axis_index("tp")
    heads = head_params.shape[1]
    channels = heads * HEADDIM
    nb = length // STRETCH
    chunk = width // nf
    half = chunk // 2
    share = width // nt
    line = nt == nf
    rot = t if line else jnp.zeros_like(t)
    ext = HALO + length
    both = ("fsdp", "ctx")
    spots = [(i, j) for i in range(nf) for j in range(nc)]
    role = [(i * nc + j, (i ^ (1 + j)) * nc + j) for i, j in spots]
    turn = [(i * nc + j, (i ^ (2 - j)) * nc + j) for i, j in spots]
    swap = [(0, 1), (1, 0)]

    def slot(a):
        return lax.rem(a + nf - rot, nf)

    def tp_sum(v):
        if not line:
            return lax.psum(v, "tp")
        one, two, three = (
            lax.ppermute(v, "tp", [(i, i ^ m) for i in range(nt)]) for m in (1, 2, 3)
        )
        return (v + one) + (two + three)

    def gather_rows(shard):
        columns = shard.shape[1]
        pieces = shard.reshape(2, half, columns)
        near = lax.ppermute(pieces, both, role)
        far = lax.ppermute(lax.dynamic_slice_in_dim(near, c, 1, 0), both, turn)
        near_other = lax.ppermute(near, "ctx", swap)
        far_other = lax.ppermute(far, "ctx", swap)
        out = jnp.zeros((2 * nf, half, columns), shard.dtype)
        for piece, place in (
            (pieces, 2 * slot(f)),
            (near, 2 * slot(f ^ (1 + c))),
            (near_other, 2 * slot(f ^ (2 - c))),
            (far, 2 * slot(f ^ 3) + c),
            (far_other, 2 * slot(f ^ 3) + 1 - c),
        ):
            out = lax.dynamic_update_slice_in_dim(out, piece, place, 0)
        return out.reshape(nf * chunk, columns)

    def scatter_rows(grad):
        columns = grad.shape[1]
        pieces = grad.reshape(2 * nf, half, columns)

        def take(place, n):
            return lax.dynamic_slice_in_dim(pieces, place, n, 0)

        def add(a, b):
            return (a.astype(F32) + b.astype(F32)).astype(BF)

        sent = jnp.concatenate(
            [
                take(2 * slot(f ^ (2 - c)), 2),
                take(2 * slot(f ^ 3) + 1 - c, 1),
                take(2 * slot(f) + 1 - c, 1),
            ],
            axis=0,
        )
        got = lax.ppermute(sent, "ctx", swap)
        far = lax.ppermute(add(take(2 * slot(f ^ 3) + c, 1), got[2:3]), both, turn)
        near = take(2 * slot(f ^ (1 + c)), 2).astype(F32) + got[0:2].astype(F32)
        which = iota((2, 1, 1), 0) == c
        near = (near + jnp.where(which, far.astype(F32), 0.0)).astype(BF)
        near = lax.ppermute(near, both, role)
        other = lax.ppermute(lax.dynamic_slice_in_dim(near, 1 - c, 1, 0), "ctx", swap)
        own = take(2 * slot(f) + c, 1).astype(F32) + got[3:4].astype(F32)
        own = own + lax.dynamic_slice_in_dim(near, c, 1, 0).astype(F32) + other.astype(F32)
        return own[0]

    def scatter_tp(full):
        if not line:
            return lax.psum_scatter(full, "tp", scatter_dimension=1, tiled=True).astype(F32)

        def piece(q):
            return full[:, q * chunk : (q + 1) * chunk]

        right = left = None
        for r in range(1, nt):
            a, b = piece(nt - r), piece(r)
            if right is not None:
                a = (a.astype(F32) + right.astype(F32)).astype(BF)
                b = (b.astype(F32) + left.astype(F32)).astype(BF)
            right = lax.ppermute(a, "tp", [(i, i + 1) for i in range(r)])
            left = lax.ppermute(b, "tp", [(i, i - 1) for i in range(nt - r, nt)])
        return piece(0).astype(F32) + right.astype(F32) + left.astype(F32)

    tokens2, cot2 = tokens[0], cotangent[0]
    halo = lax.ppermute(tokens2[length - HALO :], "ctx", [(0, 1)])
    shard_in = jnp.concatenate(
        [proj_shared, jnp.pad(proj_step, ((0, 0), (0, LANES - heads))), proj_main[1]], axis=1
    )
    w_in = gather_rows(shard_in)
    w_gate = gather_rows(proj_main[0])
    w_out = gather_rows(jnp.transpose(output_projection))

    padded = jnp.concatenate([jnp.full((HALO,), -1, jnp.int32), segments[0]])
    seg_ext = lax.dynamic_slice_in_dim(padded, c * length, ext, 0)
    seg = seg_ext[HALO:]
    seg_before = jnp.repeat(seg_ext[HALO - 1 : ext - 1 : STRETCH], STRETCH)
    seg_last = jnp.repeat(seg[STRETCH - 1 :: STRETCH], STRETCH)
    col = jnp.stack(
        [seg == seg_ext[HALO - j : ext - j] for j in (1, 2, 3)]
        + [seg == seg_before, seg == seg_last, seg, seg, seg],
        axis=1,
    ).astype(F32)
    seg_row = jnp.broadcast_to(seg.astype(F32)[None], (8, length))

    km = jnp.pad(conv_main, ((0, 3), (0, 0)))
    ks = jnp.pad(conv_shared, ((0, 3), (0, 0)))
    hp = jnp.pad(head_params, ((0, 5), (0, LANES - heads)))
    skip = jnp.broadcast_to(jnp.repeat(head_params[2], HEADDIM)[None], (8, channels))
    gate_row = jnp.broadcast_to(gate_gain[None], (8, channels))
    gain_row = jnp.broadcast_to(norm_gain[None], (8, width))
    expand = (
        jnp.arange(channels)[:, None] // HEADDIM == jnp.arange(LANES)[None]
    ).astype(BF)

    def block(columns, back=False):
        if back:
            return pl.BlockSpec((STRETCH, columns), lambda i, *_: (nb - 1 - i, 0))
        return pl.BlockSpec((STRETCH, columns), lambda i, *_: (i, 0))

    def across(back=False):
        if back:
            return pl.BlockSpec((8, STRETCH), lambda i, *_: (0, nb - 1 - i))
        return pl.BlockSpec((8, STRETCH), lambda i, *_: (0, i))

    def stacked(rows, columns, back=False, off=0):
        if back:
            return pl.BlockSpec((1, rows, columns), lambda i, *_: (nb - 1 - i + off, 0, 0))
        return pl.BlockSpec((1, rows, columns), lambda i, *_: (i + off, 0, 0))

    ins = (rot.reshape(1).astype(jnp.int32), tokens2, halo, cot2, gain_row)
    outs = (shape((ext, width), BF), shape((length, chunk), BF), shape((length, LANES), F32), shape((length, width), BF))
    normed, own_tokens, inv_rms, cot_q = call(
        functools.partial(prep_kernel, chunk), (nb,), ins,
        [block(width), whole(halo), block(width), whole(gain_row)],
        outs, [whole(outs[0]), block(chunk), block(LANES), block(width)], prefetch=1,
    )
    if not line:
        own_tokens = lax.dynamic_slice_in_dim(tokens2, t * share, share, 1)
        own_cot = lax.dynamic_slice_in_dim(cot2, t * share, share, 1)
    else:
        own_cot = cot_q[:, :chunk]

    def matmul(a, b, dims):
        return lax.dot_general(a, b, (dims, ((), ())), preferred_element_type=F32).astype(BF)

    pre = matmul(normed, w_in, ((1,), (0,)))

    outs = (
        shape((length, channels), BF), shape((length, channels), BF), shape((length, channels), BF),
        shape((length, SHARED), BF), shape((length, SHARED), BF),
        shape((length, LANES), F32), shape((length, LANES), F32), shape((length, LANES), F32),
        shape((nb, STATE, channels), F32), shape((nb, 8, channels), F32), shape((STATE, channels), BF),
    )
    ins = (pre, km, ks, hp, col, expand)
    x, xs, slope, bc, slopes, step, cum, sgm, states, fac, total = call(
        first_kernel, (nb,), ins,
        [whole(pre), whole(km), whole(ks), whole(hp), block(8), whole(expand)],
        outs,
        [block(channels)] * 3 + [block(SHARED)] * 2 + [block(LANES)] * 3
        + [stacked(STATE, channels), stacked(8, channels), whole(outs[-1])],
        scratch=[pltpu.VMEM((STATE, channels), F32)],
        flops=2 * length * STATE * channels,
    )
    enter = lax.ppermute(total, "ctx", [(0, 1)])
    gate = matmul(normed[HALO:], w_gate, ((1,), (0,)))
    gng = matmul(cot_q, w_out, ((1,), (0,)))

    outs = (
        shape((length, channels), F32), shape((length, channels), BF), shape((8, length), F32),
        shape((nb + 1, STATE, channels), BF),
    )
    ins = (bc, x, xs, cum, states, fac, enter, gate, gng, gate_row, skip, col, seg_row)
    y, gg, stat, hist = call(
        second_kernel, (nb,), ins,
        [
            block(SHARED), block(channels), block(channels), block(LANES), stacked(STATE, channels),
            stacked(8, channels), whole(enter), block(channels), block(channels), whole(gate_row),
            whole(skip), block(8), across(),
        ],
        outs, [block(channels), block(channels), across(), whole(outs[3])],
        scratch=[pltpu.VMEM((STATE, channels), F32)],
        flops=8 * length * STRETCH * channels,
    )
    stat = tp_sum(stat)
    out_part = matmul(gg, w_out, ((1,), (1,)))
    out_sum = scatter_tp(out_part)

    outs = (
        shape((length, channels), BF), shape((length, channels), BF), shape((length, LANES), F32),
        shape((STATE, channels), BF), shape((8, channels), F32),
    )
    ins = (stat, y, gate, gng, gate_row, bc, cum, fac, col)
    gy, gi, inv_gate, flow, gate_grad = call(
        third_kernel, (nb,), ins,
        [
            across(True), block(channels, True), block(channels, True), block(channels, True), whole(gate_row),
            block(SHARED, True), block(LANES, True), stacked(8, channels, True), block(8, True),
        ],
        outs, [block(channels, True), block(channels, True), block(LANES, True), whole(outs[3]), whole(outs[4])],
        scratch=[pltpu.VMEM((STATE, channels), F32)],
        flops=2 * length * STATE * channels,
    )
    leaving = lax.ppermute(flow, "ctx", [(1, 0)])
    output = (own_tokens.astype(F32) + inv_gate[:, :1] * out_sum).astype(BF)

    wide = 2 * channels
    outs = shape((width, wide), BF)
    ins = (normed, gi, cot_q, inv_gate, gg)
    grad_go = call(
        gate_out_kernel, (nf,), ins,
        [
            pl.BlockSpec((ext, chunk), lambda i: (0, i)), whole(gi),
            pl.BlockSpec((length, chunk), lambda i: (0, i)), whole(inv_gate), whole(gg),
        ],
        (outs,), [pl.BlockSpec((chunk, wide), lambda i: (i, 0))],
        flops=2 * length * width * wide,
    )[0]
    grad_go = scatter_rows(grad_go)

    lead = LEAD + channels
    outs = (
        shape((ext, lead), BF), shape((8, channels), F32), shape((8, SHARED), F32), shape((8, LANES), F32),
        shape((8, channels), F32),
    )
    ins = (
        gy, x, xs, slope, y, bc, slopes, step, cum, sgm, pre, hist, hist, fac, leaving, km, ks, hp, skip, expand,
        col, seg_row,
    )
    g_in, km_grad, ks_grad, head_grad, _ = call(
        fourth_kernel, (nb,), ins,
        [block(channels, True)] * 5 + [block(SHARED, True)] * 2 + [block(LANES, True)] * 3
        + [
            whole(pre), stacked(STATE, channels, True), stacked(STATE, channels, True, 1),
            stacked(8, channels, True), whole(leaving), whole(km), whole(ks), whole(hp), whole(skip),
            whole(expand), block(8, True), across(True),
        ],
        outs, [whole(o) for o in outs],
        scratch=[pltpu.VMEM((STATE, channels), F32), pltpu.VMEM((HALO, lead), F32)],
        flops=16 * length * STRETCH * channels,
    )

    edge = lax.dot_general(g_in[:HALO], w_in, (((1,), (1,)), ((), ())), preferred_element_type=F32)
    edge = lax.ppermute(edge, "ctx", [(1, 0)])
    mid = length // 2
    parts = []
    for at in (0, mid):
        rows = slice(at, at + mid)
        last = at + mid == length
        ins = (gi[rows], g_in[HALO:][rows], w_gate, w_in, normed[HALO:][rows]) + ((edge,) if last else ())
        outs = (shape((mid, width), BF), shape((8, mid), F32), shape((8, width), F32))
        kernel = functools.partial(normed_kernel, chunk)
        if not last:
            kernel = functools.partial(no_halo, chunk)
        parts.append(
            call(
                kernel, (mid // STRETCH,), ins,
                [block(channels), block(lead), whole(w_gate), whole(w_in), block(width)]
                + ([whole(edge)] if last else []),
                outs, [block(width), across(), whole(outs[2])],
                scratch=[pltpu.VMEM((STRETCH, chunk), F32)],
                flops=2 * mid * width * (lead + channels),
            )
        )
    cross = tp_sum(jnp.concatenate([parts[0][1], parts[1][1]], axis=1))
    normed_sum = jnp.concatenate([scatter_tp(parts[0][0]), scatter_tp(parts[1][0])], axis=0)

    outs = shape((width, lead), BF)
    grad_w = call(
        weight_kernel, (nf,), (normed, g_in),
        [pl.BlockSpec((ext, chunk), lambda i: (0, i)), whole(g_in)],
        (outs,), [pl.BlockSpec((chunk, lead), lambda i: (i, 0))],
        flops=2 * ext * width * lead,
    )[0]
    grad_w = scatter_rows(grad_w)

    gain_part = (parts[0][2][0] + parts[1][2][0]).reshape(nf, chunk)
    gain_part = jnp.roll(gain_part, rot, axis=0)
    n_ks = 5 * SHARED
    flat = jnp.concatenate(
        [
            gain_part.reshape(-1), ks_grad[:5].reshape(-1), km_grad[:5].reshape(-1),
            gate_grad[0], head_grad[:3, :heads].reshape(-1),
        ]
    )
    used = flat.shape[0]
    flat = jnp.pad(flat, (0, -used % 1024)).reshape(-1, LANES)
    flat = flat + lax.ppermute(flat, "ctx", swap)
    for m in (1, 2):
        flat = flat + lax.ppermute(flat, "fsdp", [(i, i ^ m) for i in range(nf)])
    n_tp = width + n_ks
    rows_tp = -(-n_tp // 1024) * 8
    over_tp = tp_sum(flat[:rows_tp]).reshape(-1)
    flat = flat.reshape(-1)
    grad_gain = lax.dynamic_slice_in_dim(over_tp, t * share, share, 0)
    own_gain = lax.dynamic_slice_in_dim(norm_gain, t * share, share, 0)
    grad_gain = grad_gain / own_gain
    grad_ks = over_tp[width:n_tp].reshape(5, SHARED)
    grad_km = flat[n_tp : n_tp + 5 * channels].reshape(5, channels)
    at = n_tp + 5 * channels
    grad_gate_gain = flat[at : at + channels]
    grad_head = flat[at + channels : at + channels + 3 * heads].reshape(3, heads)

    inv = inv_rms[:, :1]
    grad_tokens = (
        inv * own_gain * normed_sum
        - own_tokens.astype(F32) * (inv * inv * (cross[0][:, None] / width))
        + own_cot.astype(F32)
    )
    return (
        output[None],
        grad_tokens[None],
        grad_gain,
        jnp.stack([grad_go[:, :channels], grad_w[:, LEAD:]]),
        tp_sum(grad_w[:, :SHARED]),
        grad_w[:, SHARED : SHARED + heads],
        grad_km,
        grad_ks,
        grad_head,
        grad_gate_gain,
        jnp.transpose(grad_go[:, channels:]),
    )


def no_halo(chunk, gi_ref, g_ref, w0_ref, w1_ref, normed_ref, out_ref, cross_ref, gain_ref, acc):
    normed_kernel(chunk, gi_ref, g_ref, w0_ref, w1_ref, normed_ref, None, out_ref, cross_ref, gain_ref, acc)


def solution(mesh):
    return jax.shard_map(
        per_device,
        mesh=mesh,
        in_specs=(
            P("fsdp", "ctx", None),
            P("fsdp", None),
            P(),
            P(None, "fsdp", "tp"),
            P("fsdp", None),
            P("fsdp", "tp"),
            P(None, "tp"),
            P(),
            P(None, "tp"),
            P("tp"),
            P("tp", "fsdp"),
            P("fsdp", "ctx", None),
        ),
        out_specs=(
            P("fsdp", "ctx", "tp"),
            P("fsdp", "ctx", "tp"),
            P("tp"),
            P(None, ("fsdp", "ctx"), "tp"),
            P(("fsdp", "ctx"), None),
            P(("fsdp", "ctx"), "tp"),
            P(None, "tp"),
            P(),
            P(None, "tp"),
            P("tp"),
            P("tp", ("fsdp", "ctx")),
        ),
        check_vma=False,
    )
```

```python
import functools

import jax
import jax.numpy as jnp
from jax import lax
from jax.experimental import pallas as pl
from jax.experimental.pallas import tpu as pltpu
from jax.sharding import PartitionSpec as P


HEADDIM = 64
STATE = 128
STRETCH = 256
HALF = STRETCH // 2
INNER = 3072
EPSILON = 1e-05
HALO = 16
LANES = 128
SHARED = 2 * STATE
LEAD = SHARED + LANES
BF = jnp.bfloat16
F32 = jnp.float32
VMEM_LIMIT = 60 * 2**20


def dot_nn(a, b):
    return lax.dot_general(a, b, (((1,), (0,)), ((), ())), preferred_element_type=F32)


def dot_nt(a, b):
    return lax.dot_general(a, b, (((1,), (1,)), ((), ())), preferred_element_type=F32)


def dot_tn(a, b):
    return lax.dot_general(a, b, (((0,), (0,)), ((), ())), preferred_element_type=F32)


def split(v, n):
    terms = []
    for _ in range(n):
        high = v.astype(BF)
        terms.append(high)
        v = v - high.astype(F32)
    return terms


def exact(dot, a, b, n, left):
    total = None
    for term in split(a if left else b, n):
        part = dot(term, b) if left else dot(a, term)
        total = part if total is None else total + part
    return total


def iota(shape, axis):
    return lax.broadcasted_iota(jnp.int32, shape, axis)


def pair_widths(channels):
    return [(at, min(LANES, channels - at)) for at in range(0, channels, LANES)]


def spread(v, pair, width):
    first = v[:, 2 * pair : 2 * pair + 1]
    if width == HEADDIM:
        return jnp.broadcast_to(first, (v.shape[0], HEADDIM))
    second = v[:, 2 * pair + 1 : 2 * pair + 2]
    lane = iota((v.shape[0], LANES), 1)
    return jnp.where(lane < HEADDIM, first, second)


def head_masks(width):
    if width == HEADDIM:
        return [None]
    lane = iota((1, LANES), 1)
    return [(lane < HEADDIM).astype(F32).astype(BF), (lane >= HEADDIM).astype(F32).astype(BF)]


def masked(v, mask):
    return v if mask is None else v * mask


def sigmoid(v):
    return 1.0 / (1.0 + jnp.exp(-v))


def pack_in_kernel(shared_ref, step_ref, main_ref, out_ref):
    out_ref[:, 0:SHARED] = shared_ref[...]
    out_ref[:, SHARED:LEAD] = jnp.zeros((out_ref.shape[0], LANES), BF)
    out_ref[:, SHARED : SHARED + step_ref.shape[1]] = step_ref[...]
    out_ref[:, LEAD:] = main_ref[0]


def pack_go_kernel(main_ref, out_proj_ref, out_ref):
    channels = main_ref.shape[2]
    wide = out_ref.shape[1] // 2
    if wide != channels:
        out_ref[...] = jnp.zeros_like(out_ref)
    out_ref[:, 0:channels] = main_ref[0]
    out_ref[:, wide : wide + channels] = jnp.transpose(out_proj_ref[...].astype(F32)).astype(BF)


def fetches(idx_ref, pieces, held, sems, columns=None):
    own, near, near_other, far, far_other = pieces
    half = held.shape[1] // 2
    c = idx_ref[4]
    top, bottom = (pl.ds(pl.multiple_of(h * half, HALO), half) for h in (c, 1 - c))
    targets = (
        (own, held.at[idx_ref[0]]),
        (near, held.at[idx_ref[1]]),
        (near_other, held.at[idx_ref[2]]),
        (far, held.at[idx_ref[3], top]),
        (far_other, held.at[idx_ref[3], bottom]),
    )
    return [
        pltpu.make_async_copy(
            source if columns is None else source.at[:, columns], target, sems.at[i]
        )
        for i, (source, target) in enumerate(targets)
    ]


def fetch_all(copies):
    for copy in copies:
        copy.start()
    for copy in copies:
        copy.wait()


def prep_kernel(
    chunk, idx_ref, tok_ref, halo_ref, cot_ref, gain_ref, seg_ref, normed_ref, nhalo_ref, own_ref, owncot_ref,
    inv_ref, tab_ref,
):
    k = pl.program_id(0)

    def scale_of(x):
        return lax.rsqrt(jnp.mean(x * x, axis=-1, keepdims=True) + EPSILON)

    x = tok_ref[...].astype(F32)
    inv = scale_of(x)
    inv_ref[...] = jnp.broadcast_to(inv, inv_ref.shape)
    normed_ref[...] = (x * inv * gain_ref[0:1, :]).astype(BF)
    mine = pl.ds(pl.multiple_of(idx_ref[5] * chunk, LANES), chunk)
    own_ref[...] = tok_ref[:, mine]
    owncot_ref[...] = cot_ref[:, mine]

    @pl.when(k == 0)
    def _():
        x = halo_ref[...].astype(F32)
        nhalo_ref[...] = (x * scale_of(x) * gain_ref[0:1, :]).astype(BF)

    start = (idx_ref[4] * pl.num_programs(0) + k) * STRETCH
    here = seg_ref[0:1, pl.ds(pl.multiple_of(start, LANES), STRETCH)].astype(F32)
    before = seg_ref[0:1, pl.ds(pl.multiple_of(jnp.maximum(start - LANES, 0), LANES), LANES)].astype(F32)
    before = jnp.where(start == 0, -1.0, before)
    both = jnp.broadcast_to(jnp.concatenate([before, here], axis=1), (8, LANES + STRETCH))
    row = iota((8, STRETCH), 0)
    tab = both[:, LANES:]
    for j in (1, 2, 3):
        tab = jnp.where(row == j, pltpu.roll(both, j, 1)[:, LANES:], tab)
    tab = jnp.where(row == 4, before[:, LANES - 1 :], tab)
    tab_ref[...] = jnp.where(row == 5, here[:, STRETCH - 1 :], tab)


def columns_of(tab_ref):
    tab = tab_ref[...]
    row = iota(tab.shape, 0)
    test = jnp.where(tab == tab[0:1], 1.0, 0.0)
    value = jnp.where(row == 0, tab, test).astype(BF)
    eye = (iota((8, LANES), 0) == iota((8, LANES), 1)).astype(F32).astype(BF)
    return dot_tn(value, eye)


def load_heads(hp_ref, wide_ref):
    wide_ref[...] = jnp.zeros_like(wide_ref)
    wide_ref[0:3, 0 : hp_ref.shape[1]] = hp_ref[...]


def expand_of(channels):
    head = jnp.right_shift(iota((channels, LANES), 0), 6)
    return (head == iota((channels, LANES), 1)).astype(F32).astype(BF)


def skip_of(wide_ref, expand):
    return exact(dot_nt, jnp.broadcast_to(wide_ref[2:3, :], (8, LANES)), expand, 3, True)


def conv_taps(u, taps, masks):
    total = taps[4:5] + taps[3:4] * u[HALO:]
    for j in (1, 2, 3):
        total = total + taps[3 - j : 4 - j] * (pltpu.roll(u, j, 0)[HALO:] * masks[j - 1])
    return total


def act_and_slope(v):
    sig = sigmoid(v)
    act = v * sig
    return act, sig + act * (1.0 - sig)


def first_kernel(
    idx_ref, own_ref, near_ref, nearx_ref, far_ref, farx_ref, normed_ref, nhalo_ref, km_ref, ks_ref, heads_ref, tab_ref,
    pre_ref, phalo_ref, x_ref, xs_ref, slope_ref, bc_ref, slopes_ref, step_ref, cum_ref, sgm_ref, state_ref, fac_ref,
    total_ref,
    held, sems, edge, carry, hp_ref, expand_ref,
):
    k = pl.program_id(0)
    channels = x_ref.shape[1]
    count, chunk = held.shape[0], held.shape[1]

    def project(rows):
        total = dot_nn(rows[:, :chunk], held[0])
        for a in range(1, count):
            total = total + dot_nn(rows[:, a * chunk : (a + 1) * chunk], held[a])
        return total.astype(BF)

    @pl.when(k == 0)
    def _():
        copies = fetches(idx_ref, (own_ref, near_ref, nearx_ref, far_ref, farx_ref), held, sems)
        for copy in copies:
            copy.start()
        carry[...] = jnp.zeros_like(carry)
        load_heads(heads_ref, hp_ref)
        expand_ref[...] = expand_of(channels)
        for copy in copies:
            copy.wait()
        before = project(nhalo_ref[...])
        phalo_ref[...] = before
        edge[...] = before

    pre_ref[...] = project(normed_ref[...])

    def ext(lanes):
        return jnp.concatenate([edge[:, lanes].astype(F32), pre_ref[:, lanes].astype(F32)], axis=0)

    col = columns_of(tab_ref)
    masks = [col[:, j : j + 1] for j in (1, 2, 3)]
    alive, ends = col[:, 4:5], col[:, 5:6]

    raw = pre_ref[:, SHARED:LEAD].astype(F32)
    pre = raw + hp_ref[1:2, :]
    soft = jnp.exp(-jnp.abs(pre))
    step = jnp.maximum(pre, 0.0) + jnp.log1p(soft)
    step_ref[...] = step
    sgm_ref[...] = sigmoid(pre)
    log_decay = step * -jnp.exp(hp_ref[0:1, :])
    tri = (iota((STRETCH, STRETCH), 0) >= iota((STRETCH, STRETCH), 1)).astype(F32).astype(BF)
    cum = exact(dot_nn, tri, log_decay, 3, False)
    cum_ref[...] = cum
    last = cum[STRETCH - 1 : STRETCH]
    ef = jnp.exp(last - cum) * ends
    factor = jnp.exp(last) * alive[STRETCH - 1 : STRETCH]
    fac_row = exact(dot_nt, jnp.broadcast_to(factor, (8, LANES)), expand_ref[...], 3, True)
    fac_ref[0] = fac_row

    acts, slopes = act_and_slope(
        conv_taps(ext(slice(0, SHARED)), ks_ref[...], masks)
    )
    bc_ref[...] = acts.astype(BF)
    slopes_ref[...] = slopes.astype(BF)
    keys_t = jnp.transpose(acts[:, 0:STATE]).astype(BF)
    for pair, (at, width) in enumerate(pair_widths(channels)):
        lanes = slice(at, at + width)
        u = ext(slice(LEAD + at, LEAD + at + width))
        act, slope = act_and_slope(conv_taps(u, km_ref[:, lanes], masks))
        low = act.astype(BF)
        x_ref[:, lanes] = low
        slope_ref[:, lanes] = slope.astype(BF)
        xs = (low.astype(F32) * spread(step, pair, width)).astype(BF)
        xs_ref[:, lanes] = xs
        xe = (xs.astype(F32) * spread(ef, pair, width)).astype(BF)
        state = dot_nn(keys_t, xe)
        state_ref[0, :, lanes] = state
        carry[:, lanes] = carry[:, lanes] * fac_row[0:1, lanes] + state

    edge[...] = pre_ref[STRETCH - HALO :, :]

    @pl.when(k == pl.num_programs(0) - 1)
    def _():
        total_ref[...] = carry[...].astype(BF)


def doc_mask(seg_col, seg_row, shape, transposed):
    down, across = iota(shape, 0), iota(shape, 1)
    order = (across >= down) if transposed else (down >= across)
    return (seg_col == seg_row) & order


def second_kernel(
    bc_ref, x_ref, xs_ref, cum_ref, state_ref, fac_ref, enter_ref, heads_ref, tab_ref,
    y_ref, hist_ref,
    hold, hp_ref, skip_ref,
):
    k = pl.program_id(0)
    channels = x_ref.shape[1]

    @pl.when(k == 0)
    def _():
        hold[...] = enter_ref[...].astype(F32)
        load_heads(heads_ref, hp_ref)
        skip_ref[...] = skip_of(hp_ref, expand_of(channels))

    hist_ref[pl.ds(k, 1)] = hold[...].astype(BF)[None]
    col = columns_of(tab_ref)
    alive = col[:, 4:5]
    keys, queries = bc_ref[:, 0:STATE], bc_ref[:, STATE:SHARED]
    gram = dot_nt(queries, keys)
    valid = doc_mask(col[:, 0:1], tab_ref[0:1, :], (STRETCH, STRETCH), False)
    gram = jnp.where(valid, gram, 0.0)
    cum = cum_ref[...]
    cum_t = jnp.transpose(cum)
    rise = jnp.exp(cum) * alive
    for pair, (at, width) in enumerate(pair_widths(channels)):
        lanes = slice(at, at + width)
        xs = xs_ref[:, lanes]
        top = bottom = 0.0
        for which, mask in enumerate(head_masks(width)):
            h = 2 * pair + which
            here = masked(xs, mask)
            down, across = cum[:, h : h + 1], cum_t[h : h + 1, :]
            decay = jnp.exp(jnp.minimum(down[:HALF] - across[:, :HALF], 0.0))
            top = top + dot_nn((decay * gram[:HALF, :HALF]).astype(BF), here[:HALF])
            decay = jnp.exp(jnp.minimum(down[HALF:] - across, 0.0))
            bottom = bottom + dot_nn((decay * gram[HALF:]).astype(BF), here)
        within = jnp.concatenate([top, bottom], axis=0)
        old = hold[:, lanes]
        carried = dot_nn(queries, old.astype(BF)) * spread(rise, pair, width)
        hold[:, lanes] = old * fac_ref[0, 0:1, lanes] + state_ref[0, :, lanes]
        y = within + carried + skip_ref[0:1, lanes] * x_ref[:, lanes].astype(F32)
        y_ref[:, lanes] = y

    @pl.when(k == pl.num_programs(0) - 1)
    def _():
        hist_ref[pl.ds(k + 1, 1)] = hold[...].astype(BF)[None]


def gate_kernel(
    idx_ref, own_ref, near_ref, nearx_ref, far_ref, farx_ref, normed_ref, y_ref, cot_ref, gain_ref,
    gate_ref, gg_ref, out0_ref, out1_ref, out2_ref, out3_ref, stat_ref,
    held, sems,
):
    k = pl.program_id(0)
    channels = y_ref.shape[1]
    count, chunk = held.shape[0], held.shape[1]
    at_out = held.shape[2] // 2

    @pl.when(k == 0)
    def _():
        fetch_all(fetches(idx_ref, (own_ref, near_ref, nearx_ref, far_ref, farx_ref), held, sems))

    gates = dot_nn(normed_ref[:, :chunk], held[0, :, 0:channels])
    for a in range(1, count):
        gates = gates + dot_nn(normed_ref[:, a * chunk : (a + 1) * chunk], held[a, :, 0:channels])
    gate_ref[...] = gates.astype(BF)
    square = jnp.zeros((STRETCH, LANES), F32)
    for at, width in pair_widths(channels):
        lanes = slice(at, at + width)
        gate = gate_ref[:, lanes].astype(F32)
        gated = y_ref[:, lanes] * (gate * sigmoid(gate))
        gg_ref[:, lanes] = (gated * gain_ref[0:1, lanes]).astype(BF)
        square = square + padded(gated * gated)
    cross = jnp.zeros((STRETCH, LANES), F32)
    for q, out_ref in enumerate((out0_ref, out1_ref, out2_ref, out3_ref)):
        a = lax.rem(idx_ref[6] + q, count)
        out = dot_nt(gg_ref[...], held[a, :, at_out : at_out + channels])
        out_ref[...] = out.astype(BF)
        inner = out * cot_ref[:, pl.ds(pl.multiple_of(a * chunk, LANES), chunk)].astype(F32)
        for part in range(0, chunk, LANES):
            cross = cross + inner[:, part : part + LANES]
    ones = jnp.ones((8, LANES), BF)
    square = exact(dot_nt, ones, square, 3, False)
    cross = exact(dot_nt, ones, cross, 3, False)
    stat_ref[...] = jnp.where(iota((8, STRETCH), 0) == 0, square, cross)


def padded(v):
    if v.shape[1] == LANES:
        return v
    return jnp.concatenate([v, jnp.zeros((v.shape[0], LANES - v.shape[1]), v.dtype)], axis=1)


def gng_kernel(idx_ref, own_ref, near_ref, nearx_ref, far_ref, farx_ref, cot_ref, gng_ref, held, sems):
    count, chunk = held.shape[0], held.shape[1]
    channels = gng_ref.shape[1]

    @pl.when(pl.program_id(0) == 0)
    def _():
        out = pl.ds(own_ref.shape[1] // 2, held.shape[2])
        fetch_all(fetches(idx_ref, (own_ref, near_ref, nearx_ref, far_ref, farx_ref), held, sems, out))

    total = dot_nn(cot_ref[:, :chunk], held[0, :, 0:channels])
    for a in range(1, count):
        total = total + dot_nn(cot_ref[:, a * chunk : (a + 1) * chunk], held[a, :, 0:channels])
    gng_ref[...] = total.astype(BF)


def third_kernel(
    stat_ref, y_ref, gate_ref, gng_ref, gain_ref, bc_ref, cum_ref, fac_ref, tab_ref,
    gy_ref, gi_ref, inv_ref, flow_ref, gaingrad_ref,
    hold,
):
    i = pl.program_id(0)
    channels = y_ref.shape[1]

    @pl.when(i == 0)
    def _():
        hold[...] = jnp.zeros_like(hold)
        gaingrad_ref[...] = jnp.zeros_like(gaingrad_ref)

    pick = iota((8, LANES), 0)
    stat = stat_ref[...]
    square = exact(dot_tn, stat, (pick == 0).astype(F32).astype(BF), 3, True)
    cross = exact(dot_tn, stat, (pick == 1).astype(F32).astype(BF), 3, True)
    inv = lax.rsqrt(square / INNER + EPSILON)
    inv_ref[...] = inv
    back = inv * inv * inv * (cross / INNER)
    rise = jnp.exp(cum_ref[...]) * columns_of(tab_ref)[:, 4:5]
    queries_t = jnp.transpose(bc_ref[:, STATE:SHARED].astype(F32)).astype(BF)
    for pair, (at, width) in enumerate(pair_widths(channels)):
        lanes = slice(at, at + width)
        gate = gate_ref[:, lanes].astype(F32)
        act, slope = act_and_slope(gate)
        y = y_ref[:, lanes]
        gated = y * act
        gng = gng_ref[:, lanes].astype(F32)
        along = inv[:, :width]
        grad = along * (gain_ref[0:1, lanes] * gng) - gated * back[:, :width]
        gaingrad_ref[0:1, lanes] += jnp.sum(gng * gated * along, axis=0, keepdims=True)
        gy = (grad * act).astype(BF)
        gy_ref[:, lanes] = gy
        gi_ref[:, lanes] = (grad * y * slope).astype(BF)
        gyr = (gy.astype(F32) * spread(rise, pair, width)).astype(BF)
        hold[:, lanes] = dot_nn(queries_t, gyr) + fac_ref[0, 0:1, lanes] * hold[:, lanes]

    @pl.when(i == pl.num_programs(0) - 1)
    def _():
        flow_ref[...] = hold[...].astype(BF)


def conv_back(post, u, taps, masks, kgrad_ref, lanes):
    full = post.shape[0] + HALO
    pad = jnp.zeros((HALO, post.shape[1]), F32)
    total = jnp.concatenate([pad, post * taps[3:4]], axis=0)
    kgrad_ref[4:5, lanes] += jnp.sum(post, axis=0, keepdims=True)
    kgrad_ref[3:4, lanes] += jnp.sum(post * u[HALO:], axis=0, keepdims=True)
    for j in (1, 2, 3):
        here = post * masks[j - 1]
        kgrad_ref[3 - j : 4 - j, lanes] += jnp.sum(
            here * pltpu.roll(u, j, 0)[HALO:], axis=0, keepdims=True
        )
        wide = jnp.concatenate([pad, here * taps[3 - j : 4 - j]], axis=0)
        total = total + pltpu.roll(wide, full - j, 0)
    return total


def fourth_kernel(
    idx_ref, own_ref, near_ref, nearx_ref, far_ref, farx_ref,
    gy_ref, x_ref, xs_ref, slope_ref, y_ref, bc_ref, slopes_ref, step_ref, cum_ref, sgm_ref, pre_ref, prev_ref,
    phalo_ref, ht_ref, hn_ref, fac_ref, enter_ref, km_ref, ks_ref, heads_ref, tab_ref, gategrad_ref,
    g_ref, ghalo_ref, small_ref, back_ref,
    held, sems, hold, edge, hp_ref, expand_ref, skip_ref, skipgrad_ref, kmgrad_ref, ksgrad_ref, head_ref,
):
    i = pl.program_id(0)
    k = pl.num_programs(0) - 1 - i
    channels = x_ref.shape[1]
    copies = fetches(idx_ref, (own_ref, near_ref, nearx_ref, far_ref, farx_ref), held, sems)

    @pl.when(i == 0)
    def _():
        for copy in copies:
            copy.start()
        hold[...] = enter_ref[...].astype(F32)
        edge[...] = jnp.zeros_like(edge)
        load_heads(heads_ref, hp_ref)
        expand_ref[...] = expand_of(channels)
        skip_ref[...] = skip_of(hp_ref, expand_ref[...])
        kmgrad_ref[...] = jnp.zeros_like(kmgrad_ref)
        ksgrad_ref[...] = jnp.zeros_like(ksgrad_ref)
        head_ref[...] = jnp.zeros_like(head_ref)
        skipgrad_ref[...] = jnp.zeros_like(skipgrad_ref)

    def ext(lanes):
        before = jnp.where(k == 0, phalo_ref[:, lanes].astype(F32), prev_ref[:, lanes].astype(F32))
        return jnp.concatenate([before, pre_ref[:, lanes].astype(F32)], axis=0)

    def put(lanes, total):
        g_ref[0 : STRETCH - HALO, lanes] = total[HALO:STRETCH].astype(BF)
        g_ref[STRETCH - HALO :, lanes] = (total[STRETCH:] + edge[:, lanes]).astype(BF)
        edge[:, lanes] = total[:HALO]

    col = columns_of(tab_ref)
    masks = [col[:, j : j + 1] for j in (1, 2, 3)]
    alive, ends = col[:, 4:5], col[:, 5:6]
    keys, queries = bc_ref[:, 0:STATE], bc_ref[:, STATE:SHARED]
    queries_t = jnp.transpose(queries.astype(F32)).astype(BF)
    valid = doc_mask(col[:, 0:1], tab_ref[0:1, :], (STRETCH, STRETCH), True)
    gram = jnp.where(valid, dot_nt(keys, queries), 0.0)
    step, cum = step_ref[...], cum_ref[...]
    cum_t = jnp.transpose(cum)
    rise = jnp.exp(cum) * alive
    ef = jnp.exp(cum[STRETCH - 1 : STRETCH] - cum) * ends
    gram_top = jnp.zeros((HALF, STRETCH), F32)
    gram_bottom = jnp.zeros((HALF, HALF), F32)
    grad_keys = jnp.zeros((STRETCH, STATE), F32)
    grad_queries = jnp.zeros((STRETCH, STATE), F32)
    rowterm = jnp.zeros((STRETCH, LANES), F32)
    colterm = jnp.zeros((STRETCH, LANES), F32)
    endterm = jnp.zeros((8, LANES), F32)
    for pair, (at, width) in enumerate(pair_widths(channels)):
        lanes = slice(at, at + width)
        expand = expand_ref[lanes, :]
        gy, xs = gy_ref[:, lanes], xs_ref[:, lanes]
        gyf, xf = gy.astype(F32), x_ref[:, lanes].astype(F32)
        skip = skip_ref[0:1, lanes]
        top = bottom = 0.0
        for which, mask in enumerate(head_masks(width)):
            h = 2 * pair + which
            here = masked(gy, mask)
            down, across = cum[:, h : h + 1], cum_t[h : h + 1, :]
            decay = jnp.exp(jnp.minimum(across - down[:HALF], 0.0))
            top = top + dot_nn((decay * gram[:HALF]).astype(BF), here)
            gram_top = gram_top + dot_nt(xs[:HALF], here) * decay
            decay = jnp.exp(jnp.minimum(across[:, HALF:] - down[HALF:], 0.0))
            bottom = bottom + dot_nn((decay * gram[HALF:, HALF:]).astype(BF), here[HALF:])
            gram_bottom = gram_bottom + dot_nt(xs[HALF:], here[HALF:]) * decay
        grad_xs = jnp.concatenate([top, bottom], axis=0)
        after = hold[:, lanes]
        low = after.astype(BF)
        efs = spread(ef, pair, width)
        grad_xs = grad_xs + dot_nn(keys, low) * efs
        gyr = (gyf * spread(rise, pair, width)).astype(BF)
        xe = (xs.astype(F32) * efs).astype(BF)
        grad_queries = grad_queries + dot_nt(gyr, ht_ref[0, :, lanes])
        grad_keys = grad_keys + dot_nt(xe, low)
        ended = jnp.sum(after * hn_ref[0, :, lanes].astype(F32), axis=0, keepdims=True)
        endterm = endterm + exact(dot_nn, jnp.broadcast_to(ended, (8, width)), expand, 3, True)
        hold[:, lanes] = dot_nn(queries_t, gyr) + fac_ref[0, 0:1, lanes] * after
        rowterm = rowterm + exact(dot_nn, gyf * (y_ref[:, lanes] - skip * xf), expand, 2, True)
        colterm = colterm + exact(dot_nn, xf * grad_xs, expand, 2, True)
        skipgrad_ref[0:1, lanes] += jnp.sum(gyf * xf, axis=0, keepdims=True)
        grad_x = grad_xs * spread(step, pair, width) + skip * gyf
        post = grad_x * slope_ref[:, lanes].astype(F32)
        at_g = slice(LEAD + at, LEAD + at + width)
        put(at_g, conv_back(post, ext(at_g), km_ref[:, lanes], masks, kmgrad_ref, lanes))

    gram_top = jnp.where(valid[:HALF], gram_top, 0.0).astype(BF)
    gram_bottom = jnp.where(valid[HALF:, HALF:], gram_bottom, 0.0).astype(BF)
    grad_keys = grad_keys + jnp.concatenate(
        [dot_nn(gram_top, queries), dot_nn(gram_bottom, queries[HALF:])], axis=0
    )
    lower = jnp.concatenate([jnp.zeros((HALF, HALF), BF), gram_bottom], axis=1)
    gram_all = jnp.concatenate([gram_top, lower], axis=0)
    grad_queries = grad_queries + dot_tn(gram_all, keys)
    post = jnp.concatenate([grad_keys, grad_queries], axis=1) * slopes_ref[...].astype(F32)
    shared = slice(0, SHARED)
    put(shared, conv_back(post, ext(shared), ks_ref[...], masks, ksgrad_ref, shared))

    rate = -jnp.exp(hp_ref[0:1, :])
    grad_cum = rowterm - step * colterm
    at_end = iota((STRETCH, LANES), 0) == STRETCH - 1
    grad_cum = grad_cum + jnp.where(at_end, endterm[0:1], 0.0)
    upper = (iota((STRETCH, STRETCH), 1) >= iota((STRETCH, STRETCH), 0)).astype(F32).astype(BF)
    grad_log = exact(dot_nn, upper, grad_cum, 3, False)
    grad_pre = (colterm + grad_log * rate) * sgm_ref[...]
    g_ref[:, SHARED:LEAD] = grad_pre.astype(BF)
    head_ref[0:1, :] += jnp.sum(grad_log * step, axis=0, keepdims=True) * rate
    head_ref[1:2, :] += jnp.sum(grad_pre, axis=0, keepdims=True)

    @pl.when(k == 0)
    def _():
        ghalo_ref[:, 0:SHARED] = edge[:, 0:SHARED].astype(BF)
        ghalo_ref[:, LEAD:] = edge[:, LEAD:].astype(BF)
        ghalo_ref[:, SHARED:LEAD] = jnp.zeros((HALO, LANES), BF)
        wide = jnp.broadcast_to(skipgrad_ref[0:1, :], (8, channels))
        small_ref[...] = jnp.zeros_like(small_ref)
        small_ref[1:6, 0:channels] = kmgrad_ref[0:5, :]
        small_ref[6:11, 0:SHARED] = ksgrad_ref[0:5, :]
        small_ref[11:12, 0:channels] = gategrad_ref[0:1, :]
        small_ref[12:14, 0:LANES] = head_ref[0:2, :]
        small_ref[14:15, 0:LANES] = exact(dot_nn, wide, expand_ref[...], 3, True)[0:1]
        for copy in copies:
            copy.wait()
        chunk = held.shape[1]
        for a in range(held.shape[0]):
            back_ref[:, a * chunk : (a + 1) * chunk] = dot_nt(ghalo_ref[...], held[a])


def normed_kernel(
    idx_ref, own0_ref, near0_ref, nearx0_ref, far0_ref, farx0_ref, own_ref, near_ref, nearx_ref, far_ref, farx_ref,
    gi_ref, g_ref, normed_ref, back_ref, small_ref,
    out0_ref, out1_ref, out2_ref, out3_ref, cross_ref, sums_ref,
    held0, held, sems0, sems, acc,
):
    i = pl.program_id(0)
    last = i == pl.num_programs(0) - 1
    rows = gi_ref.shape[0]
    count, chunk, channels = held0.shape

    @pl.when(i == 0)
    def _():
        pieces = (own0_ref, near0_ref, nearx0_ref, far0_ref, farx0_ref)
        columns = pl.ds(0, channels)
        copies = fetches(idx_ref, pieces, held0, sems0, columns)
        copies += fetches(idx_ref, (own_ref, near_ref, nearx_ref, far_ref, farx_ref), held, sems)
        fetch_all(copies)
        sums_ref[...] = small_ref[...]

    cross = jnp.zeros((rows, LANES), F32)
    for q, out_ref in enumerate((out0_ref, out1_ref, out2_ref, out3_ref)):
        a = lax.rem(idx_ref[6] + q, count)
        lanes = pl.ds(pl.multiple_of(a * chunk, LANES), chunk)
        width = gi_ref.shape[1]
        acc[...] = dot_nt(gi_ref[...], held0[a, :, 0:width]) + dot_nt(g_ref[...], held[a])

        @pl.when(last)
        def _():
            acc[rows - HALO :, :] += back_ref[:, lanes]

        total = acc[...]
        out_ref[...] = total.astype(BF)
        inner = total * normed_ref[:, lanes].astype(F32)
        sums_ref[0:1, lanes] += jnp.sum(inner, axis=0, keepdims=True)
        for part in range(0, chunk, LANES):
            cross = cross + inner[:, part : part + LANES]
    cross_ref[...] = exact(dot_nt, jnp.ones((8, LANES), BF), cross, 3, False)


def put_chunk(idx_ref, keep_ref, send_ref, lanes, value):
    j = pl.program_id(0)
    half = keep_ref.shape[1]
    top, bottom = value[:half].astype(BF), value[half:].astype(BF)

    @pl.when(j == idx_ref[1])
    def _():
        keep_ref[0, :, lanes] = top
        keep_ref[1, :, lanes] = bottom

    @pl.when(j == idx_ref[2])
    def _():
        send_ref[0, :, lanes] = top
        send_ref[1, :, lanes] = bottom

    for source, target in ((0, 3), (3, 2)):
        for c, (mine, other) in enumerate(((top, bottom), (bottom, top))):

            @pl.when((j == idx_ref[source]) & (idx_ref[4] == c))
            def _():
                keep_ref[target, :, lanes] = mine
                send_ref[target, :, lanes] = other


def weight_kernel(idx_ref, normed_ref, nhalo_ref, g_ref, ghalo_ref, keep_ref, send_ref):
    value = dot_tn(normed_ref[...], g_ref[...]) + dot_tn(nhalo_ref[...], ghalo_ref[...])
    put_chunk(idx_ref, keep_ref, send_ref, slice(None), value)


def gate_out_kernel(idx_ref, normed_ref, gi_ref, cot_ref, inv_ref, gg_ref, keep_ref, send_ref):
    channels = gi_ref.shape[1]
    wide = keep_ref.shape[2] // 2
    put_chunk(idx_ref, keep_ref, send_ref, slice(0, channels), dot_tn(normed_ref[...], gi_ref[...]))
    scaled = [
        (cot_ref[:, at : at + LANES].astype(F32) * inv_ref[...]).astype(BF)
        for at in range(0, cot_ref.shape[1], LANES)
    ]
    value = dot_tn(jnp.concatenate(scaled, axis=1), gg_ref[...])
    put_chunk(idx_ref, keep_ref, send_ref, slice(wide, wide + channels), value)


def output_kernel(own_ref, inv_ref, part_ref, right_ref, left_ref, out_ref):
    inv = inv_ref[...]
    for at in range(0, out_ref.shape[1], LANES):
        lanes = slice(at, at + LANES)
        total = part_ref[:, lanes].astype(F32) + right_ref[:, lanes].astype(F32)
        total = (total + left_ref[:, lanes].astype(F32)) * inv
        out_ref[:, lanes] = (own_ref[:, lanes].astype(F32) + total).astype(BF)


def tokens_kernel(
    width, own_ref, cot_ref, inv_ref, cross_ref, gain_ref, part_ref, right_ref, left_ref, out_ref
):
    inv = inv_ref[...]
    pick = (iota((8, LANES), 0) == 0).astype(F32).astype(BF)
    cross = exact(dot_tn, cross_ref[...], pick, 3, True)
    back = inv * inv * (cross / width)
    for at in range(0, out_ref.shape[1], LANES):
        lanes = slice(at, at + LANES)
        total = part_ref[:, lanes].astype(F32) + right_ref[:, lanes].astype(F32)
        total = total + left_ref[:, lanes].astype(F32)
        out_ref[:, lanes] = (
            inv * gain_ref[0:1, lanes] * total
            - own_ref[:, lanes].astype(F32) * back
            + cot_ref[:, lanes].astype(F32)
        )


def whole(array):
    rank = len(array.shape)
    return pl.BlockSpec(array.shape, lambda *_: (0,) * rank)


def call(kernel, grid, ins, in_specs, outs, out_specs, scratch=(), flops=0, prefetch=0):
    moved = sum(a.size * a.dtype.itemsize for a in (*ins, *outs))
    return pl.pallas_call(
        kernel,
        out_shape=outs,
        grid_spec=pltpu.PrefetchScalarGridSpec(
            num_scalar_prefetch=prefetch,
            grid=grid,
            in_specs=in_specs,
            out_specs=out_specs,
            scratch_shapes=list(scratch),
        ),
        compiler_params=pltpu.CompilerParams(
            dimension_semantics=("arbitrary",) * len(grid), vmem_limit_bytes=VMEM_LIMIT
        ),
        cost_estimate=pl.CostEstimate(
            flops=int(flops), bytes_accessed=int(moved), transcendentals=0
        ),
    )(*ins)


def shape(dims, kind):
    return jax.ShapeDtypeStruct(dims, kind)


def add(*terms):
    return sum(term.astype(F32) for term in terms).astype(BF)


def per_device(
    tokens, segments, norm_gain, proj_main, proj_shared, proj_step, conv_main, conv_shared,
    head_params, gate_gain, output_projection, cotangent,
):
    _, length, width = tokens.shape
    nf, nc, nt = lax.axis_size("fsdp"), lax.axis_size("ctx"), lax.axis_size("tp")
    assert nf == 4 and nc == 2
    f, c, t = lax.axis_index("fsdp"), lax.axis_index("ctx"), lax.axis_index("tp")
    heads = head_params.shape[1]
    channels = heads * HEADDIM
    lead = LEAD + channels
    wide = -(-channels // LANES) * LANES
    nb = length // STRETCH
    chunk = width // nf
    half = chunk // 2
    share = width // nt
    line = nt == nf
    rot = t if line else jnp.zeros_like(t)
    both = ("fsdp", "ctx")
    spots = [(i, j) for i in range(nf) for j in range(nc)]
    role = [(i * nc + j, (i ^ (1 + j)) * nc + j) for i, j in spots]
    turn = [(i * nc + j, (i ^ (2 - j)) * nc + j) for i, j in spots]
    across_chip = [(i * nc + j, (i ^ 3) * nc + j) for i, j in spots]
    swap = [(0, 1), (1, 0)]
    idx = jnp.stack([f, f ^ (1 + c), f ^ (2 - c), f ^ 3, c, rot, rot, rot]).astype(jnp.int32)

    def tp_sum(v):
        if not line:
            return lax.psum(v, "tp")
        first, second, third = (
            lax.ppermute(v, "tp", [(i, i ^ m) for i in range(nt)]) for m in (1, 2, 3)
        )
        return (v + first) + (second + third)

    def one(v, at):
        return lax.dynamic_slice_in_dim(v, at, 1, 0)

    def gather_rows(shard, direct):
        columns = shard.shape[1]
        pieces = shard.reshape(2, half, columns)
        near = lax.ppermute(pieces, both, role)
        if direct:
            far = lax.ppermute(one(pieces, c), both, across_chip)
        else:
            far = lax.ppermute(one(near, c), both, turn)
        near_other = lax.ppermute(near, "ctx", swap)
        far_other = lax.ppermute(far, "ctx", swap)
        return (
            shard, near.reshape(chunk, columns), near_other.reshape(chunk, columns), far[0], far_other[0]
        )

    def scatter_rows(keep, send):
        got = lax.ppermute(send, "ctx", swap)
        far = lax.ppermute(add(keep[2:3], got[2:3]), both, turn)
        which = iota((2, 1, 1), 0) == c
        near = add(keep[0:2], got[0:2], jnp.where(which, far.astype(F32), 0.0))
        near = lax.ppermute(near, both, role)
        other = lax.ppermute(one(near, 1 - c), "ctx", swap)
        own = keep[3].astype(F32) + got[3].astype(F32)
        return own + one(near, c)[0].astype(F32) + other[0].astype(F32)

    def scatter_tp(pieces):
        if not line:
            full = jnp.concatenate(pieces, axis=1)
            total = lax.psum_scatter(full, "tp", scatter_dimension=1, tiled=True)
            return total, jnp.zeros_like(total), jnp.zeros_like(total)
        right = left = None
        for r in range(1, nt):
            a, b = pieces[nt - r], pieces[r]
            if right is not None:
                a, b = add(a, right), add(b, left)
            right = lax.ppermute(a, "tp", [(i, i + 1) for i in range(r)])
            left = lax.ppermute(b, "tp", [(i, i - 1) for i in range(nt - r, nt)])
        return pieces[0], right, left

    any_spec = pl.BlockSpec(memory_space=pl.ANY)
    sems = pltpu.SemaphoreType.DMA((5,))

    def block(columns, back=False):
        if back:
            return pl.BlockSpec((STRETCH, columns), lambda i, *_: (nb - 1 - i, 0))
        return pl.BlockSpec((STRETCH, columns), lambda i, *_: (i, 0))

    def across(back=False):
        if back:
            return pl.BlockSpec((8, STRETCH), lambda i, *_: (0, nb - 1 - i))
        return pl.BlockSpec((8, STRETCH), lambda i, *_: (0, i))

    def stacked(rows, columns, back=False, off=0):
        if back:
            return pl.BlockSpec((1, rows, columns), lambda i, *_: (nb - 1 - i + off, 0, 0))
        return pl.BlockSpec((1, rows, columns), lambda i, *_: (i + off, 0, 0))

    def main_part(which):
        return pl.BlockSpec((1, chunk, channels), lambda i: (which, 0, 0))

    tokens2, cot2 = tokens[0], cotangent[0]
    ins = (proj_shared, proj_step, proj_main)
    outs = (shape((chunk, lead), BF),)
    shard_in = call(
        pack_in_kernel, (1,), ins, [whole(proj_shared), whole(proj_step), main_part(1)],
        outs, [whole(outs[0])],
    )[0]
    w_in = gather_rows(shard_in, False)
    halo = lax.ppermute(tokens2[length - HALO :], "ctx", [(0, 1)])
    ins = (proj_main, output_projection)
    outs = (shape((chunk, 2 * wide), BF),)
    shard_go = call(
        pack_go_kernel, (1,), ins, [main_part(0), whole(output_projection)],
        outs, [whole(outs[0])],
    )[0]
    w_go = gather_rows(shard_go, True)

    gate_row = gate_gain[None]
    gain_row = norm_gain[None]

    ins = (idx, tokens2, halo, cot2, gain_row, segments)
    outs = (
        shape((length, width), BF), shape((HALO, width), BF), shape((length, chunk), BF),
        shape((length, chunk), BF), shape((length, LANES), F32), shape((8, length), F32),
    )
    normed, nhalo, own_tokens, own_cot, inv_rms, tab = call(
        functools.partial(prep_kernel, chunk), (nb,), ins,
        [block(width), whole(halo), block(width), whole(gain_row), whole(segments)],
        outs, [block(width), whole(outs[1]), block(chunk), block(chunk), block(LANES), across()], prefetch=1,
    )
    if not line:
        own_tokens = lax.dynamic_slice_in_dim(tokens2, t * share, share, 1)
        own_cot = lax.dynamic_slice_in_dim(cot2, t * share, share, 1)

    outs = (
        shape((length, lead), BF), shape((HALO, lead), BF),
        shape((length, channels), BF), shape((length, channels), BF), shape((length, channels), BF),
        shape((length, SHARED), BF), shape((length, SHARED), BF),
        shape((length, LANES), F32), shape((length, LANES), F32), shape((length, LANES), F32),
        shape((nb, STATE, channels), F32), shape((nb, 8, channels), F32), shape((STATE, channels), BF),
    )
    ins = (idx, *w_in, normed, nhalo, conv_main, conv_shared, head_params, tab)
    wide_row = pltpu.VMEM((8, LANES), F32)
    held_in = pltpu.VMEM((nf, chunk, lead), BF)
    pre, phalo, x, xs, slope, bc, slopes, step, cum, sgm, states, fac, total = call(
        first_kernel, (nb,), ins,
        [any_spec] * 5
        + [block(width), whole(nhalo), whole(conv_main), whole(conv_shared), whole(head_params), across()],
        outs,
        [block(lead), whole(outs[1])] + [block(channels)] * 3 + [block(SHARED)] * 2 + [block(LANES)] * 3
        + [stacked(STATE, channels), stacked(8, channels), whole(outs[-1])],
        scratch=[
            held_in, sems, pltpu.VMEM((HALO, lead), BF), pltpu.VMEM((STATE, channels), F32), wide_row,
            pltpu.VMEM((channels, LANES), BF),
        ],
        prefetch=1, flops=2 * length * (STATE * channels + width * lead),
    )
    enter = lax.ppermute(total, "ctx", [(0, 1)])

    outs = (shape((length, channels), F32), shape((nb + 1, STATE, channels), BF))
    ins = (bc, x, xs, cum, states, fac, enter, head_params, tab)
    y, hist = call(
        second_kernel, (nb,), ins,
        [
            block(SHARED), block(channels), block(channels), block(LANES), stacked(STATE, channels),
            stacked(8, channels), whole(enter), whole(head_params), across(),
        ],
        outs, [block(channels), whole(outs[1])],
        scratch=[pltpu.VMEM((STATE, channels), F32), wide_row, pltpu.VMEM((8, channels), F32)],
        flops=8 * length * STRETCH * channels,
    )

    outs = (shape((length, channels), BF),) * 2 + (shape((length, chunk), BF),) * nf + (shape((8, length), F32),)
    ins = (idx, *w_go, normed, y, cot2, gate_row)
    gate, gg, *out_parts, stat = call(
        gate_kernel, (nb,), ins,
        [any_spec] * 5 + [block(width), block(channels), block(width), whole(gate_row)],
        outs, [block(channels)] * 2 + [block(chunk)] * nf + [across()],
        scratch=[pltpu.VMEM((nf, chunk, 2 * wide), BF), sems],
        prefetch=1, flops=4 * length * width * channels,
    )
    out_terms = scatter_tp(out_parts)
    stat = tp_sum(stat)
    outs = (shape((length, channels), BF),)
    gng = call(
        gng_kernel, (nb,), (idx, *w_go, cot2), [any_spec] * 5 + [block(width)], outs, [block(channels)],
        scratch=[pltpu.VMEM((nf, chunk, wide), BF), sems], prefetch=1, flops=2 * length * width * channels,
    )[0]

    outs = (
        shape((length, channels), BF), shape((length, channels), BF), shape((length, LANES), F32),
        shape((STATE, channels), BF), shape((8, channels), F32),
    )
    ins = (stat, y, gate, gng, gate_row, bc, cum, fac, tab)
    gy, gi, inv_gate, flow, gate_grad = call(
        third_kernel, (nb,), ins,
        [
            across(True), block(channels, True), block(channels, True), block(channels, True), whole(gate_row),
            block(SHARED, True), block(LANES, True), stacked(8, channels, True), across(True),
        ],
        outs, [block(channels, True), block(channels, True), block(LANES, True), whole(outs[3]), whole(outs[4])],
        scratch=[pltpu.VMEM((STATE, channels), F32)],
        flops=2 * length * STATE * channels,
    )
    leaving = lax.ppermute(flow, "ctx", [(1, 0)])

    outs = (shape((4, half, 2 * wide), BF),) * 2
    ins = (idx, normed, gi, cot2, inv_gate, gg)
    grad_go = call(
        gate_out_kernel, (nf,), ins,
        [
            pl.BlockSpec((length, chunk), lambda i, *_: (0, i)), whole(gi),
            pl.BlockSpec((length, chunk), lambda i, *_: (0, i)), whole(inv_gate), whole(gg),
        ],
        outs, [whole(outs[0])] * 2, prefetch=1,
        flops=4 * length * width * channels,
    )
    grad_go = scatter_rows(*grad_go)

    outs = (
        shape((length, lead), BF), shape((HALO, lead), BF), shape((16, width), F32), shape((HALO, width), F32),
    )
    ins = (
        idx, *w_in, gy, x, xs, slope, y, bc, slopes, step, cum, sgm, pre, pre, phalo, hist, hist, fac, leaving,
        conv_main, conv_shared, head_params, tab, gate_grad,
    )
    per_block = STRETCH // HALO
    g_in, ghalo, small, back = call(
        fourth_kernel, (nb,), ins,
        [any_spec] * 5
        + [block(channels, True)] * 5 + [block(SHARED, True)] * 2 + [block(LANES, True)] * 3
        + [
            block(lead, True),
            pl.BlockSpec((HALO, lead), lambda i, *_: (jnp.maximum((nb - 1 - i) * per_block - 1, 0), 0)),
            whole(phalo), stacked(STATE, channels, True), stacked(STATE, channels, True, 1),
            stacked(8, channels, True), whole(leaving), whole(conv_main), whole(conv_shared),
            whole(head_params), across(True), whole(gate_grad),
        ],
        outs, [block(lead, True)] + [whole(o) for o in outs[1:]],
        scratch=[
            held_in, sems, pltpu.VMEM((STATE, channels), F32), pltpu.VMEM((HALO, lead), F32), wide_row,
            pltpu.VMEM((channels, LANES), BF), pltpu.VMEM((8, channels), F32), pltpu.VMEM((8, channels), F32),
            pltpu.VMEM((8, channels), F32), pltpu.VMEM((8, SHARED), F32), wide_row,
        ],
        prefetch=1, flops=16 * length * STRETCH * channels,
    )
    back = lax.ppermute(back, "ctx", [(1, 0)])

    outs = (shape((length, chunk), BF),) * nf + (shape((8, length), F32), shape((16, width), F32))
    ins = (idx, *w_go, *w_in, gi, g_in, normed, back, small)
    *normed_parts, cross, sums = call(
        normed_kernel, (nb,), ins,
        [any_spec] * 10 + [block(channels), block(lead), block(width), whole(back), whole(small)],
        outs, [block(chunk)] * nf + [across(), whole(outs[-1])],
        scratch=[
            pltpu.VMEM((nf, chunk, wide), BF), held_in, sems, sems, pltpu.VMEM((STRETCH, chunk), F32),
        ],
        prefetch=1, flops=2 * length * width * (lead + channels),
    )
    normed_terms = scatter_tp(normed_parts)
    cross = tp_sum(cross)

    outs = (shape((4, half, lead), BF),) * 2
    grad_w = call(
        weight_kernel, (nf,), (idx, normed, nhalo, g_in, ghalo),
        [
            pl.BlockSpec((length, chunk), lambda i, *_: (0, i)), pl.BlockSpec((HALO, chunk), lambda i, *_: (0, i)),
            whole(g_in), whole(ghalo),
        ],
        outs, [whole(outs[0])] * 2, prefetch=1,
        flops=2 * length * width * lead,
    )
    grad_w = scatter_rows(*grad_w)

    sums = sums + lax.ppermute(sums, "ctx", swap)
    for m in (1, 2):
        sums = sums + lax.ppermute(sums, "fsdp", [(i, i ^ m) for i in range(nf)])
    over_tp = tp_sum(sums)
    own_gain = lax.dynamic_slice_in_dim(norm_gain, t * share, share, 0)
    grad_gain = lax.dynamic_slice_in_dim(over_tp[0], t * share, share, 0) / own_gain

    outs = (shape((length, share), BF),)
    if line:
        spec = pl.BlockSpec((length // 2, share), lambda i: (i, 0))
        inv_spec = pl.BlockSpec((length // 2, LANES), lambda i: (i, 0))
        output = call(
            output_kernel, (2,), (own_tokens, inv_gate, *out_terms), [spec, inv_spec, spec, spec, spec],
            outs, [spec],
        )[0]
        outs = (shape((length, share), F32),)
        gain2 = own_gain[None]
        grad_tokens = call(
            functools.partial(tokens_kernel, width), (2,),
            (own_tokens, own_cot, inv_rms, cross, gain2, *normed_terms),
            [
                spec, spec, inv_spec, pl.BlockSpec((8, length // 2), lambda i: (0, i)), whole(gain2), spec, spec,
                spec,
            ],
            outs, [spec],
        )[0]
    else:
        output = (own_tokens.astype(F32) + inv_gate[:, :1] * out_terms[0].astype(F32)).astype(BF)
        inv = inv_rms[:, :1]
        grad_tokens = (
            inv * own_gain * normed_terms[0].astype(F32)
            - own_tokens.astype(F32) * (inv * inv * (cross[0][:, None] / width))
            + own_cot.astype(F32)
        )
    return (
        output[None],
        grad_tokens[None],
        grad_gain,
        jnp.stack([grad_go[:, :channels], grad_w[:, LEAD:]]),
        tp_sum(grad_w[:, :SHARED]),
        grad_w[:, SHARED : SHARED + heads],
        sums[1:6, :channels],
        over_tp[6:11, :SHARED],
        sums[12:15, :heads],
        sums[11, :channels],
        jnp.transpose(grad_go[:, wide : wide + channels]),
    )


def solution(mesh):
    return jax.shard_map(
        per_device,
        mesh=mesh,
        in_specs=(
            P("fsdp", "ctx", None),
            P("fsdp", None),
            P(),
            P(None, "fsdp", "tp"),
            P("fsdp", None),
            P("fsdp", "tp"),
            P(None, "tp"),
            P(),
            P(None, "tp"),
            P("tp"),
            P("tp", "fsdp"),
            P("fsdp", "ctx", None),
        ),
        out_specs=(
            P("fsdp", "ctx", "tp"),
            P("fsdp", "ctx", "tp"),
            P("tp"),
            P(None, ("fsdp", "ctx"), "tp"),
            P(("fsdp", "ctx"), None),
            P(("fsdp", "ctx"), "tp"),
            P(None, "tp"),
            P(),
            P(None, "tp"),
            P("tp"),
            P("tp", ("fsdp", "ctx")),
        ),
        check_vma=False,
    )
```

```python
import functools

import jax
import jax.numpy as jnp
from jax import lax
from jax.experimental import pallas as pl
from jax.experimental.pallas import tpu as pltpu
from jax.sharding import PartitionSpec as P


HEADDIM = 64
STATE = 128
STRETCH = 256
HALF = STRETCH // 2
INNER = 3072
EPSILON = 1e-05
HALO = 16
LANES = 128
SHARED = 2 * STATE
LEAD = SHARED + LANES
BF = jnp.bfloat16
F32 = jnp.float32
LIMITS = {"k_final": 60, "k_tokens": 60, "k_sums": 60}


def dot_nn(a, b):
    return lax.dot_general(a, b, (((1,), (0,)), ((), ())), preferred_element_type=F32)


def dot_nt(a, b):
    return lax.dot_general(a, b, (((1,), (1,)), ((), ())), preferred_element_type=F32)


def dot_tn(a, b):
    return lax.dot_general(a, b, (((0,), (0,)), ((), ())), preferred_element_type=F32)


def split(v, n):
    terms = []
    for _ in range(n):
        high = v.astype(BF)
        terms.append(high)
        v = v - high.astype(F32)
    return terms


def exact(dot, a, b, n, left):
    total = None
    for term in split(a if left else b, n):
        part = dot(term, b) if left else dot(a, term)
        total = part if total is None else total + part
    return total


def iota(shape, axis):
    return lax.broadcasted_iota(jnp.int32, shape, axis)


def pair_widths(channels):
    return [(at, min(LANES, channels - at)) for at in range(0, channels, LANES)]


def spread(v, pair, width):
    first = v[:, 2 * pair : 2 * pair + 1]
    if width == HEADDIM:
        return jnp.broadcast_to(first, (v.shape[0], HEADDIM))
    second = v[:, 2 * pair + 1 : 2 * pair + 2]
    lane = iota((v.shape[0], LANES), 1)
    return jnp.where(lane < HEADDIM, first, second)


def head_masks(width):
    if width == HEADDIM:
        return [None]
    lane = iota((1, LANES), 1)
    return [(lane < HEADDIM).astype(F32).astype(BF), (lane >= HEADDIM).astype(F32).astype(BF)]


def masked(v, mask):
    return v if mask is None else v * mask


def sigmoid(v):
    return 1.0 / (1.0 + jnp.exp(-v))


def pack_in_kernel(shared_ref, step_ref, main_ref, out_ref):
    out_ref[:, 0:SHARED] = shared_ref[...]
    heads, rows = step_ref.shape
    tall = jnp.concatenate([step_ref[...].astype(F32), jnp.zeros((LANES - heads, rows), F32)], axis=0)
    out_ref[:, SHARED:LEAD] = jnp.transpose(tall).astype(BF)
    out_ref[:, LEAD:] = main_ref[0]


def pack_go_kernel(main_ref, out_proj_ref, out_ref):
    channels = main_ref.shape[2]
    wide = out_ref.shape[1] // 2
    if wide != channels:
        out_ref[...] = jnp.zeros_like(out_ref)
    out_ref[:, 0:channels] = main_ref[0]
    out_ref[:, wide : wide + channels] = jnp.transpose(out_proj_ref[...].astype(F32)).astype(BF)


def fetches(idx_ref, pieces, held, sems, columns=None):
    own, near, near_other, far, far_other = pieces
    half = held.shape[1] // 2
    c = idx_ref[4]
    top, bottom = (pl.ds(pl.multiple_of(h * half, HALO), half) for h in (c, 1 - c))
    targets = (
        (own, held.at[idx_ref[0]]),
        (near, held.at[idx_ref[1]]),
        (near_other, held.at[idx_ref[2]]),
        (far, held.at[idx_ref[3], top]),
        (far_other, held.at[idx_ref[3], bottom]),
    )
    return [
        pltpu.make_async_copy(
            source if columns is None else source.at[:, columns], target, sems.at[i]
        )
        for i, (source, target) in enumerate(targets)
    ]


def fetch_all(copies):
    for copy in copies:
        copy.start()
    for copy in copies:
        copy.wait()


def prep_kernel(
    chunk, idx_ref, tok_ref, halo_ref, cot_ref, gain_ref, seg_ref, normed_ref, nhalo_ref, own_ref, owncot_ref,
    inv_ref, tab_ref,
):
    k = pl.program_id(0)

    def scale_of(x):
        return lax.rsqrt(jnp.mean(x * x, axis=-1, keepdims=True) + EPSILON)

    x = tok_ref[...].astype(F32)
    inv = scale_of(x)
    inv_ref[...] = jnp.broadcast_to(inv, inv_ref.shape)
    normed_ref[...] = (x * inv * gain_ref[0:1, :]).astype(BF)
    mine = pl.ds(pl.multiple_of(idx_ref[5] * chunk, LANES), chunk)
    own_ref[...] = tok_ref[:, mine]
    owncot_ref[...] = cot_ref[:, mine]

    @pl.when(k == 0)
    def _():
        x = halo_ref[...].astype(F32)
        nhalo_ref[...] = (x * scale_of(x) * gain_ref[0:1, :]).astype(BF)

    start = (idx_ref[4] * pl.num_programs(0) + k) * STRETCH
    here = seg_ref[0:1, pl.ds(pl.multiple_of(start, LANES), STRETCH)].astype(F32)
    before = seg_ref[0:1, pl.ds(pl.multiple_of(jnp.maximum(start - LANES, 0), LANES), LANES)].astype(F32)
    before = jnp.where(start == 0, -1.0, before)
    both = jnp.broadcast_to(jnp.concatenate([before, here], axis=1), (8, LANES + STRETCH))
    row = iota((8, STRETCH), 0)
    tab = both[:, LANES:]
    for j in (1, 2, 3):
        tab = jnp.where(row == j, pltpu.roll(both, j, 1)[:, LANES:], tab)
    tab = jnp.where(row == 4, before[:, LANES - 1 :], tab)
    tab_ref[...] = jnp.where(row == 5, here[:, STRETCH - 1 :], tab)


def columns_of(tab_ref):
    tab = tab_ref[...]
    row = iota(tab.shape, 0)
    test = jnp.where(tab == tab[0:1], 1.0, 0.0)
    value = jnp.where(row == 0, tab, test).astype(BF)
    eye = (iota((8, LANES), 0) == iota((8, LANES), 1)).astype(F32).astype(BF)
    return dot_tn(value, eye)


def load_heads(hp_ref, wide_ref):
    wide_ref[...] = jnp.zeros_like(wide_ref)
    wide_ref[0:3, 0 : hp_ref.shape[1]] = hp_ref[...]


def expand_of(channels):
    head = jnp.right_shift(iota((channels, LANES), 0), 6)
    return (head == iota((channels, LANES), 1)).astype(F32).astype(BF)


def skip_of(wide_ref, expand):
    return exact(dot_nt, jnp.broadcast_to(wide_ref[2:3, :], (8, LANES)), expand, 3, True)


def conv_taps(u, taps, masks):
    total = taps[4:5] + taps[3:4] * u[HALO:]
    for j in (1, 2, 3):
        total = total + taps[3 - j : 4 - j] * (pltpu.roll(u, j, 0)[HALO:] * masks[j - 1])
    return total


def act_and_slope(v):
    sig = sigmoid(v)
    act = v * sig
    return act, sig + act * (1.0 - sig)


def first_kernel(
    idx_ref, own_ref, near_ref, nearx_ref, far_ref, farx_ref, normed_ref, nhalo_ref, km_ref, ks_ref, heads_ref, tab_ref,
    pre_ref, phalo_ref, x_ref, xs_ref, slope_ref, bc_ref, slopes_ref, step_ref, cum_ref, sgm_ref, state_ref, fac_ref,
    total_ref,
    held, sems, edge, carry, hp_ref, expand_ref,
):
    k = pl.program_id(0)
    channels = x_ref.shape[1]
    count, chunk = held.shape[0], held.shape[1]

    def project(rows):
        total = dot_nn(rows[:, :chunk], held[0])
        for a in range(1, count):
            total = total + dot_nn(rows[:, a * chunk : (a + 1) * chunk], held[a])
        return total.astype(BF)

    @pl.when(k == 0)
    def _():
        copies = fetches(idx_ref, (own_ref, near_ref, nearx_ref, far_ref, farx_ref), held, sems)
        for copy in copies:
            copy.start()
        carry[...] = jnp.zeros_like(carry)
        load_heads(heads_ref, hp_ref)
        expand_ref[...] = expand_of(channels)
        for copy in copies:
            copy.wait()
        before = project(nhalo_ref[...])
        phalo_ref[...] = before
        edge[...] = before

    pre_ref[...] = project(normed_ref[...])

    def ext(lanes):
        return jnp.concatenate([edge[:, lanes].astype(F32), pre_ref[:, lanes].astype(F32)], axis=0)

    col = columns_of(tab_ref)
    masks = [col[:, j : j + 1] for j in (1, 2, 3)]
    alive, ends = col[:, 4:5], col[:, 5:6]

    raw = pre_ref[:, SHARED:LEAD].astype(F32)
    pre = raw + hp_ref[1:2, :]
    soft = jnp.exp(-jnp.abs(pre))
    step = jnp.maximum(pre, 0.0) + jnp.log1p(soft)
    step_ref[...] = step
    sgm_ref[...] = sigmoid(pre)
    log_decay = step * -jnp.exp(hp_ref[0:1, :])
    tri = (iota((STRETCH, STRETCH), 0) >= iota((STRETCH, STRETCH), 1)).astype(F32).astype(BF)
    cum = exact(dot_nn, tri, log_decay, 3, False)
    cum_ref[...] = cum
    last = cum[STRETCH - 1 : STRETCH]
    ef = jnp.exp(last - cum) * ends
    factor = jnp.exp(last) * alive[STRETCH - 1 : STRETCH]
    fac_row = exact(dot_nt, jnp.broadcast_to(factor, (8, LANES)), expand_ref[...], 3, True)
    fac_ref[0] = fac_row

    acts, slopes = act_and_slope(
        conv_taps(ext(slice(0, SHARED)), ks_ref[...], masks)
    )
    bc_ref[...] = acts.astype(BF)
    slopes_ref[...] = slopes.astype(BF)
    keys_t = jnp.transpose(acts[:, 0:STATE]).astype(BF)
    for pair, (at, width) in enumerate(pair_widths(channels)):
        lanes = slice(at, at + width)
        u = ext(slice(LEAD + at, LEAD + at + width))
        act, slope = act_and_slope(conv_taps(u, km_ref[:, lanes], masks))
        low = act.astype(BF)
        x_ref[:, lanes] = low
        slope_ref[:, lanes] = slope.astype(BF)
        xs = (low.astype(F32) * spread(step, pair, width)).astype(BF)
        xs_ref[:, lanes] = xs
        xe = (xs.astype(F32) * spread(ef, pair, width)).astype(BF)
        state = dot_nn(keys_t, xe)
        state_ref[0, :, lanes] = state
        carry[:, lanes] = carry[:, lanes] * fac_row[0:1, lanes] + state

    edge[...] = pre_ref[STRETCH - HALO :, :]

    @pl.when(k == pl.num_programs(0) - 1)
    def _():
        total_ref[...] = carry[...].astype(BF)


def doc_mask(seg_col, seg_row, shape, transposed):
    down, across = iota(shape, 0), iota(shape, 1)
    order = (across >= down) if transposed else (down >= across)
    return (seg_col == seg_row) & order


def second_kernel(
    bc_ref, x_ref, xs_ref, cum_ref, state_ref, fac_ref, enter_ref, heads_ref, tab_ref,
    y_ref, hist_ref,
    hold, hp_ref, skip_ref,
):
    k = pl.program_id(0)
    channels = x_ref.shape[1]

    @pl.when(k == 0)
    def _():
        hold[...] = enter_ref[...].astype(F32)
        load_heads(heads_ref, hp_ref)
        skip_ref[...] = skip_of(hp_ref, expand_of(channels))

    hist_ref[pl.ds(k, 1)] = hold[...].astype(BF)[None]
    col = columns_of(tab_ref)
    alive = col[:, 4:5]
    keys, queries = bc_ref[:, 0:STATE], bc_ref[:, STATE:SHARED]
    gram = dot_nt(queries, keys)
    valid = doc_mask(col[:, 0:1], tab_ref[0:1, :], (STRETCH, STRETCH), False)
    gram = jnp.where(valid, gram, 0.0)
    cum = cum_ref[...]
    cum_t = jnp.transpose(cum)
    rise = jnp.exp(cum) * alive
    for pair, (at, width) in enumerate(pair_widths(channels)):
        lanes = slice(at, at + width)
        xs = xs_ref[:, lanes]
        top = bottom = 0.0
        for which, mask in enumerate(head_masks(width)):
            h = 2 * pair + which
            here = masked(xs, mask)
            down, across = cum[:, h : h + 1], cum_t[h : h + 1, :]
            decay = jnp.exp(jnp.minimum(down[:HALF] - across[:, :HALF], 0.0))
            top = top + dot_nn((decay * gram[:HALF, :HALF]).astype(BF), here[:HALF])
            decay = jnp.exp(jnp.minimum(down[HALF:] - across, 0.0))
            bottom = bottom + dot_nn((decay * gram[HALF:]).astype(BF), here)
        within = jnp.concatenate([top, bottom], axis=0)
        old = hold[:, lanes]
        carried = dot_nn(queries, old.astype(BF)) * spread(rise, pair, width)
        hold[:, lanes] = old * fac_ref[0, 0:1, lanes] + state_ref[0, :, lanes]
        y = within + carried + skip_ref[0:1, lanes] * x_ref[:, lanes].astype(F32)
        y_ref[:, lanes] = y

    @pl.when(k == pl.num_programs(0) - 1)
    def _():
        hist_ref[pl.ds(k + 1, 1)] = hold[...].astype(BF)[None]


def store_halves(outs, *refs):
    first = pl.program_id(0) < pl.num_programs(0) // 2
    for here, keep_ref, send_ref in ((first, *refs[:2]), (~first, *refs[2:])):

        @pl.when(here)
        def _():
            for q, out in enumerate(outs):
                (send_ref if q % 2 else keep_ref)[q // 2] = out


def gate_kernel(
    idx_ref, own_ref, near_ref, nearx_ref, far_ref, farx_ref, normed_ref, y_ref, cot_ref, gain_ref,
    gate_ref, gg_ref, keepa_ref, senda_ref, keepb_ref, sendb_ref, stat_ref,
    held, sems,
):
    k = pl.program_id(0)
    channels = y_ref.shape[1]
    count, chunk = held.shape[0], held.shape[1]
    at_out = held.shape[2] // 2

    @pl.when(k == 0)
    def _():
        fetch_all(fetches(idx_ref, (own_ref, near_ref, nearx_ref, far_ref, farx_ref), held, sems))

    gates = dot_nn(normed_ref[:, :chunk], held[0, :, 0:channels])
    for a in range(1, count):
        gates = gates + dot_nn(normed_ref[:, a * chunk : (a + 1) * chunk], held[a, :, 0:channels])
    gate_ref[...] = gates.astype(BF)
    square = jnp.zeros((STRETCH, LANES), F32)
    for at, width in pair_widths(channels):
        lanes = slice(at, at + width)
        gate = gate_ref[:, lanes].astype(F32)
        gated = y_ref[:, lanes] * (gate * sigmoid(gate))
        gg_ref[:, lanes] = (gated * gain_ref[0:1, lanes]).astype(BF)
        square = square + padded(gated * gated)
    cross = jnp.zeros((STRETCH, LANES), F32)
    outs = []
    for q in range(count):
        a = jnp.bitwise_xor(idx_ref[6], q)
        out = dot_nt(gg_ref[...], held[a, :, at_out : at_out + channels])
        outs.append(out.astype(BF))
        inner = out * cot_ref[:, pl.ds(pl.multiple_of(a * chunk, LANES), chunk)].astype(F32)
        for part in range(0, chunk, LANES):
            cross = cross + inner[:, part : part + LANES]
    ones = jnp.ones((8, LANES), BF)
    square = exact(dot_nt, ones, square, 3, False)
    cross = exact(dot_nt, ones, cross, 3, False)
    stat_ref[...] = jnp.where(iota((8, STRETCH), 0) == 0, square, cross)
    store_halves(outs, keepa_ref, senda_ref, keepb_ref, sendb_ref)


def padded(v):
    if v.shape[1] == LANES:
        return v
    return jnp.concatenate([v, jnp.zeros((v.shape[0], LANES - v.shape[1]), v.dtype)], axis=1)


def gng_kernel(idx_ref, own_ref, near_ref, nearx_ref, far_ref, farx_ref, cot_ref, gng_ref, held, sems):
    count, chunk = held.shape[0], held.shape[1]
    channels = gng_ref.shape[1]

    @pl.when(pl.program_id(0) == 0)
    def _():
        out = pl.ds(own_ref.shape[1] // 2, held.shape[2])
        fetch_all(fetches(idx_ref, (own_ref, near_ref, nearx_ref, far_ref, farx_ref), held, sems, out))

    total = dot_nn(cot_ref[:, :chunk], held[0, :, 0:channels])
    for a in range(1, count):
        total = total + dot_nn(cot_ref[:, a * chunk : (a + 1) * chunk], held[a, :, 0:channels])
    gng_ref[...] = total.astype(BF)


def third_kernel(
    stat_ref, y_ref, gate_ref, gng_ref, gain_ref, bc_ref, cum_ref, fac_ref, tab_ref,
    gy_ref, gi_ref, inv_ref, flow_ref, gaingrad_ref,
    hold,
):
    i = pl.program_id(0)
    channels = y_ref.shape[1]

    @pl.when(i == 0)
    def _():
        hold[...] = jnp.zeros_like(hold)
        gaingrad_ref[...] = jnp.zeros_like(gaingrad_ref)

    pick = iota((8, LANES), 0)
    stat = stat_ref[...]
    square = exact(dot_tn, stat, (pick == 0).astype(F32).astype(BF), 3, True)
    cross = exact(dot_tn, stat, (pick == 1).astype(F32).astype(BF), 3, True)
    inv = lax.rsqrt(square / INNER + EPSILON)
    inv_ref[...] = inv
    back = inv * inv * inv * (cross / INNER)
    rise = jnp.exp(cum_ref[...]) * columns_of(tab_ref)[:, 4:5]
    queries_t = jnp.transpose(bc_ref[:, STATE:SHARED].astype(F32)).astype(BF)
    for pair, (at, width) in enumerate(pair_widths(channels)):
        lanes = slice(at, at + width)
        gate = gate_ref[:, lanes].astype(F32)
        act, slope = act_and_slope(gate)
        y = y_ref[:, lanes]
        gated = y * act
        gng = gng_ref[:, lanes].astype(F32)
        along = inv[:, :width]
        grad = along * (gain_ref[0:1, lanes] * gng) - gated * back[:, :width]
        gaingrad_ref[0:1, lanes] += jnp.sum(gng * gated * along, axis=0, keepdims=True)
        gy = (grad * act).astype(BF)
        gy_ref[:, lanes] = gy
        gi_ref[:, lanes] = (grad * y * slope).astype(BF)
        gyr = (gy.astype(F32) * spread(rise, pair, width)).astype(BF)
        hold[:, lanes] = dot_nn(queries_t, gyr) + fac_ref[0, 0:1, lanes] * hold[:, lanes]

    @pl.when(i == pl.num_programs(0) - 1)
    def _():
        flow_ref[...] = hold[...].astype(BF)


def conv_back(post, u, taps, masks, kgrad_ref, lanes):
    full = post.shape[0] + HALO
    pad = jnp.zeros((HALO, post.shape[1]), F32)
    total = jnp.concatenate([pad, post * taps[3:4]], axis=0)
    kgrad_ref[4:5, lanes] += jnp.sum(post, axis=0, keepdims=True)
    kgrad_ref[3:4, lanes] += jnp.sum(post * u[HALO:], axis=0, keepdims=True)
    for j in (1, 2, 3):
        here = post * masks[j - 1]
        kgrad_ref[3 - j : 4 - j, lanes] += jnp.sum(
            here * pltpu.roll(u, j, 0)[HALO:], axis=0, keepdims=True
        )
        wide = jnp.concatenate([pad, here * taps[3 - j : 4 - j]], axis=0)
        total = total + pltpu.roll(wide, full - j, 0)
    return total


def fourth_kernel(
    idx_ref, own_ref, near_ref, nearx_ref, far_ref, farx_ref,
    gy_ref, x_ref, xs_ref, slope_ref, y_ref, bc_ref, slopes_ref, step_ref, cum_ref, sgm_ref, pre_ref, prev_ref,
    phalo_ref, ht_ref, hn_ref, fac_ref, enter_ref, km_ref, ks_ref, heads_ref, tab_ref, gategrad_ref,
    g_ref, ghalo_ref, small_ref, back_ref,
    held, sems, hold, edge, hp_ref, expand_ref, skip_ref, skipgrad_ref, kmgrad_ref, ksgrad_ref, head_ref,
):
    i = pl.program_id(0)
    k = pl.num_programs(0) - 1 - i
    channels = x_ref.shape[1]
    copies = fetches(idx_ref, (own_ref, near_ref, nearx_ref, far_ref, farx_ref), held, sems)

    @pl.when(i == 0)
    def _():
        for copy in copies:
            copy.start()
        hold[...] = enter_ref[...].astype(F32)
        edge[...] = jnp.zeros_like(edge)
        load_heads(heads_ref, hp_ref)
        expand_ref[...] = expand_of(channels)
        skip_ref[...] = skip_of(hp_ref, expand_ref[...])
        kmgrad_ref[...] = jnp.zeros_like(kmgrad_ref)
        ksgrad_ref[...] = jnp.zeros_like(ksgrad_ref)
        head_ref[...] = jnp.zeros_like(head_ref)
        skipgrad_ref[...] = jnp.zeros_like(skipgrad_ref)

    def ext(lanes):
        before = jnp.where(k == 0, phalo_ref[:, lanes].astype(F32), prev_ref[:, lanes].astype(F32))
        return jnp.concatenate([before, pre_ref[:, lanes].astype(F32)], axis=0)

    def put(lanes, total):
        g_ref[0 : STRETCH - HALO, lanes] = total[HALO:STRETCH].astype(BF)
        g_ref[STRETCH - HALO :, lanes] = (total[STRETCH:] + edge[:, lanes]).astype(BF)
        edge[:, lanes] = total[:HALO]

    col = columns_of(tab_ref)
    masks = [col[:, j : j + 1] for j in (1, 2, 3)]
    alive, ends = col[:, 4:5], col[:, 5:6]
    keys, queries = bc_ref[:, 0:STATE], bc_ref[:, STATE:SHARED]
    queries_t = jnp.transpose(queries.astype(F32)).astype(BF)
    valid = doc_mask(col[:, 0:1], tab_ref[0:1, :], (STRETCH, STRETCH), True)
    gram = jnp.where(valid, dot_nt(keys, queries), 0.0)
    step, cum = step_ref[...], cum_ref[...]
    cum_t = jnp.transpose(cum)
    rise = jnp.exp(cum) * alive
    ef = jnp.exp(cum[STRETCH - 1 : STRETCH] - cum) * ends
    gram_top = jnp.zeros((HALF, STRETCH), F32)
    gram_bottom = jnp.zeros((HALF, HALF), F32)
    grad_keys = jnp.zeros((STRETCH, STATE), F32)
    grad_queries = jnp.zeros((STRETCH, STATE), F32)
    cumterm = jnp.zeros((STRETCH, LANES), F32)
    colterm = jnp.zeros((STRETCH, LANES), F32)
    endterm = jnp.zeros((8, LANES), F32)
    for pair, (at, width) in enumerate(pair_widths(channels)):
        lanes = slice(at, at + width)
        expand = expand_ref[lanes, :]
        gy, xs = gy_ref[:, lanes], xs_ref[:, lanes]
        gyf, xf = gy.astype(F32), x_ref[:, lanes].astype(F32)
        skip = skip_ref[0:1, lanes]
        top = bottom = 0.0
        for which, mask in enumerate(head_masks(width)):
            h = 2 * pair + which
            here = masked(gy, mask)
            down, across = cum[:, h : h + 1], cum_t[h : h + 1, :]
            decay = jnp.exp(jnp.minimum(across - down[:HALF], 0.0))
            top = top + dot_nn((decay * gram[:HALF]).astype(BF), here)
            gram_top = gram_top + dot_nt(xs[:HALF], here) * decay
            decay = jnp.exp(jnp.minimum(across[:, HALF:] - down[HALF:], 0.0))
            bottom = bottom + dot_nn((decay * gram[HALF:, HALF:]).astype(BF), here[HALF:])
            gram_bottom = gram_bottom + dot_nt(xs[HALF:], here[HALF:]) * decay
        grad_xs = jnp.concatenate([top, bottom], axis=0)
        after = hold[:, lanes]
        low = after.astype(BF)
        efs = spread(ef, pair, width)
        from_end = dot_nn(keys, low) * efs
        grad_xs = grad_xs + from_end
        gyr = (gyf * spread(rise, pair, width)).astype(BF)
        xe = (xs.astype(F32) * efs).astype(BF)
        grad_queries = grad_queries + dot_nt(gyr, ht_ref[0, :, lanes])
        grad_keys = grad_keys + dot_nt(xe, low)
        ended = jnp.sum(after * ht_ref[0, :, lanes].astype(F32), axis=0, keepdims=True)
        ended = ended * fac_ref[0, 0:1, lanes] + jnp.sum(xs.astype(F32) * from_end, axis=0, keepdims=True)
        endterm = endterm + exact(dot_nn, jnp.broadcast_to(ended, (8, width)), expand, 3, True)
        hold[:, lanes] = dot_nn(queries_t, gyr) + fac_ref[0, 0:1, lanes] * after
        xsf = xs.astype(F32)
        colterm = colterm + exact(dot_nn, xf * grad_xs, expand, 1, True)
        cumterm = cumterm + exact(dot_nn, gyf * (y_ref[:, lanes] - skip * xf) - xsf * grad_xs, expand, 2, True)
        skipgrad_ref[0:1, lanes] += jnp.sum(gyf * xf, axis=0, keepdims=True)
        grad_x = grad_xs * spread(step, pair, width) + skip * gyf
        post = grad_x * slope_ref[:, lanes].astype(F32)
        at_g = slice(LEAD + at, LEAD + at + width)
        put(at_g, conv_back(post, ext(at_g), km_ref[:, lanes], masks, kmgrad_ref, lanes))

    gram_top = jnp.where(valid[:HALF], gram_top, 0.0).astype(BF)
    gram_bottom = jnp.where(valid[HALF:, HALF:], gram_bottom, 0.0).astype(BF)
    grad_keys = grad_keys + jnp.concatenate(
        [dot_nn(gram_top, queries), dot_nn(gram_bottom, queries[HALF:])], axis=0
    )
    lower = jnp.concatenate([jnp.zeros((HALF, HALF), BF), gram_bottom], axis=1)
    gram_all = jnp.concatenate([gram_top, lower], axis=0)
    grad_queries = grad_queries + dot_tn(gram_all, keys)
    post = jnp.concatenate([grad_keys, grad_queries], axis=1) * slopes_ref[...].astype(F32)
    shared = slice(0, SHARED)
    put(shared, conv_back(post, ext(shared), ks_ref[...], masks, ksgrad_ref, shared))

    rate = -jnp.exp(hp_ref[0:1, :])
    grad_cum = cumterm
    at_end = iota((STRETCH, LANES), 0) == STRETCH - 1
    grad_cum = grad_cum + jnp.where(at_end, endterm[0:1], 0.0)
    upper = (iota((STRETCH, STRETCH), 1) >= iota((STRETCH, STRETCH), 0)).astype(F32).astype(BF)
    grad_log = exact(dot_nn, upper, grad_cum, 3, False)
    grad_pre = (colterm + grad_log * rate) * sgm_ref[...]
    g_ref[:, SHARED:LEAD] = grad_pre.astype(BF)
    head_ref[0:1, :] += jnp.sum(grad_log * step, axis=0, keepdims=True) * rate
    head_ref[1:2, :] += jnp.sum(grad_pre, axis=0, keepdims=True)

    @pl.when(k == 0)
    def _():
        ghalo_ref[:, 0:SHARED] = edge[:, 0:SHARED].astype(BF)
        ghalo_ref[:, LEAD:] = edge[:, LEAD:].astype(BF)
        ghalo_ref[:, SHARED:LEAD] = jnp.zeros((HALO, LANES), BF)
        wide = jnp.broadcast_to(skipgrad_ref[0:1, :], (8, channels))
        small_ref[...] = jnp.zeros_like(small_ref)
        for tap in range(5):
            small_ref[1:2, tap * SHARED : (tap + 1) * SHARED] = ksgrad_ref[tap : tap + 1, :]
        small_ref[3:8, 0:channels] = kmgrad_ref[0:5, :]
        small_ref[8:9, 0:channels] = gategrad_ref[0:1, :]
        small_ref[9:11, 0:LANES] = head_ref[0:2, :]
        small_ref[11:12, 0:LANES] = exact(dot_nn, wide, expand_ref[...], 3, True)[0:1]
        for copy in copies:
            copy.wait()
        chunk = held.shape[1]
        for a in range(held.shape[0]):
            back_ref[:, a * chunk : (a + 1) * chunk] = dot_nt(ghalo_ref[...], held[a])


def normed_kernel(
    idx_ref, own0_ref, near0_ref, nearx0_ref, far0_ref, farx0_ref, own_ref, near_ref, nearx_ref, far_ref, farx_ref,
    gi_ref, g_ref, normed_ref, back_ref, small_ref,
    keepa_ref, senda_ref, keepb_ref, sendb_ref, sums_ref, cross_ref,
    held0, held, sems0, sems,
):
    i = pl.program_id(0)
    last = i == pl.num_programs(0) - 1
    rows = gi_ref.shape[0]
    count, chunk, channels = held0.shape

    @pl.when(i == 0)
    def _():
        pieces = (own0_ref, near0_ref, nearx0_ref, far0_ref, farx0_ref)
        columns = pl.ds(0, channels)
        copies = fetches(idx_ref, pieces, held0, sems0, columns)
        copies += fetches(idx_ref, (own_ref, near_ref, nearx_ref, far_ref, farx_ref), held, sems)
        fetch_all(copies)
        sums_ref[...] = small_ref[...]
        cross_ref[...] = jnp.zeros_like(cross_ref)

    cross = jnp.zeros((rows, LANES), F32)
    outs = []
    for q in range(count):
        a = jnp.bitwise_xor(idx_ref[6], q)
        lanes = pl.ds(pl.multiple_of(a * chunk, LANES), chunk)
        width = gi_ref.shape[1]
        total = dot_nt(gi_ref[...], held0[a, :, 0:width]) + dot_nt(g_ref[...], held[a])
        tail = total[rows - HALO :] + jnp.where(last, back_ref[:, lanes], 0.0)
        total = jnp.concatenate([total[: rows - HALO], tail], axis=0)
        outs.append(total.astype(BF))
        inner = total * normed_ref[:, lanes].astype(F32)
        sums_ref[0:1, lanes] += jnp.sum(inner, axis=0, keepdims=True)
        for part in range(0, chunk, LANES):
            cross = cross + inner[:, part : part + LANES]
    row = exact(dot_nt, jnp.ones((8, LANES), BF), cross, 3, False)[0:1]
    cross_ref[2:3, pl.ds(pl.multiple_of(i * rows, LANES), rows)] = row
    store_halves(outs, keepa_ref, senda_ref, keepb_ref, sendb_ref)


def put_chunk(idx_ref, keep_ref, send_ref, lanes, value):
    j = pl.program_id(0)
    half = keep_ref.shape[1]
    top, bottom = value[:half].astype(BF), value[half:].astype(BF)

    @pl.when(j == idx_ref[1])
    def _():
        keep_ref[0, :, lanes] = top
        keep_ref[1, :, lanes] = bottom

    @pl.when(j == idx_ref[2])
    def _():
        send_ref[0, :, lanes] = top
        send_ref[1, :, lanes] = bottom

    for source, target in ((0, 3), (3, 2)):
        for c, (mine, other) in enumerate(((top, bottom), (bottom, top))):

            @pl.when((j == idx_ref[source]) & (idx_ref[4] == c))
            def _():
                keep_ref[target, :, lanes] = mine
                send_ref[target, :, lanes] = other


def weight_kernel(idx_ref, normed_ref, nhalo_ref, g_ref, ghalo_ref, keep_ref, send_ref):
    value = dot_tn(normed_ref[...], g_ref[...]) + dot_tn(nhalo_ref[...], ghalo_ref[...])
    put_chunk(idx_ref, keep_ref, send_ref, slice(None), value)


def gate_out_kernel(idx_ref, normed_ref, gi_ref, cot_ref, inv_ref, gg_ref, keep_ref, send_ref):
    channels = gi_ref.shape[1]
    wide = keep_ref.shape[2] // 2
    put_chunk(idx_ref, keep_ref, send_ref, slice(0, channels), dot_tn(normed_ref[...], gi_ref[...]))
    scaled = [
        (cot_ref[:, at : at + LANES].astype(F32) * inv_ref[...]).astype(BF)
        for at in range(0, cot_ref.shape[1], LANES)
    ]
    value = dot_tn(jnp.concatenate(scaled, axis=1), gg_ref[...])
    put_chunk(idx_ref, keep_ref, send_ref, slice(wide, wide + channels), value)


def final_kernel(idx_ref, *refs):
    go, w, (main_ref, step_ref, shared_ref, out_ref) = refs[:4], refs[4:8], refs[8:]
    channels = main_ref.shape[2]
    wide = go[0].shape[2] // 2

    def total(terms, lanes):
        value = terms[0][0, :, lanes].astype(F32)
        for term in terms[1:]:
            value = value + term[0, :, lanes].astype(F32)
        return value

    shared_ref[...] = total(w, slice(0, SHARED)).astype(shared_ref.dtype)
    steps = total(w, slice(SHARED, LEAD))
    rows = step_ref.shape[1]
    steps = jnp.concatenate([steps, jnp.zeros((-rows % LANES, LANES), F32)], axis=0)
    step_ref[...] = jnp.transpose(steps)[0 : step_ref.shape[0], 0:rows]
    for at, width in pair_widths(channels):
        lanes = slice(at, at + width)
        main_ref[0, :, lanes] = total(go, lanes)
        main_ref[1, :, lanes] = total(w, slice(LEAD + at, LEAD + at + width))
        out_ref[:, lanes] = total(go, slice(wide + at, wide + at + width))


def sums_kernel(sums_ref, gain_ref, *refs):
    terms, (all_ref, km_ref, ks_ref, head_ref, gate_ref) = refs[:-5], refs[-5:]
    channels = km_ref.shape[1]
    over = terms[0][0:2]
    if len(terms) == 4:
        over = (over + terms[1][0:2]) + (terms[2][0:2] + terms[3][0:2])
    all_ref[...] = over[0:1] / gain_ref[...]
    for tap in range(5):
        ks_ref[tap : tap + 1, :] = over[1:2, tap * SHARED : (tap + 1) * SHARED]
    km_ref[...] = sums_ref[3:8, 0:channels]
    gate_ref[...] = sums_ref[8:9, 0:channels]
    head_ref[...] = sums_ref[9:12, 0 : head_ref.shape[1]]


def output_kernel(own_ref, inv_ref, *refs):
    out_ref = refs[-1]
    inv = inv_ref[...]
    for part, (keep_ref, got_ref, far_ref) in enumerate((refs[0:3], refs[3:6])):

        @pl.when(pl.program_id(0) == part)
        def _():
            for at in range(0, out_ref.shape[1], LANES):
                lanes = slice(at, at + LANES)
                total = keep_ref[0, :, lanes].astype(F32) + got_ref[0, :, lanes].astype(F32)
                total = (total + far_ref[0, :, lanes].astype(F32)) * inv
                out_ref[:, lanes] = (own_ref[:, lanes].astype(F32) + total).astype(BF)


def tokens_kernel(
    width, own_ref, cot_ref, inv_ref, t0_ref, t1_ref, t2_ref, t3_ref, gain_ref,
    keepa_ref, gota_ref, fara_ref, keepb_ref, gotb_ref, farb_ref, out_ref,
):
    inv = inv_ref[...]
    pick = (iota((8, LANES), 0) == 2).astype(F32).astype(BF)
    cross = (t0_ref[...] + t1_ref[...]) + (t2_ref[...] + t3_ref[...])
    cross = exact(dot_tn, cross, pick, 3, True)
    back = inv * inv * (cross / width)
    halves = ((keepa_ref, gota_ref, fara_ref), (keepb_ref, gotb_ref, farb_ref))
    for part, (keep_ref, got_ref, far_ref) in enumerate(halves):

        @pl.when(pl.program_id(0) == part)
        def _():
            for at in range(0, out_ref.shape[1], LANES):
                lanes = slice(at, at + LANES)
                total = keep_ref[0, :, lanes].astype(F32) + got_ref[0, :, lanes].astype(F32)
                total = total + far_ref[0, :, lanes].astype(F32)
                out_ref[:, lanes] = (
                    inv * gain_ref[0:1, lanes] * total
                    - own_ref[:, lanes].astype(F32) * back
                    + cot_ref[:, lanes].astype(F32)
                )


def whole(array):
    rank = len(array.shape)
    return pl.BlockSpec(array.shape, lambda *_: (0,) * rank)


def call(name, kernel, grid, ins, in_specs, outs, out_specs, scratch=(), flops=0, prefetch=0):
    moved = sum(a.size * a.dtype.itemsize for a in (*ins, *outs))
    return pl.pallas_call(
        kernel,
        out_shape=outs,
        grid_spec=pltpu.PrefetchScalarGridSpec(
            num_scalar_prefetch=prefetch,
            grid=grid,
            in_specs=in_specs,
            out_specs=out_specs,
            scratch_shapes=list(scratch),
        ),
        compiler_params=pltpu.CompilerParams(
            dimension_semantics=("arbitrary",) * len(grid), vmem_limit_bytes=LIMITS.get(name, 16) * 2**20
        ),
        cost_estimate=pl.CostEstimate(
            flops=int(flops), bytes_accessed=int(moved), transcendentals=0
        ),
    )(*ins)


def shape(dims, kind):
    return jax.ShapeDtypeStruct(dims, kind)


def add(*terms):
    return sum(term.astype(F32) for term in terms).astype(BF)


def per_device(
    tokens, segments, norm_gain, proj_main, proj_shared, proj_step, conv_main, conv_shared,
    head_params, gate_gain, output_projection, cotangent,
):
    _, length, width = tokens.shape
    nf, nc, nt = lax.axis_size("fsdp"), lax.axis_size("ctx"), lax.axis_size("tp")
    assert nf == 4 and nc == 2
    f, c, t = lax.axis_index("fsdp"), lax.axis_index("ctx"), lax.axis_index("tp")
    heads = head_params.shape[1]
    channels = heads * HEADDIM
    lead = LEAD + channels
    wide = -(-channels // LANES) * LANES
    nb = length // STRETCH
    chunk = width // nf
    half = chunk // 2
    share = width // nt
    line = nt == nf
    rot = t if line else jnp.zeros_like(t)
    both = ("fsdp", "ctx")
    spots = [(i, j) for i in range(nf) for j in range(nc)]
    role = [(i * nc + j, (i ^ (1 + j)) * nc + j) for i, j in spots]
    turn = [(i * nc + j, (i ^ (2 - j)) * nc + j) for i, j in spots]
    across_chip = [(i * nc + j, (i ^ 3) * nc + j) for i, j in spots]
    swap = [(0, 1), (1, 0)]
    idx = jnp.stack([f, f ^ (1 + c), f ^ (2 - c), f ^ 3, c, rot, rot, rot]).astype(jnp.int32)

    def tp_sum(v):
        if not line:
            return lax.psum(v, "tp")
        first, second, third = (
            lax.ppermute(v, "tp", [(i, i ^ m) for i in range(nt)]) for m in (1, 2, 3)
        )
        return (v + first) + (second + third)

    def tp_terms(v):
        if not line:
            return (lax.psum(v, "tp"),)
        return (v, *(lax.ppermute(v, "tp", [(i, i ^ m) for i in range(nt)]) for m in (1, 2, 3)))

    def one(v, at):
        return lax.dynamic_slice_in_dim(v, at, 1, 0)

    def gather_rows(shard, direct):
        columns = shard.shape[1]
        pieces = shard.reshape(2, half, columns)
        near = lax.ppermute(pieces, both, role)
        if direct:
            far = lax.ppermute(one(pieces, c), both, across_chip)
        else:
            far = lax.ppermute(one(near, c), both, turn)
        near_other = lax.ppermute(near, "ctx", swap)
        far_other = lax.ppermute(far, "ctx", swap)
        return (
            shard, near.reshape(chunk, columns), near_other.reshape(chunk, columns), far[0], far_other[0]
        )

    def scatter_rows(keep, send):
        got = lax.ppermute(send, "ctx", swap)
        far = lax.ppermute(add(keep[2:3], got[2:3]), both, turn)
        which = iota((2, 1, 1), 0) == c
        near = add(keep[0:2], got[0:2], jnp.where(which, far.astype(F32), 0.0))
        near = lax.ppermute(near, both, role)
        return keep, got, near, lax.ppermute(one(near, 1 - c), "ctx", swap)

    def scatter_tp(keep, send):
        if not line:
            full = jnp.concatenate([keep[0], send[0], keep[1], send[1]], axis=1)
            return (lax.psum_scatter(full, "tp", scatter_dimension=1, tiled=True),)
        got = lax.ppermute(send, "tp", [(i, i ^ 1) for i in range(nt)])
        far = lax.ppermute(add(keep[1:2], got[1:2]), "tp", [(i, i ^ 2) for i in range(nt)])
        return keep, got, far

    any_spec = pl.BlockSpec(memory_space=pl.ANY)
    sems = pltpu.SemaphoreType.DMA((5,))

    def block(columns, back=False):
        if back:
            return pl.BlockSpec((STRETCH, columns), lambda i, *_: (nb - 1 - i, 0))
        return pl.BlockSpec((STRETCH, columns), lambda i, *_: (i, 0))

    def across(back=False):
        if back:
            return pl.BlockSpec((8, STRETCH), lambda i, *_: (0, nb - 1 - i))
        return pl.BlockSpec((8, STRETCH), lambda i, *_: (0, i))

    def stacked(rows, columns, back=False, off=0):
        if back:
            return pl.BlockSpec((1, rows, columns), lambda i, *_: (nb - 1 - i + off, 0, 0))
        return pl.BlockSpec((1, rows, columns), lambda i, *_: (i + off, 0, 0))

    mid = length // 2
    part_a = pl.BlockSpec((2, STRETCH, chunk), lambda i, *_: (0, jnp.minimum(i, nb // 2 - 1), 0))
    part_b = pl.BlockSpec((2, STRETCH, chunk), lambda i, *_: (0, jnp.maximum(i - nb // 2, 0), 0))

    def main_part(which):
        return pl.BlockSpec((1, chunk, channels), lambda i: (which, 0, 0))

    tokens2, cot2 = tokens[0], cotangent[0]
    step_t = jnp.transpose(proj_step)
    ins = (proj_shared, step_t, proj_main)
    outs = (shape((chunk, lead), BF),)
    shard_in = call(
        "k_packin", pack_in_kernel, (1,), ins, [whole(proj_shared), whole(step_t), main_part(1)],
        outs, [whole(outs[0])],
    )[0]
    w_in = gather_rows(shard_in, False)
    halo = lax.ppermute(tokens2[length - HALO :], "ctx", [(0, 1)])
    ins = (proj_main, output_projection)
    outs = (shape((chunk, 2 * wide), BF),)
    shard_go = call(
        "k_packgo", pack_go_kernel, (1,), ins, [main_part(0), whole(output_projection)],
        outs, [whole(outs[0])],
    )[0]
    w_go = gather_rows(shard_go, True)

    gate_row = gate_gain[None]
    gain_row = norm_gain[None]

    ins = (idx, tokens2, halo, cot2, gain_row, segments)
    outs = (
        shape((length, width), BF), shape((HALO, width), BF), shape((length, chunk), BF),
        shape((length, chunk), BF), shape((length, LANES), F32), shape((8, length), F32),
    )
    normed, nhalo, own_tokens, own_cot, inv_rms, tab = call(
        "k_prep", functools.partial(prep_kernel, chunk), (nb,), ins,
        [block(width), whole(halo), block(width), whole(gain_row), whole(segments)],
        outs, [block(width), whole(outs[1]), block(chunk), block(chunk), block(LANES), across()], prefetch=1,
    )
    if not line:
        own_tokens = lax.dynamic_slice_in_dim(tokens2, t * share, share, 1)
        own_cot = lax.dynamic_slice_in_dim(cot2, t * share, share, 1)

    outs = (
        shape((length, lead), BF), shape((HALO, lead), BF),
        shape((length, channels), BF), shape((length, channels), BF), shape((length, channels), BF),
        shape((length, SHARED), BF), shape((length, SHARED), BF),
        shape((length, LANES), F32), shape((length, LANES), F32), shape((length, LANES), F32),
        shape((nb, STATE, channels), F32), shape((nb, 8, channels), F32), shape((STATE, channels), BF),
    )
    ins = (idx, *w_in, normed, nhalo, conv_main, conv_shared, head_params, tab)
    wide_row = pltpu.VMEM((8, LANES), F32)
    held_in = pltpu.VMEM((nf, chunk, lead), BF)
    pre, phalo, x, xs, slope, bc, slopes, step, cum, sgm, states, fac, total = call(
        "k_first", first_kernel, (nb,), ins,
        [any_spec] * 5
        + [block(width), whole(nhalo), whole(conv_main), whole(conv_shared), whole(head_params), across()],
        outs,
        [block(lead), whole(outs[1])] + [block(channels)] * 3 + [block(SHARED)] * 2 + [block(LANES)] * 3
        + [stacked(STATE, channels), stacked(8, channels), whole(outs[-1])],
        scratch=[
            held_in, sems, pltpu.VMEM((HALO, lead), BF), pltpu.VMEM((STATE, channels), F32), wide_row,
            pltpu.VMEM((channels, LANES), BF),
        ],
        prefetch=1, flops=2 * length * (STATE * channels + width * lead),
    )
    enter = lax.ppermute(total, "ctx", [(0, 1)])

    outs = (shape((length, channels), F32), shape((nb + 1, STATE, channels), BF))
    ins = (bc, x, xs, cum, states, fac, enter, head_params, tab)
    y, hist = call(
        "k_second", second_kernel, (nb,), ins,
        [
            block(SHARED), block(channels), block(channels), block(LANES), stacked(STATE, channels),
            stacked(8, channels), whole(enter), whole(head_params), across(),
        ],
        outs, [block(channels), whole(outs[1])],
        scratch=[pltpu.VMEM((STATE, channels), F32), wide_row, pltpu.VMEM((8, channels), F32)],
        flops=8 * length * STRETCH * channels,
    )

    outs = (
        shape((length, channels), BF), shape((length, channels), BF), *(shape((2, mid, chunk), BF),) * 4,
        shape((8, length), F32),
    )
    ins = (idx, *w_go, normed, y, cot2, gate_row)
    gate, gg, *out_parts, stat = call(
        "k_gate", gate_kernel, (nb,), ins,
        [any_spec] * 5 + [block(width), block(channels), block(width), whole(gate_row)],
        outs, [block(channels)] * 2 + [part_a, part_a, part_b, part_b, across()],
        scratch=[pltpu.VMEM((nf, chunk, 2 * wide), BF), sems],
        prefetch=1, flops=4 * length * width * channels,
    )
    out_a = scatter_tp(*out_parts[:2])
    out_b = scatter_tp(*out_parts[2:])
    stat = tp_sum(stat)
    outs = (shape((length, channels), BF),)
    gng = call(
        "k_gng", gng_kernel, (nb,), (idx, *w_go, cot2), [any_spec] * 5 + [block(width)], outs, [block(channels)],
        scratch=[pltpu.VMEM((nf, chunk, wide), BF), sems], prefetch=1, flops=2 * length * width * channels,
    )[0]

    outs = (
        shape((length, channels), BF), shape((length, channels), BF), shape((length, LANES), F32),
        shape((STATE, channels), BF), shape((8, channels), F32),
    )
    ins = (stat, y, gate, gng, gate_row, bc, cum, fac, tab)
    gy, gi, inv_gate, flow, gate_grad = call(
        "k_third", third_kernel, (nb,), ins,
        [
            across(True), block(channels, True), block(channels, True), block(channels, True), whole(gate_row),
            block(SHARED, True), block(LANES, True), stacked(8, channels, True), across(True),
        ],
        outs, [block(channels, True), block(channels, True), block(LANES, True), whole(outs[3]), whole(outs[4])],
        scratch=[pltpu.VMEM((STATE, channels), F32)],
        flops=2 * length * STATE * channels,
    )
    leaving = lax.ppermute(flow, "ctx", [(1, 0)])

    outs = (shape((4, half, 2 * wide), BF),) * 2
    ins = (idx, normed, gi, cot2, inv_gate, gg)
    grad_go = call(
        "k_go", gate_out_kernel, (nf,), ins,
        [
            pl.BlockSpec((length, chunk), lambda i, *_: (0, i)), whole(gi),
            pl.BlockSpec((length, chunk), lambda i, *_: (0, i)), whole(inv_gate), whole(gg),
        ],
        outs, [whole(outs[0])] * 2, prefetch=1,
        flops=4 * length * width * channels,
    )
    grad_go = scatter_rows(*grad_go)

    outs = (
        shape((length, lead), BF), shape((HALO, lead), BF), shape((16, width), F32), shape((HALO, width), F32),
    )
    ins = (
        idx, *w_in, gy, x, xs, slope, y, bc, slopes, step, cum, sgm, pre, pre, phalo, hist, hist, fac, leaving,
        conv_main, conv_shared, head_params, tab, gate_grad,
    )
    per_block = STRETCH // HALO
    g_in, ghalo, small, back = call(
        "k_fourth", fourth_kernel, (nb,), ins,
        [any_spec] * 5
        + [block(channels, True)] * 5 + [block(SHARED, True)] * 2 + [block(LANES, True)] * 3
        + [
            block(lead, True),
            pl.BlockSpec((HALO, lead), lambda i, *_: (jnp.maximum((nb - 1 - i) * per_block - 1, 0), 0)),
            whole(phalo), stacked(STATE, channels, True), stacked(STATE, channels, True, 1),
            stacked(8, channels, True), whole(leaving), whole(conv_main), whole(conv_shared),
            whole(head_params), across(True), whole(gate_grad),
        ],
        outs, [block(lead, True)] + [whole(o) for o in outs[1:]],
        scratch=[
            held_in, sems, pltpu.VMEM((STATE, channels), F32), pltpu.VMEM((HALO, lead), F32), wide_row,
            pltpu.VMEM((channels, LANES), BF), pltpu.VMEM((8, channels), F32), pltpu.VMEM((8, channels), F32),
            pltpu.VMEM((8, channels), F32), pltpu.VMEM((8, SHARED), F32), wide_row,
        ],
        prefetch=1, flops=16 * length * STRETCH * channels,
    )
    back = lax.ppermute(back, "ctx", [(1, 0)])

    outs = (shape((2, mid, chunk), BF),) * 4 + (shape((16, width), F32), shape((8, width), F32))
    ins = (idx, *w_go, *w_in, gi, g_in, normed, back, small)
    keep_a, send_a, keep_b, send_b, sums, cross = call(
        "k_normed", normed_kernel, (nb,), ins,
        [any_spec] * 10 + [block(channels), block(lead), block(width), whole(back), whole(small)],
        outs, [part_a, part_a, part_b, part_b, whole(outs[-2]), whole(outs[-1])],
        scratch=[pltpu.VMEM((nf, chunk, wide), BF), held_in, sems, sems],
        prefetch=1, flops=2 * length * width * (lead + channels),
    )
    normed_a = scatter_tp(keep_a, send_a)
    normed_b = scatter_tp(keep_b, send_b)

    outs = (shape((4, half, lead), BF),) * 2
    grad_w = call(
        "k_weight", weight_kernel, (nf,), (idx, normed, nhalo, g_in, ghalo),
        [
            pl.BlockSpec((length, chunk), lambda i, *_: (0, i)), pl.BlockSpec((HALO, chunk), lambda i, *_: (0, i)),
            whole(g_in), whole(ghalo),
        ],
        outs, [whole(outs[0])] * 2, prefetch=1,
        flops=2 * length * width * lead,
    )
    grad_w = scatter_rows(*grad_w)

    sums = sums + lax.ppermute(sums, "ctx", swap)
    for m in (1, 2):
        sums = sums + lax.ppermute(sums, "fsdp", [(i, i ^ m) for i in range(nf)])
    sum_terms = tp_terms(jnp.where(iota((8, 1), 0) < 2, sums[:8], cross))
    outs = (
        shape((1, width), F32), shape((5, channels), F32), shape((5, SHARED), F32), shape((3, heads), F32),
        shape((1, channels), F32),
    )
    ins = (sums, gain_row, *sum_terms)
    gain_all, grad_km, grad_ks, grad_head, grad_gate = call(
        "k_sums", sums_kernel, (1,), ins, [whole(v) for v in ins], outs, [whole(o) for o in outs]
    )
    grad_gain = lax.dynamic_slice_in_dim(gain_all[0], t * share, share, 0)
    own_gain = lax.dynamic_slice_in_dim(norm_gain, t * share, share, 0)

    def terms_of(columns):
        return [
            pl.BlockSpec((1, half, columns), lambda i, *_: (3, 0, 0)),
            pl.BlockSpec((1, half, columns), lambda i, *_: (3, 0, 0)),
            pl.BlockSpec((1, half, columns), lambda i, idx_ref: (idx_ref[4], 0, 0)),
            pl.BlockSpec((1, half, columns), lambda i, *_: (0, 0, 0)),
        ]

    outs = (
        shape((2, half, channels), F32), shape((heads, half), F32), shape((half, SHARED), BF if line else F32),
        shape((half, channels), F32),
    )
    grad_main, grad_step, grad_shared, grad_out = call(
        "k_final", final_kernel, (1,), (idx, *grad_go, *grad_w), terms_of(2 * wide) + terms_of(lead),
        outs, [whole(o) for o in outs], prefetch=1,
    )
    grad_shared = [v.astype(F32) for v in tp_terms(grad_shared)]
    if line:
        grad_shared = [(grad_shared[0] + grad_shared[1]) + (grad_shared[2] + grad_shared[3])]

    outs = (shape((length, share), BF),)
    if line:
        spec = pl.BlockSpec((mid, share), lambda i: (i, 0))
        only = pl.BlockSpec((1, mid, share), lambda i: (0, 0, 0))
        inv_spec = pl.BlockSpec((mid, LANES), lambda i: (i, 0))
        output = call(
            "k_output", output_kernel, (2,), (own_tokens, inv_gate, *out_a, *out_b), [spec, inv_spec] + [only] * 6,
            outs, [spec],
        )[0]
        outs = (shape((length, share), F32),)
        gain2 = own_gain[None]
        grad_tokens = call(
            "k_tokens", functools.partial(tokens_kernel, width), (2,),
            (own_tokens, own_cot, inv_rms, *sum_terms, gain2, *normed_a, *normed_b),
            [spec, spec, inv_spec]
            + [pl.BlockSpec((8, mid), lambda i: (0, i))] * 4
            + [whole(gain2)]
            + [only] * 6,
            outs, [spec],
        )[0]
    else:
        normed_sum = jnp.concatenate([normed_a[0], normed_b[0]], axis=0).astype(F32)
        out_sum = jnp.concatenate([out_a[0], out_b[0]], axis=0).astype(F32)
        output = (own_tokens.astype(F32) + inv_gate[:, :1] * out_sum).astype(BF)
        inv = inv_rms[:, :1]
        grad_tokens = (
            inv * own_gain * normed_sum
            - own_tokens.astype(F32) * (inv * inv * (sum_terms[0][2, :length, None] / width))
            + own_cot.astype(F32)
        )
    return (
        output[None], grad_tokens[None], grad_gain, grad_main, grad_shared[0], jnp.transpose(grad_step), grad_km,
        grad_ks, grad_head, grad_gate[0], jnp.transpose(grad_out),
    )


def solution(mesh):
    return jax.shard_map(
        per_device,
        mesh=mesh,
        in_specs=(
            P("fsdp", "ctx", None),
            P("fsdp", None),
            P(),
            P(None, "fsdp", "tp"),
            P("fsdp", None),
            P("fsdp", "tp"),
            P(None, "tp"),
            P(),
            P(None, "tp"),
            P("tp"),
            P("tp", "fsdp"),
            P("fsdp", "ctx", None),
        ),
        out_specs=(
            P("fsdp", "ctx", "tp"),
            P("fsdp", "ctx", "tp"),
            P("tp"),
            P(None, ("fsdp", "ctx"), "tp"),
            P(("fsdp", "ctx"), None),
            P(("fsdp", "ctx"), "tp"),
            P(None, "tp"),
            P(),
            P(None, "tp"),
            P("tp"),
            P("tp", ("fsdp", "ctx")),
        ),
        check_vma=False,
    )
```

```python
import functools

import jax
import jax.numpy as jnp
from jax import lax
from jax.experimental import pallas as pl
from jax.experimental.pallas import tpu as pltpu
from jax.sharding import PartitionSpec as P


HEADDIM = 64
STATE = 128
STRETCH = 256
HALF = STRETCH // 2
INNER = 3072
EPSILON = 1e-05
HALO = 16
LANES = 128
SHARED = 2 * STATE
LEAD = SHARED + LANES
BF = jnp.bfloat16
F32 = jnp.float32
OUT_FIRST = 1
LIMITS = {"k_output": 60, "k_final": 60, "k_tokens0": 60, "k_tokens1": 60, "k_sums": 60, "k_packin": 60}


def dot_nn(a, b):
    return lax.dot_general(a, b, (((1,), (0,)), ((), ())), preferred_element_type=F32)


def dot_nt(a, b):
    return lax.dot_general(a, b, (((1,), (1,)), ((), ())), preferred_element_type=F32)


def dot_tn(a, b):
    return lax.dot_general(a, b, (((0,), (0,)), ((), ())), preferred_element_type=F32)


def split(v, n):
    terms = []
    for _ in range(n):
        high = v.astype(BF)
        terms.append(high)
        v = v - high.astype(F32)
    return terms


def exact(dot, a, b, n, left):
    total = None
    for term in split(a if left else b, n):
        part = dot(term, b) if left else dot(a, term)
        total = part if total is None else total + part
    return total


def iota(shape, axis):
    return lax.broadcasted_iota(jnp.int32, shape, axis)


def pair_widths(channels):
    return [(at, min(LANES, channels - at)) for at in range(0, channels, LANES)]


def spread(v, pair, width):
    first = v[:, 2 * pair : 2 * pair + 1]
    if width == HEADDIM:
        return jnp.broadcast_to(first, (v.shape[0], HEADDIM))
    second = v[:, 2 * pair + 1 : 2 * pair + 2]
    lane = iota((v.shape[0], LANES), 1)
    return jnp.where(lane < HEADDIM, first, second)


def head_masks(width):
    if width == HEADDIM:
        return [None]
    lane = iota((1, LANES), 1)
    return [(lane < HEADDIM).astype(F32).astype(BF), (lane >= HEADDIM).astype(F32).astype(BF)]


def masked(v, mask):
    return v if mask is None else v * mask


def sigmoid(v):
    return 1.0 / (1.0 + jnp.exp(-v))


def pack_in_kernel(shared_ref, step_ref, main_ref, out_ref):
    out_ref[:, 0:SHARED] = shared_ref[...]
    heads, rows = step_ref.shape
    tall = jnp.concatenate([step_ref[...].astype(F32), jnp.zeros((LANES - heads, rows), F32)], axis=0)
    out_ref[:, SHARED:LEAD] = jnp.transpose(tall).astype(BF)
    out_ref[:, LEAD:] = main_ref[0]


def pack_go_kernel(main_ref, out_proj_ref, out_ref):
    channels = main_ref.shape[2]
    wide = out_ref.shape[1] // 2
    if wide != channels:
        out_ref[...] = jnp.zeros_like(out_ref)
    out_ref[:, 0:channels] = main_ref[0]
    out_ref[:, wide : wide + channels] = jnp.transpose(out_proj_ref[...].astype(F32)).astype(BF)


def fetches(idx_ref, pieces, held, sems, columns=None):
    own, near, near_other, far, far_other = pieces
    half = held.shape[1] // 2
    c = idx_ref[4]
    top, bottom = (pl.ds(pl.multiple_of(h * half, HALO), half) for h in (c, 1 - c))
    targets = (
        (own, held.at[idx_ref[0]]),
        (near, held.at[idx_ref[1]]),
        (near_other, held.at[idx_ref[2]]),
        (far, held.at[idx_ref[3], top]),
        (far_other, held.at[idx_ref[3], bottom]),
    )
    return [
        pltpu.make_async_copy(
            source if columns is None else source.at[:, columns], target, sems.at[i]
        )
        for i, (source, target) in enumerate(targets)
    ]


def fetch_all(copies):
    for copy in copies:
        copy.start()
    for copy in copies:
        copy.wait()


def prep_kernel(
    chunk, idx_ref, tok_ref, halo_ref, cot_ref, gain_ref, seg_ref, normed_ref, nhalo_ref, own_ref, owncot_ref,
    inv_ref, tab_ref,
):
    k = pl.program_id(0)

    def scale_of(x):
        return lax.rsqrt(jnp.mean(x * x, axis=-1, keepdims=True) + EPSILON)

    x = tok_ref[...].astype(F32)
    inv = scale_of(x)
    inv_ref[...] = jnp.broadcast_to(inv, inv_ref.shape)
    normed_ref[...] = (x * inv * gain_ref[0:1, :]).astype(BF)
    mine = pl.ds(pl.multiple_of(idx_ref[5] * chunk, LANES), chunk)
    own_ref[...] = tok_ref[:, mine]
    owncot_ref[...] = cot_ref[:, mine]

    @pl.when(k == 0)
    def _():
        x = halo_ref[...].astype(F32)
        nhalo_ref[...] = (x * scale_of(x) * gain_ref[0:1, :]).astype(BF)

    start = (idx_ref[4] * pl.num_programs(0) + k) * STRETCH
    here = seg_ref[0:1, pl.ds(pl.multiple_of(start, LANES), STRETCH)].astype(F32)
    before = seg_ref[0:1, pl.ds(pl.multiple_of(jnp.maximum(start - LANES, 0), LANES), LANES)].astype(F32)
    before = jnp.where(start == 0, -1.0, before)
    both = jnp.broadcast_to(jnp.concatenate([before, here], axis=1), (8, LANES + STRETCH))
    row = iota((8, STRETCH), 0)
    tab = both[:, LANES:]
    for j in (1, 2, 3):
        tab = jnp.where(row == j, pltpu.roll(both, j, 1)[:, LANES:], tab)
    tab = jnp.where(row == 4, before[:, LANES - 1 :], tab)
    tab_ref[...] = jnp.where(row == 5, here[:, STRETCH - 1 :], tab)


def columns_of(tab_ref):
    tab = tab_ref[...]
    row = iota(tab.shape, 0)
    test = jnp.where(tab == tab[0:1], 1.0, 0.0)
    value = jnp.where(row == 0, tab, test).astype(BF)
    eye = (iota((8, LANES), 0) == iota((8, LANES), 1)).astype(F32).astype(BF)
    return dot_tn(value, eye)


def load_heads(hp_ref, wide_ref):
    wide_ref[...] = jnp.zeros_like(wide_ref)
    wide_ref[0:3, 0 : hp_ref.shape[1]] = hp_ref[...]


def expand_of(channels):
    head = jnp.right_shift(iota((channels, LANES), 0), 6)
    return (head == iota((channels, LANES), 1)).astype(F32).astype(BF)


def skip_of(wide_ref, expand):
    return exact(dot_nt, jnp.broadcast_to(wide_ref[2:3, :], (8, LANES)), expand, 3, True)


def conv_taps(u, taps, masks):
    total = taps[4:5] + taps[3:4] * u[HALO:]
    for j in (1, 2, 3):
        total = total + taps[3 - j : 4 - j] * (pltpu.roll(u, j, 0)[HALO:] * masks[j - 1])
    return total


def act_and_slope(v):
    sig = sigmoid(v)
    act = v * sig
    return act, sig + act * (1.0 - sig)


def first_kernel(
    idx_ref, own_ref, near_ref, nearx_ref, far_ref, farx_ref, normed_ref, nhalo_ref, km_ref, ks_ref, heads_ref, tab_ref,
    pre_ref, phalo_ref, x_ref, xs_ref, slope_ref, bc_ref, slopes_ref, step_ref, cum_ref, sgm_ref, state_ref, fac_ref,
    total_ref,
    held, sems, edge, carry, hp_ref, expand_ref,
):
    k = pl.program_id(0)
    channels = x_ref.shape[1]
    count, chunk = held.shape[0], held.shape[1]

    def project(rows):
        total = dot_nn(rows[:, :chunk], held[0])
        for a in range(1, count):
            total = total + dot_nn(rows[:, a * chunk : (a + 1) * chunk], held[a])
        return total.astype(BF)

    @pl.when(k == 0)
    def _():
        copies = fetches(idx_ref, (own_ref, near_ref, nearx_ref, far_ref, farx_ref), held, sems)
        for copy in copies:
            copy.start()
        carry[...] = jnp.zeros_like(carry)
        load_heads(heads_ref, hp_ref)
        expand_ref[...] = expand_of(channels)
        for copy in copies:
            copy.wait()
        before = project(nhalo_ref[...])
        phalo_ref[...] = before
        edge[...] = before

    pre_ref[...] = project(normed_ref[...])

    def ext(lanes):
        return jnp.concatenate([edge[:, lanes].astype(F32), pre_ref[:, lanes].astype(F32)], axis=0)

    col = columns_of(tab_ref)
    masks = [col[:, j : j + 1] for j in (1, 2, 3)]
    alive, ends = col[:, 4:5], col[:, 5:6]

    raw = pre_ref[:, SHARED:LEAD].astype(F32)
    pre = raw + hp_ref[1:2, :]
    soft = jnp.exp(-jnp.abs(pre))
    step = jnp.maximum(pre, 0.0) + jnp.log1p(soft)
    step_ref[...] = step
    sgm_ref[...] = sigmoid(pre)
    log_decay = step * -jnp.exp(hp_ref[0:1, :])
    tri = (iota((STRETCH, STRETCH), 0) >= iota((STRETCH, STRETCH), 1)).astype(F32).astype(BF)
    cum = exact(dot_nn, tri, log_decay, 3, False)
    cum_ref[...] = cum
    last = cum[STRETCH - 1 : STRETCH]
    ef = jnp.exp(last - cum) * ends
    factor = jnp.exp(last) * alive[STRETCH - 1 : STRETCH]
    fac_row = exact(dot_nt, jnp.broadcast_to(factor, (8, LANES)), expand_ref[...], 3, True)
    fac_ref[0] = fac_row

    acts, slopes = act_and_slope(
        conv_taps(ext(slice(0, SHARED)), ks_ref[...], masks)
    )
    bc_ref[...] = acts.astype(BF)
    slopes_ref[...] = slopes.astype(BF)
    keys_t = jnp.transpose(acts[:, 0:STATE]).astype(BF)
    for pair, (at, width) in enumerate(pair_widths(channels)):
        lanes = slice(at, at + width)
        u = ext(slice(LEAD + at, LEAD + at + width))
        act, slope = act_and_slope(conv_taps(u, km_ref[:, lanes], masks))
        low = act.astype(BF)
        x_ref[:, lanes] = low
        slope_ref[:, lanes] = slope.astype(BF)
        xs = (low.astype(F32) * spread(step, pair, width)).astype(BF)
        xs_ref[:, lanes] = xs
        xe = (xs.astype(F32) * spread(ef, pair, width)).astype(BF)
        state = dot_nn(keys_t, xe)
        state_ref[0, :, lanes] = state
        carry[:, lanes] = carry[:, lanes] * fac_row[0:1, lanes] + state

    edge[...] = pre_ref[STRETCH - HALO :, :]

    @pl.when(k == pl.num_programs(0) - 1)
    def _():
        total_ref[...] = carry[...].astype(BF)


def doc_mask(seg_col, seg_row, shape, transposed):
    down, across = iota(shape, 0), iota(shape, 1)
    order = (across >= down) if transposed else (down >= across)
    return (seg_col == seg_row) & order


def second_kernel(
    bc_ref, x_ref, xs_ref, cum_ref, state_ref, fac_ref, enter_ref, heads_ref, tab_ref,
    y_ref, hist_ref,
    hold, hp_ref, skip_ref,
):
    k = pl.program_id(0)
    channels = x_ref.shape[1]

    @pl.when(k == 0)
    def _():
        hold[...] = enter_ref[...].astype(F32)
        load_heads(heads_ref, hp_ref)
        skip_ref[...] = skip_of(hp_ref, expand_of(channels))

    hist_ref[pl.ds(k, 1)] = hold[...].astype(BF)[None]
    col = columns_of(tab_ref)
    alive = col[:, 4:5]
    keys, queries = bc_ref[:, 0:STATE], bc_ref[:, STATE:SHARED]
    gram = dot_nt(queries, keys)
    valid = doc_mask(col[:, 0:1], tab_ref[0:1, :], (STRETCH, STRETCH), False)
    gram = jnp.where(valid, gram, 0.0)
    cum = cum_ref[...]
    cum_t = jnp.transpose(cum)
    rise = jnp.exp(cum) * alive
    for pair, (at, width) in enumerate(pair_widths(channels)):
        lanes = slice(at, at + width)
        xs = xs_ref[:, lanes]
        top = bottom = 0.0
        for which, mask in enumerate(head_masks(width)):
            h = 2 * pair + which
            here = masked(xs, mask)
            down, across = cum[:, h : h + 1], cum_t[h : h + 1, :]
            decay = jnp.exp(jnp.minimum(down[:HALF] - across[:, :HALF], 0.0))
            top = top + dot_nn((decay * gram[:HALF, :HALF]).astype(BF), here[:HALF])
            decay = jnp.exp(jnp.minimum(down[HALF:] - across, 0.0))
            bottom = bottom + dot_nn((decay * gram[HALF:]).astype(BF), here)
        within = jnp.concatenate([top, bottom], axis=0)
        old = hold[:, lanes]
        carried = dot_nn(queries, old.astype(BF)) * spread(rise, pair, width)
        hold[:, lanes] = old * fac_ref[0, 0:1, lanes] + state_ref[0, :, lanes]
        y = within + carried + skip_ref[0:1, lanes] * x_ref[:, lanes].astype(F32)
        y_ref[:, lanes] = y

    @pl.when(k == pl.num_programs(0) - 1)
    def _():
        hist_ref[pl.ds(k + 1, 1)] = hold[...].astype(BF)[None]


def store_parts(outs, first, *refs):
    for here, keep_ref, send_ref in ((first, *refs[:2]), (~first, *refs[2:])):

        @pl.when(here)
        def _():
            for q, out in enumerate(outs):
                (send_ref if q % 2 else keep_ref)[q // 2] = out


def gate_kernel(
    idx_ref, own_ref, near_ref, nearx_ref, far_ref, farx_ref, normed_ref, y_ref, cot_ref, gain_ref,
    gate_ref, gg_ref, keepa_ref, senda_ref, keepb_ref, sendb_ref, stat_ref,
    held, sems,
):
    k = pl.program_id(0)
    channels = y_ref.shape[1]
    count, chunk = held.shape[0], held.shape[1]
    at_out = held.shape[2] // 2

    @pl.when(k == 0)
    def _():
        fetch_all(fetches(idx_ref, (own_ref, near_ref, nearx_ref, far_ref, farx_ref), held, sems))

    gates = dot_nn(normed_ref[:, :chunk], held[0, :, 0:channels])
    for a in range(1, count):
        gates = gates + dot_nn(normed_ref[:, a * chunk : (a + 1) * chunk], held[a, :, 0:channels])
    gate_ref[...] = gates.astype(BF)
    square = jnp.zeros((STRETCH, LANES), F32)
    for at, width in pair_widths(channels):
        lanes = slice(at, at + width)
        gate = gate_ref[:, lanes].astype(F32)
        gated = y_ref[:, lanes] * (gate * sigmoid(gate))
        gg_ref[:, lanes] = (gated * gain_ref[0:1, lanes]).astype(BF)
        square = square + padded(gated * gated)
    cross = jnp.zeros((STRETCH, LANES), F32)
    outs = []
    for q in range(count):
        a = jnp.bitwise_xor(idx_ref[6], q)
        out = dot_nt(gg_ref[...], held[a, :, at_out : at_out + channels])
        outs.append(out.astype(BF))
        inner = out * cot_ref[:, pl.ds(pl.multiple_of(a * chunk, LANES), chunk)].astype(F32)
        for part in range(0, chunk, LANES):
            cross = cross + inner[:, part : part + LANES]
    ones = jnp.ones((8, LANES), BF)
    square = exact(dot_nt, ones, square, 3, False)
    cross = exact(dot_nt, ones, cross, 3, False)
    stat_ref[...] = jnp.where(iota((8, STRETCH), 0) == 0, square, cross)
    store_parts(outs, k < OUT_FIRST, keepa_ref, senda_ref, keepb_ref, sendb_ref)


def padded(v):
    if v.shape[1] == LANES:
        return v
    return jnp.concatenate([v, jnp.zeros((v.shape[0], LANES - v.shape[1]), v.dtype)], axis=1)


def gng_kernel(idx_ref, own_ref, near_ref, nearx_ref, far_ref, farx_ref, cot_ref, gng_ref, held, sems):
    count, chunk = held.shape[0], held.shape[1]
    channels = gng_ref.shape[1]

    @pl.when(pl.program_id(0) == 0)
    def _():
        out = pl.ds(own_ref.shape[1] // 2, held.shape[2])
        fetch_all(fetches(idx_ref, (own_ref, near_ref, nearx_ref, far_ref, farx_ref), held, sems, out))

    total = dot_nn(cot_ref[:, :chunk], held[0, :, 0:channels])
    for a in range(1, count):
        total = total + dot_nn(cot_ref[:, a * chunk : (a + 1) * chunk], held[a, :, 0:channels])
    gng_ref[...] = total.astype(BF)


def third_kernel(
    stat_ref, y_ref, gate_ref, gng_ref, gain_ref, bc_ref, cum_ref, fac_ref, tab_ref,
    gy_ref, gi_ref, inv_ref, flow_ref, gaingrad_ref,
    hold,
):
    i = pl.program_id(0)
    channels = y_ref.shape[1]

    @pl.when(i == 0)
    def _():
        hold[...] = jnp.zeros_like(hold)
        gaingrad_ref[...] = jnp.zeros_like(gaingrad_ref)

    pick = iota((8, LANES), 0)
    stat = stat_ref[...]
    square = exact(dot_tn, stat, (pick == 0).astype(F32).astype(BF), 3, True)
    cross = exact(dot_tn, stat, (pick == 1).astype(F32).astype(BF), 3, True)
    inv = lax.rsqrt(square / INNER + EPSILON)
    inv_ref[...] = inv
    back = inv * inv * inv * (cross / INNER)
    rise = jnp.exp(cum_ref[...]) * columns_of(tab_ref)[:, 4:5]
    queries_t = jnp.transpose(bc_ref[:, STATE:SHARED].astype(F32)).astype(BF)
    for pair, (at, width) in enumerate(pair_widths(channels)):
        lanes = slice(at, at + width)
        gate = gate_ref[:, lanes].astype(F32)
        act, slope = act_and_slope(gate)
        y = y_ref[:, lanes]
        gated = y * act
        gng = gng_ref[:, lanes].astype(F32)
        along = inv[:, :width]
        grad = along * (gain_ref[0:1, lanes] * gng) - gated * back[:, :width]
        gaingrad_ref[0:1, lanes] += jnp.sum(gng * gated * along, axis=0, keepdims=True)
        gy = (grad * act).astype(BF)
        gy_ref[:, lanes] = gy
        gi_ref[:, lanes] = (grad * y * slope).astype(BF)
        gyr = (gy.astype(F32) * spread(rise, pair, width)).astype(BF)
        hold[:, lanes] = dot_nn(queries_t, gyr) + fac_ref[0, 0:1, lanes] * hold[:, lanes]

    @pl.when(i == pl.num_programs(0) - 1)
    def _():
        flow_ref[...] = hold[...].astype(BF)


def conv_back(post, u, taps, masks, kgrad_ref, lanes):
    full = post.shape[0] + HALO
    pad = jnp.zeros((HALO, post.shape[1]), F32)
    total = jnp.concatenate([pad, post], axis=0) * taps[3:4]
    kgrad_ref[4:5, lanes] += jnp.sum(post, axis=0, keepdims=True)
    kgrad_ref[3:4, lanes] += jnp.sum(post * u[HALO:], axis=0, keepdims=True)
    for j in (1, 2, 3):
        wide = jnp.concatenate([pad, post * masks[j - 1]], axis=0)
        moved = pltpu.roll(wide, full - j, 0)
        kgrad_ref[3 - j : 4 - j, lanes] += jnp.sum(moved * u, axis=0, keepdims=True)
        total = total + moved * taps[3 - j : 4 - j]
    return total


def fourth_kernel(
    idx_ref, own_ref, near_ref, nearx_ref, far_ref, farx_ref,
    gy_ref, x_ref, xs_ref, slope_ref, y_ref, bc_ref, slopes_ref, step_ref, cum_ref, sgm_ref, pre_ref, prev_ref,
    phalo_ref, ht_ref, hn_ref, fac_ref, enter_ref, km_ref, ks_ref, heads_ref, tab_ref, gategrad_ref,
    g_ref, ghalo_ref, small_ref, back_ref,
    held, sems, hold, edge, hp_ref, expand_ref, skip_ref, skipgrad_ref, kmgrad_ref, ksgrad_ref, head_ref,
):
    i = pl.program_id(0)
    k = pl.num_programs(0) - 1 - i
    channels = x_ref.shape[1]
    copies = fetches(idx_ref, (own_ref, near_ref, nearx_ref, far_ref, farx_ref), held, sems)

    @pl.when(i == 0)
    def _():
        for copy in copies:
            copy.start()
        hold[...] = enter_ref[...].astype(F32)
        edge[...] = jnp.zeros_like(edge)
        load_heads(heads_ref, hp_ref)
        expand_ref[...] = expand_of(channels)
        skip_ref[...] = skip_of(hp_ref, expand_ref[...])
        kmgrad_ref[...] = jnp.zeros_like(kmgrad_ref)
        ksgrad_ref[...] = jnp.zeros_like(ksgrad_ref)
        head_ref[...] = jnp.zeros_like(head_ref)
        skipgrad_ref[...] = jnp.zeros_like(skipgrad_ref)

    def ext(lanes):
        before = jnp.where(k == 0, phalo_ref[:, lanes].astype(F32), prev_ref[:, lanes].astype(F32))
        return jnp.concatenate([before, pre_ref[:, lanes].astype(F32)], axis=0)

    def put(lanes, total):
        g_ref[0 : STRETCH - HALO, lanes] = total[HALO:STRETCH].astype(BF)
        g_ref[STRETCH - HALO :, lanes] = (total[STRETCH:] + edge[:, lanes]).astype(BF)
        edge[:, lanes] = total[:HALO]

    col = columns_of(tab_ref)
    masks = [col[:, j : j + 1] for j in (1, 2, 3)]
    alive, ends = col[:, 4:5], col[:, 5:6]
    keys, queries = bc_ref[:, 0:STATE], bc_ref[:, STATE:SHARED]
    queries_t = jnp.transpose(queries.astype(F32)).astype(BF)
    valid = doc_mask(col[:, 0:1], tab_ref[0:1, :], (STRETCH, STRETCH), True)
    gram = jnp.where(valid, dot_nt(keys, queries), 0.0)
    step, cum = step_ref[...], cum_ref[...]
    cum_t = jnp.transpose(cum)
    rise = jnp.exp(cum) * alive
    ef = jnp.exp(cum[STRETCH - 1 : STRETCH] - cum) * ends
    gram_top = jnp.zeros((HALF, STRETCH), F32)
    gram_bottom = jnp.zeros((HALF, HALF), F32)
    grad_keys = jnp.zeros((STRETCH, STATE), F32)
    grad_queries = jnp.zeros((STRETCH, STATE), F32)
    cumterm = jnp.zeros((STRETCH, LANES), F32)
    colterm = jnp.zeros((STRETCH, LANES), F32)
    endterm = jnp.zeros((8, LANES), F32)
    for pair, (at, width) in enumerate(pair_widths(channels)):
        lanes = slice(at, at + width)
        expand = expand_ref[lanes, :]
        gy, xs = gy_ref[:, lanes], xs_ref[:, lanes]
        gyf, xf = gy.astype(F32), x_ref[:, lanes].astype(F32)
        skip = skip_ref[0:1, lanes]
        top = bottom = 0.0
        for which, mask in enumerate(head_masks(width)):
            h = 2 * pair + which
            here = masked(gy, mask)
            down, across = cum[:, h : h + 1], cum_t[h : h + 1, :]
            decay = jnp.exp(jnp.minimum(across - down[:HALF], 0.0))
            top = top + dot_nn((decay * gram[:HALF]).astype(BF), here)
            gram_top = gram_top + dot_nt(xs[:HALF], here) * decay
            decay = jnp.exp(jnp.minimum(across[:, HALF:] - down[HALF:], 0.0))
            bottom = bottom + dot_nn((decay * gram[HALF:, HALF:]).astype(BF), here[HALF:])
            gram_bottom = gram_bottom + dot_nt(xs[HALF:], here[HALF:]) * decay
        grad_xs = jnp.concatenate([top, bottom], axis=0)
        after = hold[:, lanes]
        low = after.astype(BF)
        efs = spread(ef, pair, width)
        from_end = dot_nn(keys, low) * efs
        grad_xs = grad_xs + from_end
        gyr = (gyf * spread(rise, pair, width)).astype(BF)
        xe = (xs.astype(F32) * efs).astype(BF)
        grad_queries = grad_queries + dot_nt(gyr, ht_ref[0, :, lanes])
        grad_keys = grad_keys + dot_nt(xe, low)
        ended = jnp.sum(after * ht_ref[0, :, lanes].astype(F32), axis=0, keepdims=True)
        ended = ended * fac_ref[0, 0:1, lanes] + jnp.sum(xs.astype(F32) * from_end, axis=0, keepdims=True)
        endterm = endterm + exact(dot_nn, jnp.broadcast_to(ended, (8, width)), expand, 3, True)
        hold[:, lanes] = dot_nn(queries_t, gyr) + fac_ref[0, 0:1, lanes] * after
        xsf = xs.astype(F32)
        colterm = colterm + exact(dot_nn, xf * grad_xs, expand, 1, True)
        cumterm = cumterm + exact(dot_nn, gyf * (y_ref[:, lanes] - skip * xf) - xsf * grad_xs, expand, 2, True)
        skipgrad_ref[0:1, lanes] += jnp.sum(gyf * xf, axis=0, keepdims=True)
        grad_x = grad_xs * spread(step, pair, width) + skip * gyf
        post = grad_x * slope_ref[:, lanes].astype(F32)
        at_g = slice(LEAD + at, LEAD + at + width)
        put(at_g, conv_back(post, ext(at_g), km_ref[:, lanes], masks, kmgrad_ref, lanes))

    gram_top = jnp.where(valid[:HALF], gram_top, 0.0).astype(BF)
    gram_bottom = jnp.where(valid[HALF:, HALF:], gram_bottom, 0.0).astype(BF)
    grad_keys = grad_keys + jnp.concatenate(
        [dot_nn(gram_top, queries), dot_nn(gram_bottom, queries[HALF:])], axis=0
    )
    lower = jnp.concatenate([jnp.zeros((HALF, HALF), BF), gram_bottom], axis=1)
    gram_all = jnp.concatenate([gram_top, lower], axis=0)
    grad_queries = grad_queries + dot_tn(gram_all, keys)
    post = jnp.concatenate([grad_keys, grad_queries], axis=1) * slopes_ref[...].astype(F32)
    shared = slice(0, SHARED)
    put(shared, conv_back(post, ext(shared), ks_ref[...], masks, ksgrad_ref, shared))

    rate = -jnp.exp(hp_ref[0:1, :])
    grad_cum = cumterm
    at_end = iota((STRETCH, LANES), 0) == STRETCH - 1
    grad_cum = grad_cum + jnp.where(at_end, endterm[0:1], 0.0)
    upper = (iota((STRETCH, STRETCH), 1) >= iota((STRETCH, STRETCH), 0)).astype(F32).astype(BF)
    grad_log = exact(dot_nn, upper, grad_cum, 3, False)
    grad_pre = (colterm + grad_log * rate) * sgm_ref[...]
    g_ref[:, SHARED:LEAD] = grad_pre.astype(BF)
    head_ref[0:1, :] += jnp.sum(grad_log * step, axis=0, keepdims=True) * rate
    head_ref[1:2, :] += jnp.sum(grad_pre, axis=0, keepdims=True)

    @pl.when(k == 0)
    def _():
        ghalo_ref[:, 0:SHARED] = edge[:, 0:SHARED].astype(BF)
        ghalo_ref[:, LEAD:] = edge[:, LEAD:].astype(BF)
        ghalo_ref[:, SHARED:LEAD] = jnp.zeros((HALO, LANES), BF)
        wide = jnp.broadcast_to(skipgrad_ref[0:1, :], (8, channels))
        small_ref[...] = jnp.zeros_like(small_ref)
        for tap in range(5):
            small_ref[1:2, tap * SHARED : (tap + 1) * SHARED] = ksgrad_ref[tap : tap + 1, :]
        small_ref[3:8, 0:channels] = kmgrad_ref[0:5, :]
        small_ref[8:9, 0:channels] = gategrad_ref[0:1, :]
        small_ref[9:11, 0:LANES] = head_ref[0:2, :]
        small_ref[11:12, 0:LANES] = exact(dot_nn, wide, expand_ref[...], 3, True)[0:1]
        for copy in copies:
            copy.wait()
        chunk = held.shape[1]
        for a in range(held.shape[0]):
            back_ref[:, a * chunk : (a + 1) * chunk] = dot_nt(ghalo_ref[...], held[a])


def normed_kernel(
    idx_ref, own0_ref, near0_ref, nearx0_ref, far0_ref, farx0_ref, own_ref, near_ref, nearx_ref, far_ref, farx_ref,
    gi_ref, g_ref, normed_ref, back_ref, small_ref,
    keepa_ref, senda_ref, keepb_ref, sendb_ref, sums_ref, cross_ref,
    held0, held, sems0, sems,
):
    i = pl.program_id(0)
    last = i == pl.num_programs(0) - 1
    rows = gi_ref.shape[0]
    count, chunk, channels = held0.shape

    @pl.when(i == 0)
    def _():
        pieces = (own0_ref, near0_ref, nearx0_ref, far0_ref, farx0_ref)
        columns = pl.ds(0, channels)
        copies = fetches(idx_ref, pieces, held0, sems0, columns)
        copies += fetches(idx_ref, (own_ref, near_ref, nearx_ref, far_ref, farx_ref), held, sems)
        fetch_all(copies)
        sums_ref[...] = small_ref[...]
        cross_ref[...] = jnp.zeros_like(cross_ref)

    cross = jnp.zeros((rows, LANES), F32)
    outs = []
    for q in range(count):
        a = jnp.bitwise_xor(idx_ref[6], q)
        lanes = pl.ds(pl.multiple_of(a * chunk, LANES), chunk)
        width = gi_ref.shape[1]
        total = dot_nt(gi_ref[...], held0[a, :, 0:width]) + dot_nt(g_ref[...], held[a])
        tail = total[rows - HALO :] + jnp.where(last, back_ref[:, lanes], 0.0)
        total = jnp.concatenate([total[: rows - HALO], tail], axis=0)
        outs.append(total.astype(BF))
        inner = total * normed_ref[:, lanes].astype(F32)
        sums_ref[0:1, lanes] += jnp.sum(inner, axis=0, keepdims=True)
        for part in range(0, chunk, LANES):
            cross = cross + inner[:, part : part + LANES]
    row = exact(dot_nt, jnp.ones((8, LANES), BF), cross, 3, False)[0:1]
    cross_ref[2:3, pl.ds(pl.multiple_of(i * rows, LANES), rows)] = row
    first = i < pl.num_programs(0) // 2
    store_parts(outs, first, keepa_ref, senda_ref, keepb_ref, sendb_ref)


def put_chunk(idx_ref, keep_ref, send_ref, lanes, value):
    j = pl.program_id(0)
    half = keep_ref.shape[1]
    top, bottom = value[:half].astype(BF), value[half:].astype(BF)

    @pl.when(j == idx_ref[1])
    def _():
        keep_ref[0, :, lanes] = top
        keep_ref[1, :, lanes] = bottom

    @pl.when(j == idx_ref[2])
    def _():
        send_ref[0, :, lanes] = top
        send_ref[1, :, lanes] = bottom

    for source, target in ((0, 3), (3, 2)):
        for c, (mine, other) in enumerate(((top, bottom), (bottom, top))):

            @pl.when((j == idx_ref[source]) & (idx_ref[4] == c))
            def _():
                keep_ref[target, :, lanes] = mine
                send_ref[target, :, lanes] = other


def weight_kernel(idx_ref, normed_ref, nhalo_ref, g_ref, ghalo_ref, keep_ref, send_ref):
    value = dot_tn(normed_ref[...], g_ref[...]) + dot_tn(nhalo_ref[...], ghalo_ref[...])
    put_chunk(idx_ref, keep_ref, send_ref, slice(None), value)


def gate_out_kernel(idx_ref, normed_ref, gi_ref, cot_ref, inv_ref, gg_ref, keep_ref, send_ref):
    channels = gi_ref.shape[1]
    wide = keep_ref.shape[2] // 2
    put_chunk(idx_ref, keep_ref, send_ref, slice(0, channels), dot_tn(normed_ref[...], gi_ref[...]))
    scaled = [
        (cot_ref[:, at : at + LANES].astype(F32) * inv_ref[...]).astype(BF)
        for at in range(0, cot_ref.shape[1], LANES)
    ]
    value = dot_tn(jnp.concatenate(scaled, axis=1), gg_ref[...])
    put_chunk(idx_ref, keep_ref, send_ref, slice(wide, wide + channels), value)


def add_kernel(a_ref, b_ref, out_ref):
    out_ref[...] = (a_ref[...].astype(F32) + b_ref[...].astype(F32)).astype(BF)


def near_kernel(idx_ref, keep_ref, got_ref, far_ref, out_ref):
    for h in (0, 1):
        total = keep_ref[h].astype(F32) + got_ref[h].astype(F32)
        out_ref[h] = (total + jnp.where(idx_ref[4] == h, far_ref[0].astype(F32), 0.0)).astype(BF)


def final_kernel(idx_ref, *refs):
    go, w, (main_ref, step_ref, shared_ref, out_ref) = refs[:4], refs[4:8], refs[8:]
    channels = main_ref.shape[2]
    wide = go[0].shape[2] // 2

    def total(terms, lanes):
        value = terms[0][0, :, lanes].astype(F32)
        for term in terms[1:]:
            value = value + term[0, :, lanes].astype(F32)
        return value

    shared_ref[...] = total(w, slice(0, SHARED)).astype(shared_ref.dtype)
    steps = total(w, slice(SHARED, LEAD))
    rows = step_ref.shape[1]
    steps = jnp.concatenate([steps, jnp.zeros((-rows % LANES, LANES), F32)], axis=0)
    step_ref[...] = jnp.transpose(steps)[0 : step_ref.shape[0], 0:rows]
    for at, width in pair_widths(channels):
        lanes = slice(at, at + width)
        main_ref[0, :, lanes] = total(go, lanes)
        main_ref[1, :, lanes] = total(w, slice(LEAD + at, LEAD + at + width))
        out_ref[:, lanes] = total(go, slice(wide + at, wide + at + width))


def sums_kernel(sums_ref, gain_ref, *refs):
    terms, (all_ref, km_ref, ks_ref, head_ref, gate_ref) = refs[:-5], refs[-5:]
    channels = km_ref.shape[1]
    over = terms[0][0:2]
    if len(terms) == 4:
        over = (over + terms[1][0:2]) + (terms[2][0:2] + terms[3][0:2])
    all_ref[...] = over[0:1] / gain_ref[...]
    for tap in range(5):
        ks_ref[tap : tap + 1, :] = over[1:2, tap * SHARED : (tap + 1) * SHARED]
    km_ref[...] = sums_ref[3:8, 0:channels]
    gate_ref[...] = sums_ref[8:9, 0:channels]
    head_ref[...] = sums_ref[9:12, 0 : head_ref.shape[1]]


def output_kernel(own_ref, inv_ref, *refs):
    out_ref = refs[-1]
    inv = inv_ref[...]
    first = pl.program_id(0) < OUT_FIRST
    for here, terms in ((first, refs[0:3]), (~first, refs[3:6])):

        @pl.when(here)
        def _():
            for at in range(0, out_ref.shape[1], LANES):
                lanes = slice(at, at + LANES)
                total = terms[0][0, :, lanes].astype(F32) + terms[1][0, :, lanes].astype(F32)
                total = (total + terms[2][0, :, lanes].astype(F32)) * inv
                out_ref[:, lanes] = (own_ref[:, lanes].astype(F32) + total).astype(BF)


def tokens_kernel(
    width, own_ref, cot_ref, inv_ref, t0_ref, t1_ref, t2_ref, t3_ref, gain_ref, keep_ref, got_ref, far_ref, *refs
):
    out_ref = refs[-1]
    inv = inv_ref[...]
    pick = (iota((8, LANES), 0) == 2).astype(F32).astype(BF)
    cross = (t0_ref[...] + t1_ref[...]) + (t2_ref[...] + t3_ref[...])
    cross = exact(dot_tn, cross, pick, 3, True)
    back = inv * inv * (cross / width)
    for at in range(0, out_ref.shape[1], LANES):
        lanes = slice(at, at + LANES)
        total = keep_ref[0, :, lanes].astype(F32) + got_ref[0, :, lanes].astype(F32)
        total = total + far_ref[0, :, lanes].astype(F32)
        out_ref[:, lanes] = (
            inv * gain_ref[0:1, lanes] * total
            - own_ref[:, lanes].astype(F32) * back
            + cot_ref[:, lanes].astype(F32)
        )


def whole(array):
    rank = len(array.shape)
    return pl.BlockSpec(array.shape, lambda *_: (0,) * rank)


def call(name, kernel, grid, ins, in_specs, outs, out_specs, scratch=(), flops=0, prefetch=0, alias={}):
    moved = sum(a.size * a.dtype.itemsize for a in (*ins, *outs))
    return pl.pallas_call(
        kernel,
        out_shape=outs,
        input_output_aliases=alias,
        grid_spec=pltpu.PrefetchScalarGridSpec(
            num_scalar_prefetch=prefetch,
            grid=grid,
            in_specs=in_specs,
            out_specs=out_specs,
            scratch_shapes=list(scratch),
        ),
        compiler_params=pltpu.CompilerParams(
            dimension_semantics=("arbitrary",) * len(grid), vmem_limit_bytes=LIMITS.get(name, 16) * 2**20
        ),
        cost_estimate=pl.CostEstimate(
            flops=int(flops), bytes_accessed=int(moved), transcendentals=0
        ),
    )(*ins)


def shape(dims, kind):
    return jax.ShapeDtypeStruct(dims, kind)


def per_device(
    tokens, segments, norm_gain, proj_main, proj_shared, proj_step, conv_main, conv_shared,
    head_params, gate_gain, output_projection, cotangent,
):
    _, length, width = tokens.shape
    nf, nc, nt = lax.axis_size("fsdp"), lax.axis_size("ctx"), lax.axis_size("tp")
    assert nf == 4 and nc == 2
    f, c, t = lax.axis_index("fsdp"), lax.axis_index("ctx"), lax.axis_index("tp")
    heads = head_params.shape[1]
    channels = heads * HEADDIM
    lead = LEAD + channels
    wide = -(-channels // LANES) * LANES
    nb = length // STRETCH
    chunk = width // nf
    half = chunk // 2
    share = width // nt
    line = nt == nf
    rot = t if line else jnp.zeros_like(t)
    both = ("fsdp", "ctx")
    spots = [(i, j) for i in range(nf) for j in range(nc)]
    role = [(i * nc + j, (i ^ (1 + j)) * nc + j) for i, j in spots]
    turn = [(i * nc + j, (i ^ (2 - j)) * nc + j) for i, j in spots]
    across_chip = [(i * nc + j, (i ^ 3) * nc + j) for i, j in spots]
    swap = [(0, 1), (1, 0)]
    idx = jnp.stack([f, f ^ (1 + c), f ^ (2 - c), f ^ 3, c, rot, rot, rot]).astype(jnp.int32)

    def tp_sum(v):
        if not line:
            return lax.psum(v, "tp")
        first, second, third = (
            lax.ppermute(v, "tp", [(i, i ^ m) for i in range(nt)]) for m in (1, 2, 3)
        )
        return (v + first) + (second + third)

    def tp_terms(v):
        if not line:
            return (lax.psum(v, "tp"),)
        return (v, *(lax.ppermute(v, "tp", [(i, i ^ m) for i in range(nt)]) for m in (1, 2, 3)))

    def one(v, at):
        return lax.dynamic_slice_in_dim(v, at, 1, 0)

    def gather_rows(shard, direct):
        columns = shard.shape[1]
        pieces = shard.reshape(2, half, columns)
        near = lax.ppermute(pieces, both, role)
        if direct:
            far = lax.ppermute(one(pieces, c), both, across_chip)
        else:
            far = lax.ppermute(one(near, c), both, turn)
        near_other = lax.ppermute(near, "ctx", swap)
        far_other = lax.ppermute(far, "ctx", swap)
        return (
            shard, near.reshape(chunk, columns), near_other.reshape(chunk, columns), far[0], far_other[0]
        )

    def add_block(name, a, b, at):
        dims = (1, *a.shape[1:])
        spec = pl.BlockSpec(dims, lambda i: (at, 0, 0))
        out = pl.BlockSpec(dims, lambda i: (0, 0, 0))
        return call(name, add_kernel, (1,), (a, b), [spec, spec], (shape(dims, BF),), [out])[0]

    def scatter_rows(name, keep, send):
        got = lax.ppermute(send, "ctx", swap)
        far = lax.ppermute(add_block(f"k_{name}2", keep, got, 2), both, turn)
        columns = keep.shape[2]
        two = pl.BlockSpec((2, half, columns), lambda i, *_: (0, 0, 0))
        outs = (shape((2, half, columns), BF),)
        near = call(
            f"k_{name}3", near_kernel, (1,), (idx, keep, got, far), [two, two, whole(far)], outs, [two], prefetch=1
        )[0]
        near = lax.ppermute(near, both, role)
        return keep, got, near, lax.ppermute(one(near, 1 - c), "ctx", swap)

    def scatter_tp(name, keep, send):
        if not line:
            full = jnp.concatenate([keep[0], send[0], keep[1], send[1]], axis=1)
            return (lax.psum_scatter(full, "tp", scatter_dimension=1, tiled=True),)
        got = lax.ppermute(send, "tp", [(i, i ^ 1) for i in range(nt)])
        far = lax.ppermute(add_block(f"k_{name}", keep, got, 1), "tp", [(i, i ^ 2) for i in range(nt)])
        return keep, got, far

    any_spec = pl.BlockSpec(memory_space=pl.ANY)
    sems = pltpu.SemaphoreType.DMA((5,))

    def block(columns, back=False):
        if back:
            return pl.BlockSpec((STRETCH, columns), lambda i, *_: (nb - 1 - i, 0))
        return pl.BlockSpec((STRETCH, columns), lambda i, *_: (i, 0))

    def across(back=False):
        if back:
            return pl.BlockSpec((8, STRETCH), lambda i, *_: (0, nb - 1 - i))
        return pl.BlockSpec((8, STRETCH), lambda i, *_: (0, i))

    def stacked(rows, columns, back=False, off=0):
        if back:
            return pl.BlockSpec((1, rows, columns), lambda i, *_: (nb - 1 - i + off, 0, 0))
        return pl.BlockSpec((1, rows, columns), lambda i, *_: (i + off, 0, 0))

    mid = length // 2
    part_a = pl.BlockSpec((2, STRETCH, chunk), lambda i, *_: (0, jnp.minimum(i, nb // 2 - 1), 0))
    part_b = pl.BlockSpec((2, STRETCH, chunk), lambda i, *_: (0, jnp.maximum(i - nb // 2, 0), 0))

    def main_part(which):
        return pl.BlockSpec((1, chunk, channels), lambda i: (which, 0, 0))

    tokens2, cot2 = tokens[0], cotangent[0]
    step_t = jnp.transpose(proj_step)
    ins = (proj_shared, step_t, proj_main)
    outs = (shape((chunk, lead), BF),)
    shard_in = call(
        "k_packin", pack_in_kernel, (1,), ins, [whole(proj_shared), whole(step_t), main_part(1)],
        outs, [whole(outs[0])],
    )[0]
    w_in = gather_rows(shard_in, False)
    halo = lax.ppermute(tokens2[length - HALO :], "ctx", [(0, 1)])
    ins = (proj_main, output_projection)
    outs = (shape((chunk, 2 * wide), BF),)
    shard_go = call(
        "k_packgo", pack_go_kernel, (1,), ins, [main_part(0), whole(output_projection)],
        outs, [whole(outs[0])],
    )[0]
    w_go = gather_rows(shard_go, True)

    gate_row = gate_gain[None]
    gain_row = norm_gain[None]

    ins = (idx, tokens2, halo, cot2, gain_row, segments)
    outs = (
        shape((length, width), BF), shape((HALO, width), BF), shape((length, chunk), BF),
        shape((length, chunk), BF), shape((length, LANES), F32), shape((8, length), F32),
    )
    normed, nhalo, own_tokens, own_cot, inv_rms, tab = call(
        "k_prep", functools.partial(prep_kernel, chunk), (nb,), ins,
        [block(width), whole(halo), block(width), whole(gain_row), whole(segments)],
        outs, [block(width), whole(outs[1]), block(chunk), block(chunk), block(LANES), across()], prefetch=1,
    )
    if not line:
        own_tokens = lax.dynamic_slice_in_dim(tokens2, t * share, share, 1)
        own_cot = lax.dynamic_slice_in_dim(cot2, t * share, share, 1)

    outs = (
        shape((length, lead), BF), shape((HALO, lead), BF),
        shape((length, channels), BF), shape((length, channels), BF), shape((length, channels), BF),
        shape((length, SHARED), BF), shape((length, SHARED), BF),
        shape((length, LANES), F32), shape((length, LANES), F32), shape((length, LANES), F32),
        shape((nb, STATE, channels), F32), shape((nb, 8, channels), F32), shape((STATE, channels), BF),
    )
    ins = (idx, *w_in, normed, nhalo, conv_main, conv_shared, head_params, tab)
    wide_row = pltpu.VMEM((8, LANES), F32)
    held_in = pltpu.VMEM((nf, chunk, lead), BF)
    pre, phalo, x, xs, slope, bc, slopes, step, cum, sgm, states, fac, total = call(
        "k_first", first_kernel, (nb,), ins,
        [any_spec] * 5
        + [block(width), whole(nhalo), whole(conv_main), whole(conv_shared), whole(head_params), across()],
        outs,
        [block(lead), whole(outs[1])] + [block(channels)] * 3 + [block(SHARED)] * 2 + [block(LANES)] * 3
        + [stacked(STATE, channels), stacked(8, channels), whole(outs[-1])],
        scratch=[
            held_in, sems, pltpu.VMEM((HALO, lead), BF), pltpu.VMEM((STATE, channels), F32), wide_row,
            pltpu.VMEM((channels, LANES), BF),
        ],
        prefetch=1, flops=2 * length * (STATE * channels + width * lead),
    )
    enter = lax.ppermute(total, "ctx", [(0, 1)])

    outs = (shape((length, channels), F32), shape((nb + 1, STATE, channels), BF))
    ins = (bc, x, xs, cum, states, fac, enter, head_params, tab)
    y, hist = call(
        "k_second", second_kernel, (nb,), ins,
        [
            block(SHARED), block(channels), block(channels), block(LANES), stacked(STATE, channels),
            stacked(8, channels), whole(enter), whole(head_params), across(),
        ],
        outs, [block(channels), whole(outs[1])],
        scratch=[pltpu.VMEM((STATE, channels), F32), wide_row, pltpu.VMEM((8, channels), F32)],
        flops=8 * length * STRETCH * channels,
    )

    outs = (
        shape((length, channels), BF), shape((length, channels), BF), *(shape((2, OUT_FIRST * STRETCH, chunk), BF),) * 2,
        *(shape((2, length - OUT_FIRST * STRETCH, chunk), BF),) * 2,
        shape((8, length), F32),
    )
    out_a = pl.BlockSpec((2, STRETCH, chunk), lambda i, *_: (0, jnp.minimum(i, OUT_FIRST - 1), 0))
    out_b = pl.BlockSpec((2, STRETCH, chunk), lambda i, *_: (0, jnp.maximum(i - OUT_FIRST, 0), 0))
    ins = (idx, *w_go, normed, y, cot2, gate_row)
    gate, gg, *out_parts, stat = call(
        "k_gate", gate_kernel, (nb,), ins,
        [any_spec] * 5 + [block(width), block(channels), block(width), whole(gate_row)],
        outs, [block(channels)] * 2 + [out_a, out_a, out_b, out_b, across()],
        scratch=[pltpu.VMEM((nf, chunk, 2 * wide), BF), sems],
        prefetch=1, flops=4 * length * width * channels,
    )
    out_terms = (*scatter_tp("roa", *out_parts[:2]), *scatter_tp("rob", *out_parts[2:]))
    stat = tp_sum(stat)
    outs = (shape((length, channels), BF),)
    gng = call(
        "k_gng", gng_kernel, (nb,), (idx, *w_go, cot2), [any_spec] * 5 + [block(width)], outs, [block(channels)],
        scratch=[pltpu.VMEM((nf, chunk, wide), BF), sems], prefetch=1, flops=2 * length * width * channels,
    )[0]

    outs = (
        shape((length, channels), BF), shape((length, channels), BF), shape((length, LANES), F32),
        shape((STATE, channels), BF), shape((8, channels), F32),
    )
    ins = (stat, y, gate, gng, gate_row, bc, cum, fac, tab)
    gy, gi, inv_gate, flow, gate_grad = call(
        "k_third", third_kernel, (nb,), ins,
        [
            across(True), block(channels, True), block(channels, True), block(channels, True), whole(gate_row),
            block(SHARED, True), block(LANES, True), stacked(8, channels, True), across(True),
        ],
        outs, [block(channels, True), block(channels, True), block(LANES, True), whole(outs[3]), whole(outs[4])],
        scratch=[pltpu.VMEM((STATE, channels), F32)],
        flops=2 * length * STATE * channels,
    )
    leaving = lax.ppermute(flow, "ctx", [(1, 0)])

    outs = (shape((4, half, 2 * wide), BF),) * 2
    ins = (idx, normed, gi, cot2, inv_gate, gg)
    grad_go = call(
        "k_go", gate_out_kernel, (nf,), ins,
        [
            pl.BlockSpec((length, chunk), lambda i, *_: (0, i)), whole(gi),
            pl.BlockSpec((length, chunk), lambda i, *_: (0, i)), whole(inv_gate), whole(gg),
        ],
        outs, [whole(outs[0])] * 2, prefetch=1,
        flops=4 * length * width * channels,
    )
    grad_go = scatter_rows("go", *grad_go)

    outs = (
        shape((length, lead), BF), shape((HALO, lead), BF), shape((16, width), F32), shape((HALO, width), F32),
    )
    ins = (
        idx, *w_in, gy, x, xs, slope, y, bc, slopes, step, cum, sgm, pre, pre, phalo, hist, hist, fac, leaving,
        conv_main, conv_shared, head_params, tab, gate_grad,
    )
    per_block = STRETCH // HALO
    g_in, ghalo, small, back = call(
        "k_fourth", fourth_kernel, (nb,), ins,
        [any_spec] * 5
        + [block(channels, True)] * 5 + [block(SHARED, True)] * 2 + [block(LANES, True)] * 3
        + [
            block(lead, True),
            pl.BlockSpec((HALO, lead), lambda i, *_: (jnp.maximum((nb - 1 - i) * per_block - 1, 0), 0)),
            whole(phalo), stacked(STATE, channels, True), stacked(STATE, channels, True, 1),
            stacked(8, channels, True), whole(leaving), whole(conv_main), whole(conv_shared),
            whole(head_params), across(True), whole(gate_grad),
        ],
        outs, [block(lead, True)] + [whole(o) for o in outs[1:]],
        scratch=[
            held_in, sems, pltpu.VMEM((STATE, channels), F32), pltpu.VMEM((HALO, lead), F32), wide_row,
            pltpu.VMEM((channels, LANES), BF), pltpu.VMEM((8, channels), F32), pltpu.VMEM((8, channels), F32),
            pltpu.VMEM((8, channels), F32), pltpu.VMEM((8, SHARED), F32), wide_row,
        ],
        prefetch=1, flops=16 * length * STRETCH * channels,
    )
    back = lax.ppermute(back, "ctx", [(1, 0)])

    outs = (shape((2, mid, chunk), BF),) * 4 + (shape((16, width), F32), shape((8, width), F32))
    ins = (idx, *w_go, *w_in, gi, g_in, normed, back, small)
    keep_a, send_a, keep_b, send_b, sums, cross = call(
        "k_normed", normed_kernel, (nb,), ins,
        [any_spec] * 10 + [block(channels), block(lead), block(width), whole(back), whole(small)],
        outs, [part_a, part_a, part_b, part_b, whole(outs[-2]), whole(outs[-1])],
        scratch=[pltpu.VMEM((nf, chunk, wide), BF), held_in, sems, sems],
        prefetch=1, flops=2 * length * width * (lead + channels),
    )
    normed_a = scatter_tp("rna", keep_a, send_a)
    normed_b = scatter_tp("rnb", keep_b, send_b)

    outs = (shape((4, half, lead), BF),) * 2
    grad_w = call(
        "k_weight", weight_kernel, (nf,), (idx, normed, nhalo, g_in, ghalo),
        [
            pl.BlockSpec((length, chunk), lambda i, *_: (0, i)), pl.BlockSpec((HALO, chunk), lambda i, *_: (0, i)),
            whole(g_in), whole(ghalo),
        ],
        outs, [whole(outs[0])] * 2, prefetch=1,
        flops=2 * length * width * lead,
    )
    grad_w = scatter_rows("w", *grad_w)

    sums = sums + lax.ppermute(sums, "ctx", swap)
    for m in (1, 2):
        sums = sums + lax.ppermute(sums, "fsdp", [(i, i ^ m) for i in range(nf)])
    sum_terms = tp_terms(jnp.where(iota((8, 1), 0) < 2, sums[:8], cross))
    outs = (
        shape((1, width), F32), shape((5, channels), F32), shape((5, SHARED), F32), shape((3, heads), F32),
        shape((1, channels), F32),
    )
    ins = (sums, gain_row, *sum_terms)
    gain_all, grad_km, grad_ks, grad_head, grad_gate = call(
        "k_sums", sums_kernel, (1,), ins, [whole(v) for v in ins], outs, [whole(o) for o in outs]
    )
    grad_gain = lax.dynamic_slice_in_dim(gain_all[0], t * share, share, 0)
    own_gain = lax.dynamic_slice_in_dim(norm_gain, t * share, share, 0)

    def terms_of(columns):
        return [
            pl.BlockSpec((1, half, columns), lambda i, *_: (3, 0, 0)),
            pl.BlockSpec((1, half, columns), lambda i, *_: (3, 0, 0)),
            pl.BlockSpec((1, half, columns), lambda i, idx_ref: (idx_ref[4], 0, 0)),
            pl.BlockSpec((1, half, columns), lambda i, *_: (0, 0, 0)),
        ]

    outs = (
        shape((2, half, channels), F32), shape((heads, half), F32), shape((half, SHARED), BF if line else F32),
        shape((half, channels), F32),
    )
    grad_main, grad_step, grad_shared, grad_out = call(
        "k_final", final_kernel, (1,), (idx, *grad_go, *grad_w), terms_of(2 * wide) + terms_of(lead),
        outs, [whole(o) for o in outs], prefetch=1,
    )
    grad_shared = [v.astype(F32) for v in tp_terms(grad_shared)]
    if line:
        grad_shared = [(grad_shared[0] + grad_shared[1]) + (grad_shared[2] + grad_shared[3])]

    outs = (shape((length, share), BF),)
    if line:
        spec = pl.BlockSpec((mid, share), lambda i: (i, 0))
        term_a = pl.BlockSpec((1, STRETCH, share), lambda i: (0, jnp.minimum(i, OUT_FIRST - 1), 0))
        term_b = pl.BlockSpec((1, STRETCH, share), lambda i: (0, jnp.maximum(i - OUT_FIRST, 0), 0))
        output = call(
            "k_output", output_kernel, (nb,), (own_tokens, inv_gate, *out_terms),
            [block(share), block(LANES)] + [term_a] * 3 + [term_b] * 3,
            outs, [block(share)],
        )[0]
        outs = (shape((length, share), F32),)
        gain2 = own_gain[None]
        grad_tokens = ()
        for part, terms in enumerate((normed_a, normed_b)):
            at = part * (mid // STRETCH)
            grad_tokens = call(
                f"k_tokens{part}", functools.partial(tokens_kernel, width), (mid // STRETCH,),
                (own_tokens, own_cot, inv_rms, *sum_terms, gain2, *terms, *grad_tokens),
                [pl.BlockSpec((STRETCH, share), lambda i, at=at: (i + at, 0))] * 2
                + [pl.BlockSpec((STRETCH, LANES), lambda i, at=at: (i + at, 0))]
                + [pl.BlockSpec((8, STRETCH), lambda i, at=at: (0, i + at))] * 4
                + [whole(gain2)]
                + [pl.BlockSpec((1, STRETCH, share), lambda i: (0, i, 0))] * 3
                + [any_spec] * part,
                outs, [pl.BlockSpec((STRETCH, share), lambda i, at=at: (i + at, 0))],
                alias={11: 0} if part else {},
            )
        grad_tokens = grad_tokens[0]
    else:
        normed_sum = jnp.concatenate([normed_a[0], normed_b[0]], axis=0).astype(F32)
        out_sum = jnp.concatenate(out_terms, axis=0).astype(F32)
        output = (own_tokens.astype(F32) + inv_gate[:, :1] * out_sum).astype(BF)
        inv = inv_rms[:, :1]
        grad_tokens = (
            inv * own_gain * normed_sum
            - own_tokens.astype(F32) * (inv * inv * (sum_terms[0][2, :length, None] / width))
            + own_cot.astype(F32)
        )
    return (
        output[None], grad_tokens[None], grad_gain, grad_main, grad_shared[0], jnp.transpose(grad_step), grad_km,
        grad_ks, grad_head, grad_gate[0], jnp.transpose(grad_out),
    )


def solution(mesh):
    return jax.shard_map(
        per_device,
        mesh=mesh,
        in_specs=(
            P("fsdp", "ctx", None),
            P("fsdp", None),
            P(),
            P(None, "fsdp", "tp"),
            P("fsdp", None),
            P("fsdp", "tp"),
            P(None, "tp"),
            P(),
            P(None, "tp"),
            P("tp"),
            P("tp", "fsdp"),
            P("fsdp", "ctx", None),
        ),
        out_specs=(
            P("fsdp", "ctx", "tp"),
            P("fsdp", "ctx", "tp"),
            P("tp"),
            P(None, ("fsdp", "ctx"), "tp"),
            P(("fsdp", "ctx"), None),
            P(("fsdp", "ctx"), "tp"),
            P(None, "tp"),
            P(),
            P(None, "tp"),
            P("tp"),
            P("tp", ("fsdp", "ctx")),
        ),
        check_vma=False,
    )
```
